32 devices in a mesh: seq: 4 (over y, core), dp: 8 (over z, x).
Axes of the slice: x: 2, y: 2, z: 4, core: 2. Of those that a mesh axis runs over, the one named last changes fastest.
Arguments:
- tokens: bfloat16 [16, 1024, 1024], P('dp', 'seq'), may hold values from -6 to 6
- cotangent: bfloat16 [16, 1024, 1024], P('dp', 'seq'), may hold values from -6 to 6
- row_lengths: int32 [16], P('dp'), may hold values from 512 to 1024
- source_lengths: int32 [16], P('dp'), may hold values from 30 to 400
- first_gain: float32 [1024], replicated, may hold values from 0.1 to 1.9
- first_shift: float32 [1024], replicated, may hold values from -2 to 2
- attend_weight: bfloat16 [1024, 3072], replicated, may hold values from -0.25 to 0.25
- attend_bias: float32 [3072], replicated, may hold values from -2 to 2
- output_weight: bfloat16 [1024, 1024], replicated, may hold values from -0.75 to 0.75
- output_bias: float32 [1024], replicated, may hold values from -2 to 2
- second_gain: float32 [1024], replicated, may hold values from 0.1 to 1.9
- second_shift: float32 [1024], replicated, may hold values from -2 to 2
- expand_weight: bfloat16 [1024, 4096], replicated, may hold values from -0.1875 to 0.1875
- expand_bias: float32 [4096], replicated, may hold values from -2 to 2
- contract_weight: bfloat16 [4096, 1024], replicated, may hold values from -0.09375 to 0.09375
- contract_bias: float32 [1024], replicated, may hold values from -2 to 2
- prefix_table: bfloat16 [10, 1024], replicated, may hold values from -6 to 6
- lift_weight: bfloat16 [1024, 512], replicated, may hold values from -0.1875 to 0.1875
- lift_bias: float32 [512], replicated, may hold values from -2 to 2
- fan_weight: bfloat16 [512, 2048], replicated, may hold values from -0.375 to 0.375
- fan_bias: float32 [2048], replicated, may hold values from -2 to 2
Outputs:
- activations: bfloat16 [16, 1024, 1024], P('dp', 'seq')
- input_grad: float32 [16, 1024, 1024], P('dp', 'seq')
- grad_table: float32 [10, 1024], replicated
- grad_lift: float32 [1024, 512], replicated
- grad_liftbias: float32 [512], replicated
- grad_fan: float32 [512, 2048], replicated
- grad_fanbias: float32 [2048], replicated
The draws below stay inside these ranges and needn't reach their ends.
All inputs are finite; a program needn't handle non-finite values.
Results may differ from the reference program's by a relative error of at most 0.025.
Values may be sent and summed in bfloat16 or wider, within the bound.
No kernel may reach another device: no remote copies, remote signals or barrier semaphores. Data moves between devices by JAX's collectives and lax.ppermute only.
A program may use at most 320 MiB of HBM per device.

```python
import jax
import jax.numpy as jnp
from jax import lax

D = 1024
HEADS = 16
HEAD_DIM = 64
FF = 4096
PREFIX = 10
PRE_HID = 512
SEQ_LEN = 1024
ROWS = 16
KV_WIDTH = 2048


def plant(values, stream_key, least, top_value):
    extent = values.shape
    spot = [jax.random.randint(jax.random.fold_in(stream_key, axis), (), 0, extent[axis]) for axis in range(len(extent))]
    values = values.at[tuple(spot)].set(least)
    longest = extent.index(max(extent))
    spot[longest] = (spot[longest] + 1) % extent[longest]
    return values.at[tuple(spot)].set(top_value)


def block_scale(key, extent, split, smallest, top_value):
    loudness, own = 1.0, jax.random.fold_in(key, 6)
    for position, shards_of in split:
        draws = jnp.exp(jax.random.uniform(jax.random.fold_in(own, position), (shards_of,), jnp.float32, smallest / len(split), top_value / len(split)))
        loudness = loudness * jnp.repeat(draws, extent[position] // shards_of).reshape([-1 if axis == position else 1 for axis in range(len(extent))])
    return loudness


def bell_draw(stream_key, dims, scale, most, split=(), dtype=jnp.bfloat16):
    entries = scale * jax.random.normal(stream_key, dims, jnp.float32)
    if split:
        entries = entries * block_scale(stream_key, dims, split, -0.22, 0.18)
    return jnp.clip(entries, -most, most).astype(dtype)


def setup_inputs(seed: int = 0) -> dict:
    streams_of = jax.random.split(jax.random.key(seed), 22)
    tokens = bell_draw(streams_of[0], (ROWS, SEQ_LEN, D), 1.0, 6.0, ((0, 8), (1, 4)))
    cotangent = bell_draw(streams_of[1], (ROWS, SEQ_LEN, D), 1.0, 6.0, ((0, 8), (1, 4)))
    row_lengths = plant(jax.random.randint(streams_of[2], (ROWS,), SEQ_LEN // 2, SEQ_LEN + 1), jax.random.fold_in(streams_of[2], 1), SEQ_LEN // 2, SEQ_LEN).astype(jnp.int32)
    source_lengths = plant(jax.random.randint(streams_of[3], (ROWS,), SEQ_LEN * 30 // 1024, SEQ_LEN * 400 // 1024 + 1), jax.random.fold_in(streams_of[3], 1), SEQ_LEN * 30 // 1024, (SEQ_LEN * 400 // 1024 + 1) - 1).astype(jnp.int32)
    first_gain = jnp.clip(1.0 + 0.18 * jax.random.normal(streams_of[4], (D,), jnp.float32), 0.1, 1.9)
    first_shift = bell_draw(streams_of[5], (D,), 0.3, 2.0, (), jnp.float32)
    attend_weight = bell_draw(streams_of[6], (D, 3 * D), (D // 2) ** -0.5, 0.25)
    attend_bias = bell_draw(streams_of[7], (3 * D,), 0.3, 2.0, (), jnp.float32)
    output_weight = bell_draw(streams_of[8], (D, D), (D // 16) ** -0.5, 0.75)
    output_bias = bell_draw(streams_of[9], (D,), 0.3, 2.0, (), jnp.float32)
    second_gain = jnp.clip(1.0 + 0.18 * jax.random.normal(streams_of[10], (D,), jnp.float32), 0.1, 1.9)
    second_shift = bell_draw(streams_of[11], (D,), 0.3, 2.0, (), jnp.float32)
    expand_weight = bell_draw(streams_of[12], (D, FF), D ** -0.5, 0.1875)
    expand_bias = bell_draw(streams_of[13], (FF,), 0.3, 2.0, (), jnp.float32)
    contract_weight = bell_draw(streams_of[14], (FF, D), FF ** -0.5, 0.09375)
    contract_bias = bell_draw(streams_of[15], (D,), 0.3, 2.0, (), jnp.float32)
    prefix_table = bell_draw(streams_of[16], (PREFIX, D), 1.0, 6.0)
    lift_weight = bell_draw(streams_of[17], (D, PRE_HID), D ** -0.5, 0.1875)
    lift_bias = bell_draw(streams_of[18], (PRE_HID,), 0.3, 2.0, (), jnp.float32)
    fan_weight = bell_draw(streams_of[19], (PRE_HID, KV_WIDTH), (PRE_HID // 2) ** -0.5, 0.375)
    fan_bias = bell_draw(streams_of[20], (KV_WIDTH,), 0.3, 2.0, (), jnp.float32)
    return {"tokens": tokens, "cotangent": cotangent, "row_lengths": row_lengths, "source_lengths": source_lengths, "first_gain": first_gain, "first_shift": first_shift, "attend_weight": attend_weight, "attend_bias": attend_bias, "output_weight": output_weight, "output_bias": output_bias, "second_gain": second_gain, "second_shift": second_shift, "expand_weight": expand_weight, "expand_bias": expand_bias, "contract_weight": contract_weight, "contract_bias": contract_bias, "prefix_table": prefix_table, "lift_weight": lift_weight, "lift_bias": lift_bias, "fan_weight": fan_weight, "fan_bias": fan_bias}


@jax.custom_vjp
def low(v):
    return lax.optimization_barrier(v.astype(jnp.bfloat16)).astype(jnp.float32)

@jax.custom_vjp
def low_back(v):
    return v

def low_keep(v):
    return (low(v), None)

def low_pass(kept, grad):
    return (grad,)

def back_keep(v):
    return (v, None)

def back_low(kept, grad):
    return (low(grad),)
low.defvjp(low_keep, low_pass)
low_back.defvjp(back_keep, back_low)
best_precision = lax.Precision.HIGHEST

def matmul(left, right):
    return jnp.dot(left, right, precision=best_precision)

def layer_norm(values, norm_gain, norm_shift):
    centred = values - lax.optimization_barrier(jnp.mean(values, axis=-1, keepdims=True))
    variance = lax.optimization_barrier(jnp.mean(centred * centred, axis=-1, keepdims=True))
    return centred * lax.rsqrt(variance + 1e-05) * norm_gain + norm_shift

def gelu_tanh(values):
    return jax.nn.gelu(values, approximate=True)

def attend_row(item, frozen, prefix_keyval):
    row_values_in, length = item
    first_gain, first_shift, attend_weight, attend_bias, output_weight, output_bias, second_gain, second_shift, expand_weight, expand_bias, contract_weight, contract_bias = frozen
    seq_total = row_values_in.shape[0]
    normed = low(layer_norm(row_values_in, first_gain, first_shift))
    project = matmul(normed, attend_weight) + attend_bias
    queries = low_back(low(project[:, :D])).reshape(seq_total, HEADS, HEAD_DIM)
    row_keyval = low_back(low(project[:, D:]))
    row_keys = row_keyval[:, :D].reshape(seq_total, HEADS, HEAD_DIM)
    row_values = row_keyval[:, D:].reshape(seq_total, HEADS, HEAD_DIM)
    prefix_keys = prefix_keyval[:, :D].reshape(PREFIX, HEADS, HEAD_DIM)
    prefix_values = prefix_keyval[:, D:].reshape(PREFIX, HEADS, HEAD_DIM)
    scores = low_back(jnp.einsum('qhd,khd->hqk', queries, row_keys, precision=best_precision) * 0.125)
    prefix_scores = low_back(jnp.einsum('qhd,phd->hqp', queries, prefix_keys, precision=best_precision) * 0.125)
    places = jnp.arange(seq_total)
    visible = (places[None, :] <= places[:, None]) & (places[None, :] < length)
    scores = jnp.where(visible[None], scores, -jnp.inf)
    highest = jnp.maximum(lax.optimization_barrier(jnp.max(scores, axis=-1, keepdims=True)), lax.optimization_barrier(jnp.max(prefix_scores, axis=-1, keepdims=True)))
    denominator = lax.optimization_barrier(jnp.sum(jnp.exp(scores - highest), axis=-1, keepdims=True)) + lax.optimization_barrier(jnp.sum(jnp.exp(prefix_scores - highest), axis=-1, keepdims=True))
    log_total = highest + jnp.log(denominator)
    weights = jnp.exp(scores - log_total)
    prefix_weights = jnp.exp(prefix_scores - log_total)
    attended = jnp.einsum('hqk,khd->qhd', low(weights), row_values, precision=best_precision)
    attended = attended + jnp.einsum('hqp,phd->qhd', low(prefix_weights), prefix_values, precision=best_precision)
    mixed_heads = low_back(low(attended.reshape(seq_total, D)))
    residual = row_values_in + low_back(matmul(mixed_heads, output_weight)) + output_bias
    normed_two = low(layer_norm(residual, second_gain, second_shift))
    expanded = low_back(matmul(normed_two, expand_weight) + expand_bias)
    activated = low(gelu_tanh(expanded))
    return residual + matmul(activated, contract_weight) + contract_bias

def reference(tokens, cotangent, row_lengths, source_lengths, first_gain, first_shift, attend_weight, attend_bias, output_weight, output_bias, second_gain, second_shift, expand_weight, expand_bias, contract_weight, contract_bias, prefix_table, lift_weight, lift_bias, fan_weight, fan_bias):
    frozen = (first_gain, first_shift, attend_weight.astype(jnp.float32), attend_bias, output_weight.astype(jnp.float32), output_bias, second_gain, second_shift, expand_weight.astype(jnp.float32), expand_bias, contract_weight.astype(jnp.float32), contract_bias)

    def forward(inputs, table_values, lift_matrix, lift_vector, fan_matrix, fan_vector):
        lifted = jnp.tanh(matmul(table_values, lift_matrix) + lift_vector)
        prefix_keyval = low(matmul(low(lifted), fan_matrix) + fan_vector)

        def one_row(item):
            return attend_row(item, frozen, prefix_keyval)
        return lax.map(jax.checkpoint(one_row), (inputs, row_lengths))
    result, backward = jax.vjp(forward, tokens.astype(jnp.float32), prefix_table.astype(jnp.float32), lift_weight.astype(jnp.float32), lift_bias, fan_weight.astype(jnp.float32), fan_bias)
    places = jnp.arange(SEQ_LEN)
    target = (places[None, :] >= source_lengths[:, None]) & (places[None, :] < row_lengths[:, None])
    grad_out = jnp.where(target[:, :, None], cotangent.astype(jnp.float32), jnp.zeros((), jnp.float32))
    grads = backward(grad_out)
    return (result.astype(jnp.bfloat16), grads[0], grads[1], grads[2], grads[3], grads[4], grads[5])
```

```python
import functools

import jax
import jax.numpy as jnp
from jax import lax
from jax.experimental import pallas as pl
from jax.experimental.pallas import tpu as pltpu
from jax.sharding import PartitionSpec as P

D = 1024
HEADS = 16
HEAD_DIM = 64
PAIRS = HEADS // 2
PREFIX = 10
PREFIX_PAD = 16
LEAST_LENGTH = 512
NN = (((1,), (0,)), ((), ()))
NT = (((1,), (1,)), ((), ()))
MIB = 1 << 20
BF16 = jnp.bfloat16
F32 = jnp.float32


def dot(left, right, dims=NN):
    return lax.dot_general(left, right, dims, preferred_element_type=F32)


def params(limit, steps):
    return pltpu.CompilerParams(
        dimension_semantics=("arbitrary",) * steps, vmem_limit_bytes=limit * MIB
    )


def normalize(values):
    centred = values - jnp.mean(values, axis=-1, keepdims=True)
    scale = lax.rsqrt(jnp.mean(centred * centred, axis=-1, keepdims=True) + 1e-05)
    return centred * scale, scale


def norm_back(grad, normed, scale):
    return scale * (
        grad
        - jnp.mean(grad, axis=-1, keepdims=True)
        - normed * jnp.mean(grad * normed, axis=-1, keepdims=True)
    )


def project_kernel(has_queries, tokens_ref, gain_ref, shift_ref, weight_ref, bias_ref, *rest):
    if has_queries:
        query_ref, keyval_ref, normed_ref = rest
    else:
        keyval_ref, normed_ref = rest
    step = pl.program_id(0)
    rows, toks = tokens_ref.shape[0], tokens_ref.shape[1]
    tile = weight_ref.shape[1]
    query_steps = D // tile if has_queries else 0

    @pl.when(step == 0)
    def _():
        normed, _ = normalize(tokens_ref[...].reshape(rows * toks, D).astype(F32))
        normed_ref[...] = (normed * gain_ref[...] + shift_ref[...]).astype(BF16)

    result = (dot(normed_ref[...], weight_ref[...]) + bias_ref[...]).astype(BF16)
    if has_queries:

        @pl.when(step < query_steps)
        def _():
            query_ref[...] = (result * 0.125).reshape(rows, toks, tile)

    @pl.when(step >= query_steps)
    def _():
        keyval_ref[...] = result.reshape(rows, 1, toks, tile)


def project(tokens, gain, shift, weight, bias, has_queries, tile=512):
    rows, toks, _ = tokens.shape
    tiles = D // tile
    query_steps = tiles if has_queries else 0
    first = 0 if has_queries else tiles
    out_shape = [jax.ShapeDtypeStruct((rows, 2, toks, D), BF16)]

    def keyval_map(step):
        at = jnp.maximum(step - query_steps, 0)
        return (0, at // tiles, 0, at % tiles)

    out_specs = [pl.BlockSpec((rows, 1, toks, tile), keyval_map)]
    if has_queries:
        out_shape.insert(0, jax.ShapeDtypeStruct((rows, toks, D), BF16))
        out_specs.insert(
            0, pl.BlockSpec((rows, toks, tile), lambda step: (0, 0, jnp.minimum(step, tiles - 1)))
        )
    steps = query_steps + 2 * tiles
    return pl.pallas_call(
        functools.partial(project_kernel, has_queries),
        grid=(steps,),
        in_specs=[
            pl.BlockSpec((rows, toks, D), lambda step: (0, 0, 0)),
            pl.BlockSpec((1, D), lambda step: (0, 0)),
            pl.BlockSpec((1, D), lambda step: (0, 0)),
            pl.BlockSpec((D, tile), lambda step: (0, step + first)),
            pl.BlockSpec((1, tile), lambda step: (0, step + first)),
        ],
        out_specs=out_specs,
        out_shape=out_shape,
        scratch_shapes=[pltpu.VMEM((rows * toks, D), BF16)],
        compiler_params=params(40, 1),
        cost_estimate=pl.CostEstimate(
            flops=2 * rows * toks * D * tile * steps,
            bytes_accessed=2 * (D * tile * steps + rows * toks * (D + tile * steps)),
            transcendentals=0,
        ),
        name="project_own" if has_queries else "project_up",
    )(tokens, gain, shift, weight, bias)


def head_lanes(values, head):
    lanes = lax.broadcasted_iota(jnp.int32, values.shape, 1)
    keep = lanes < HEAD_DIM if head == 0 else lanes >= HEAD_DIM
    return jnp.where(keep, values, jnp.zeros_like(values))


def prefix_mask(values, fill):
    places = lax.broadcasted_iota(jnp.int32, values.shape, 0)
    return jnp.where(places < PREFIX, values, fill)


class Places:
    def __init__(self, toks, level_count):
        self.toks = toks
        self.level_count = level_count

    def masked(self, block):
        if block < 2:
            return True
        level = block // 2
        return (self.level_count - level) * 2 * self.toks > LEAST_LENGTH

    def limits(self, place, length):
        base = place * self.toks
        queries = base + lax.broadcasted_iota(jnp.int32, (1, self.toks), 1)
        return jnp.minimum(queries, length - 1)

    def visible(self, block, place, limit):
        if block == 0:
            base = place * self.toks
        else:
            base = (lax.bitwise_xor(place, block % 2) - (block // 2) * 2) * self.toks
        keys = lax.broadcasted_iota(jnp.int32, (self.toks, self.toks), 0)
        return keys <= limit - base


def spread_prefix(prefix):
    tiled = jnp.concatenate([prefix] * HEADS, axis=0)
    rows = lax.broadcasted_iota(jnp.int32, tiled.shape, 0) // PREFIX_PAD
    cols = lax.broadcasted_iota(jnp.int32, tiled.shape, 1) // HEAD_DIM
    return jnp.where(rows == cols, tiled, jnp.zeros_like(tiled))


def attend_kernel(places, first_row, pair_step, place_ref, length_ref, query_all_ref, query_ref, *rest):
    block_count = 2 * places.level_count
    keyval_refs = rest[:block_count]
    prefix_all_ref, prefix_ref, mixed_ref, total_ref, spread_ref, scores_ref, hide_ref = rest[block_count:]
    place = place_ref[0]
    level = place // 2
    length = length_ref[first_row + pl.program_id(0)]
    limit = places.limits(place, length)
    step = pl.program_id(1)
    masked_blocks = [block for block in range(block_count) if places.masked(block)]

    @pl.when((pl.program_id(0) == 0) & (step == 0))
    def _():
        spread_ref[...] = spread_prefix(prefix_all_ref[0])

    @pl.when(step == 0)
    def _():
        scores_ref[...] = dot(spread_ref[...], query_all_ref[0], NT)
        for at, block in enumerate(masked_blocks):
            hide_ref[at] = jnp.where(places.visible(block, place, limit), 0.0, -jnp.inf)

    def attend(blocks):
        def scores_of(at):
            pair, head = at // 2, at % 2
            cols = slice(pair * 128, (pair + 1) * 128)
            queries = head_lanes(query_ref[0, :, cols], head)
            spread = scores_ref[pl.ds(pl.multiple_of((step * pair_step * 2 + at) * PREFIX_PAD, PREFIX_PAD), PREFIX_PAD), :]
            prefix_scores = prefix_mask(spread, -jnp.inf)
            highest = jnp.max(prefix_scores, axis=0, keepdims=True)
            scores = []
            for block in range(blocks):
                part = dot(keyval_refs[block][0, 0, :, cols], queries, NT)
                if places.masked(block):
                    part = part + hide_ref[masked_blocks.index(block)]
                highest = jnp.maximum(highest, jnp.max(part, axis=0, keepdims=True))
                scores.append(part)
            return prefix_scores, scores, highest

        ahead = scores_of(0)
        outs = []
        for at in range(2 * pair_step):
            pair, head = at // 2, at % 2
            cols = slice(pair * 128, (pair + 1) * 128)
            prefix_scores, scores, highest = ahead
            if at + 1 < 2 * pair_step:
                ahead = scores_of(at + 1)
            if head == 0:
                values_t = [keyval_refs[block][0, 1, :, cols].T for block in range(blocks)]
                prefix_values_t = prefix_ref[1, :, cols].T
            rows = slice(head * HEAD_DIM, (head + 1) * HEAD_DIM)
            prefix_weights = jnp.exp(prefix_scores - highest)
            total = jnp.sum(prefix_weights, axis=0, keepdims=True)
            mixed = dot(prefix_values_t[rows], prefix_weights.astype(BF16))
            for block in range(blocks):
                weights = jnp.exp(scores[block] - highest)
                total = total + jnp.sum(weights, axis=0, keepdims=True)
                mixed = mixed + dot(values_t[block][rows], weights.astype(BF16))
            outs.append(mixed * (1.0 / total))
            total_ref[0, at : at + 1, :] = highest + jnp.log(total)
            if head == 1:
                mixed_ref[0, :, cols] = jnp.concatenate(outs, axis=0).T.astype(BF16)
                outs = []

    for levels in range(places.level_count):

        @pl.when(level == levels)
        def _():
            attend(2 * (levels + 1))


def block_spec(shape, first_row, pair_last=True):
    if len(shape) == 3:
        return pl.BlockSpec(
            (1, shape[1], shape[2]), lambda row, pair, *_: (row + first_row, 0, pair)
        )
    return pl.BlockSpec(
        (1, shape[1], shape[2], shape[3]), lambda row, pair, *_: (row + first_row, 0, 0, pair)
    )


def attend(place, lengths, queries, keyvals, prefix_keyval, first_row, row_count, pair_step=4):
    toks = queries.shape[1]
    places = Places(toks, len(keyvals) // 2)
    width = 128 * pair_step
    return pl.pallas_call(
        functools.partial(attend_kernel, places, first_row, pair_step),
        grid_spec=pltpu.PrefetchScalarGridSpec(
            num_scalar_prefetch=2,
            grid=(row_count, PAIRS // pair_step),
            in_specs=[
                pl.BlockSpec((1, toks, D), lambda row, pair, *_: (row + first_row, 0, 0)),
                block_spec((1, toks, width), first_row),
            ]
            + [block_spec((1, 2, toks, width), row) for _, row in keyvals]
            + [
                pl.BlockSpec((2, PREFIX_PAD, D), lambda row, pair, *_: (0, 0, 0)),
                pl.BlockSpec((2, PREFIX_PAD, width), lambda row, pair, *_: (0, 0, pair)),
            ],
            out_specs=[
                block_spec((1, toks, width), 0),
                pl.BlockSpec((1, 2 * pair_step, toks), lambda row, pair, *_: (row, pair, 0)),
            ],
            scratch_shapes=[
                pltpu.VMEM((HEADS * PREFIX_PAD, D), BF16),
                pltpu.VMEM((HEADS * PREFIX_PAD, toks), F32),
                pltpu.VMEM((sum(places.masked(b) for b in range(len(keyvals))), toks, toks), F32),
            ],
        ),
        out_shape=[
            jax.ShapeDtypeStruct((row_count, toks, D), BF16),
            jax.ShapeDtypeStruct((row_count, HEADS, toks), F32),
        ],
        compiler_params=params(40, 2),
        cost_estimate=pl.CostEstimate(
            flops=row_count * 16 * 4 * toks * toks * len(keyvals) * 256,
            bytes_accessed=row_count * toks * D * 2 * (2 + 2 * len(keyvals)),
            transcendentals=row_count * HEADS * toks * toks * len(keyvals),
        ),
        name="attend",
    )(place, lengths, queries, queries, *[array for array, _ in keyvals], prefix_keyval, prefix_keyval)


def prefix_back_kernel(query_ref, grad_ref, mixed_ref, total_ref, prefix_ref, inner_ref, start_ref, prefix_grad_ref, spread_ref):
    row = pl.program_id(0)
    toks = query_ref.shape[1]

    @pl.when(row == 0)
    def _():
        spread_ref[0] = spread_prefix(prefix_ref[0])
        spread_ref[1] = spread_prefix(prefix_ref[1])
        prefix_grad_ref[...] = jnp.zeros_like(prefix_grad_ref)

    queries = query_ref[0]
    grads = grad_ref[0]
    product = grads.astype(F32) * mixed_ref[0].astype(F32)
    head_of = lax.broadcasted_iota(jnp.int32, (HEADS, D), 1) // HEAD_DIM
    chosen = jnp.where(head_of == lax.broadcasted_iota(jnp.int32, (HEADS, D), 0), 1.0, 0.0).astype(BF16)
    high = product.astype(BF16)
    low = (product - high.astype(F32)).astype(BF16)
    inner = dot(chosen, high, NT) + dot(chosen, low, NT)
    inner_ref[0] = inner

    def per_head(values):
        return values.reshape(HEADS, PREFIX_PAD, toks)

    scores = per_head(dot(spread_ref[0], queries, NT))
    grad_weights = per_head(dot(spread_ref[1], grads, NT))
    weights = jnp.exp(scores - total_ref[0][:, None, :])
    valid = lax.broadcasted_iota(jnp.int32, weights.shape, 1) < PREFIX
    weights = jnp.where(valid, weights, 0.0)
    grad_scores = weights * (grad_weights - inner[:, None, :])
    weights = weights.reshape(HEADS * PREFIX_PAD, toks).astype(BF16)
    grad_scores = grad_scores.reshape(HEADS * PREFIX_PAD, toks).astype(BF16)
    start_ref[0] = dot(grad_scores.T, spread_ref[0])
    own = (
        lax.broadcasted_iota(jnp.int32, (HEADS * PREFIX_PAD, D), 0) // PREFIX_PAD
        == lax.broadcasted_iota(jnp.int32, (HEADS * PREFIX_PAD, D), 1) // HEAD_DIM
    )

    def gather(values):
        return jnp.sum(jnp.where(own, values, 0.0).reshape(HEADS, PREFIX_PAD, D), axis=0)

    prefix_grad_ref[0] += gather(dot(grad_scores, queries))
    prefix_grad_ref[1] += gather(dot(weights, grads))


def prefix_back(queries, grads, mixed, total, prefix_keyval, first_row):
    row_count, toks, _ = grads.shape
    row_block = pl.BlockSpec((1, toks, D), lambda row: (row, 0, 0))
    head_block = pl.BlockSpec((1, HEADS, toks), lambda row: (row, 0, 0))
    return pl.pallas_call(
        prefix_back_kernel,
        grid=(row_count,),
        in_specs=[
            pl.BlockSpec((1, toks, D), lambda row: (row + first_row, 0, 0)),
            row_block,
            row_block,
            head_block,
            pl.BlockSpec((2, PREFIX_PAD, D), lambda row: (0, 0, 0)),
        ],
        out_specs=[
            head_block,
            row_block,
            pl.BlockSpec((2, PREFIX_PAD, D), lambda row: (0, 0, 0)),
        ],
        out_shape=[
            jax.ShapeDtypeStruct((row_count, HEADS, toks), F32),
            jax.ShapeDtypeStruct((row_count, toks, D), F32),
            jax.ShapeDtypeStruct((2, PREFIX_PAD, D), F32),
        ],
        scratch_shapes=[pltpu.VMEM((2, HEADS * PREFIX_PAD, D), BF16)],
        compiler_params=params(40, 1),
        cost_estimate=pl.CostEstimate(
            flops=row_count * 12 * toks * D * 256,
            bytes_accessed=row_count * toks * D * 10,
            transcendentals=row_count * toks * 256,
        ),
        name="prefix_back",
    )(queries, grads, mixed, total, prefix_keyval)


def attend_back_kernel(places, blocks, first_row, pair_step, final, place_ref, length_ref, query_ref, grad_ref, total_ref, inner_ref, start_ref, *rest):
    count = len(blocks)
    keyval_refs = dict(zip(blocks, rest[:count]))
    grad_query_ref = rest[count]
    out_refs = dict(zip(blocks, rest[count + 1 : 2 * count + 1]))
    hide_ref = rest[2 * count + 1]
    place = place_ref[0]
    level = place // 2
    length = length_ref[first_row + pl.program_id(0)]
    limit = places.limits(place, length)
    masked_blocks = [block for block in blocks if places.masked(block)]

    if masked_blocks:

        @pl.when(pl.program_id(1) == 0)
        def _():
            for at, block in enumerate(masked_blocks):
                hide_ref[at] = jnp.where(places.visible(block, place, limit), 0.0, -jnp.inf)

    def back(active):
        def products_of(at):
            pair, head = at // 2, at % 2
            cols = slice(pair * 128, (pair + 1) * 128)
            queries = head_lanes(query_ref[0, :, cols], head)
            grads = head_lanes(grad_ref[0, :, cols], head)
            scores = {}
            grad_weights = {}
            for block in active:
                part = dot(keyval_refs[block][0, 0, :, cols], queries, NT)
                if block in masked_blocks:
                    part = part + hide_ref[masked_blocks.index(block)]
                scores[block] = part
                grad_weights[block] = dot(keyval_refs[block][0, 1, :, cols], grads, NT)
            return queries, grads, scores, grad_weights

        ahead = products_of(0)
        for at in range(2 * pair_step):
            pair, head = at // 2, at % 2
            cols = slice(pair * 128, (pair + 1) * 128)
            queries, grads, scores, grad_weights = ahead
            if at + 1 < 2 * pair_step:
                ahead = products_of(at + 1)
            if head == 0:
                keys_t = {block: keyval_refs[block][0, 0, :, cols].T for block in active}
                grad_keys = {}
                grad_values = {}
                outs = []
            total = total_ref[0, at : at + 1, :]
            inner = inner_ref[0, at : at + 1, :]
            rows = slice(head * HEAD_DIM, (head + 1) * HEAD_DIM)
            grad_query = None
            for block in active:
                weights = jnp.exp(scores[block] - total)
                grad_scores = (weights * (grad_weights[block] - inner)).astype(BF16)
                part_values = dot(weights.astype(BF16), grads)
                part_keys = dot(grad_scores, queries)
                part_query = dot(keys_t[block][rows], grad_scores)
                if head == 0:
                    grad_values[block], grad_keys[block] = part_values, part_keys
                else:
                    out_refs[block][0, 0, :, cols] = (grad_keys[block] + part_keys).astype(BF16)
                    out_refs[block][0, 1, :, cols] = (grad_values[block] + part_values).astype(BF16)
                grad_query = part_query if grad_query is None else grad_query + part_query
            outs.append(grad_query)
            if head == 1:
                grad_query = jnp.concatenate(outs, axis=0).T + start_ref[0, :, cols]
                if final:
                    grad_query = (grad_query * 0.125).astype(BF16)
                grad_query_ref[0, :, cols] = grad_query

    for levels in range(places.level_count):
        active = [block for block in blocks if block < 2 * (levels + 1)]

        @pl.when(level == levels)
        def _():
            if active:
                back(active)
            else:
                grad_query_ref[...] = start_ref[...]


def attend_back(place, lengths, queries, grads, total, inner, start, keyvals, level_count, first_row, final, pair_step=4):
    row_count, toks, _ = grads.shape
    blocks = sorted(keyvals)
    places = Places(toks, level_count)
    width = 128 * pair_step
    row_block = block_spec((1, toks, width), 0)
    head_block = pl.BlockSpec((1, 2 * pair_step, toks), lambda row, pair, *_: (row, pair, 0))
    masked = max(1, sum(places.masked(block) for block in blocks))
    return pl.pallas_call(
        functools.partial(attend_back_kernel, places, blocks, first_row, pair_step, final),
        grid_spec=pltpu.PrefetchScalarGridSpec(
            num_scalar_prefetch=2,
            grid=(row_count, PAIRS // pair_step),
            in_specs=[block_spec((1, toks, width), first_row), row_block, head_block, head_block, row_block]
            + [block_spec((1, 2, toks, width), keyvals[block][1]) for block in blocks],
            out_specs=[row_block] + [block_spec((1, 2, toks, width), 0)] * len(blocks),
            scratch_shapes=[pltpu.VMEM((masked, toks, toks), F32)],
        ),
        out_shape=[jax.ShapeDtypeStruct((row_count, toks, D), BF16 if final else F32)]
        + [jax.ShapeDtypeStruct((row_count, 2, toks, D), BF16)] * len(blocks),
        compiler_params=params(48, 2),
        cost_estimate=pl.CostEstimate(
            flops=row_count * HEADS * 10 * toks * toks * len(blocks) * 256,
            bytes_accessed=row_count * toks * D * 2 * (5 + 4 * len(blocks)),
            transcendentals=row_count * HEADS * toks * toks * len(blocks),
        ),
        name="attend_back",
    )(place, lengths, queries, grads, total, inner, start, *[keyvals[block][0] for block in blocks])


GELU_SCALE = 0.7978845608028654
GELU_CUBE = 0.044715


def feed_forward_kernel(first_row, sub, place_ref, length_ref, source_ref, tokens_ref, cotangent_ref, mixed_ref, output_weight_ref, output_bias_ref, gain_ref, shift_ref, expand_weight_ref, expand_bias_ref, contract_weight_ref, contract_bias_ref, *rest):
    activations_ref, grad_residual_ref, grad_heads_ref, residual_ref, normed_ref, grad_out_ref, active_ref, grad_expand_ref, result_ref, grad_normed_ref = rest[-10:]
    step = pl.program_id(0)
    rows, toks, _ = tokens_ref.shape
    count = rows * toks
    tile = expand_weight_ref.shape[1]

    @pl.when(step == 0)
    def _():
        projected = dot(mixed_ref[...].reshape(count, D), output_weight_ref[...])
        residual = tokens_ref[...].reshape(count, D).astype(F32) + projected + output_bias_ref[...]
        residual_ref[...] = residual
        normed, _ = normalize(residual)
        normed_ref[...] = (normed * gain_ref[...] + shift_ref[...]).astype(BF16)
        spots = place_ref[0] * toks + lax.broadcasted_iota(jnp.int32, (toks, D), 0)
        for row in range(rows):
            target = (spots >= source_ref[first_row + row]) & (spots < length_ref[first_row + row])
            values = cotangent_ref[row].astype(F32)
            grad_out_ref[row * toks : (row + 1) * toks, :] = jnp.where(target, values, 0.0).astype(BF16)

    for at in range(tile // sub):
        cols = slice(at * sub, (at + 1) * sub)
        values = dot(normed_ref[...], expand_weight_ref[:, cols]) + expand_bias_ref[:, cols]
        grad_hidden = dot(grad_out_ref[...], contract_weight_ref[cols, :], NT)
        square = values * values
        bend = jnp.tanh(values * (GELU_SCALE + GELU_SCALE * GELU_CUBE * square))
        half = 0.5 * (1.0 + bend)
        slope = half + (0.5 * values) * (1.0 - bend * bend) * (
            GELU_SCALE + 3.0 * GELU_SCALE * GELU_CUBE * square
        )
        active_ref[:, cols] = (values * half).astype(BF16)
        grad_expand_ref[:, cols] = (grad_hidden * slope).astype(BF16)

    part = dot(active_ref[...], contract_weight_ref[...])
    grad_part = dot(grad_expand_ref[...], expand_weight_ref[...], NT)

    @pl.when(step == 0)
    def _():
        result_ref[...] = part
        grad_normed_ref[...] = grad_part

    @pl.when(step > 0)
    def _():
        result_ref[...] += part
        grad_normed_ref[...] += grad_part

    @pl.when(step == pl.num_programs(0) - 1)
    def _():
        residual = residual_ref[...]
        activations_ref[...] = (residual + result_ref[...] + contract_bias_ref[...]).astype(BF16).reshape(rows, toks, D)
        normed, scale = normalize(residual)
        grad = grad_out_ref[...].astype(F32) + norm_back(grad_normed_ref[...] * gain_ref[...], normed, scale)
        grad_residual_ref[...] = grad.reshape(rows, toks, D)
        heads = dot(grad.astype(BF16), output_weight_ref[...], NT)
        grad_heads_ref[...] = heads.astype(BF16).reshape(rows, toks, D)


def feed_forward(place, lengths, sources, tokens, cotangent, mixed, weights, first_row, earlier, tile=512, sub=256):
    row_count, toks, _ = mixed.shape
    count = row_count * toks
    output_weight, output_bias, gain, shift, expand_weight, expand_bias, contract_weight, contract_bias = weights
    hidden = expand_weight.shape[1]
    given = [] if earlier is None else [earlier]
    at_row = first_row // row_count

    def whole(shape):
        return pl.BlockSpec(shape, lambda step, *_: (0,) * len(shape))

    some_rows = pl.BlockSpec((row_count, toks, D), lambda step, *_: (at_row, 0, 0))
    return pl.pallas_call(
        functools.partial(feed_forward_kernel, first_row, sub),
        grid_spec=pltpu.PrefetchScalarGridSpec(
            num_scalar_prefetch=3,
            grid=(hidden // tile,),
            in_specs=[
                some_rows,
                some_rows,
                whole((row_count, toks, D)),
                whole((D, D)),
                whole((1, D)),
                whole((1, D)),
                whole((1, D)),
                pl.BlockSpec((D, tile), lambda step, *_: (0, step)),
                pl.BlockSpec((1, tile), lambda step, *_: (0, step)),
                pl.BlockSpec((tile, D), lambda step, *_: (step, 0)),
                whole((1, D)),
            ]
            + [pl.BlockSpec(memory_space=pl.ANY)] * len(given),
            out_specs=[some_rows, whole((row_count, toks, D)), whole((row_count, toks, D))],
            scratch_shapes=[
                pltpu.VMEM((count, D), F32),
                pltpu.VMEM((count, D), BF16),
                pltpu.VMEM((count, D), BF16),
                pltpu.VMEM((count, tile), BF16),
                pltpu.VMEM((count, tile), BF16),
                pltpu.VMEM((count, D), F32),
                pltpu.VMEM((count, D), F32),
            ],
        ),
        out_shape=[
            jax.ShapeDtypeStruct(tokens.shape, BF16),
            jax.ShapeDtypeStruct((row_count, toks, D), F32),
            jax.ShapeDtypeStruct((row_count, toks, D), BF16),
        ],
        input_output_aliases={14: 0} if given else {},
        compiler_params=params(56, 1),
        cost_estimate=pl.CostEstimate(
            flops=count * D * (8 * hidden + 4 * D),
            bytes_accessed=4 * D * hidden + 2 * D * D + 16 * count * D,
            transcendentals=count * hidden,
        ),
        name="feed_forward",
    )(place, lengths, sources, tokens, cotangent, mixed, output_weight, output_bias, gain, shift, expand_weight, expand_bias, contract_weight, contract_bias, *given)


def up_back_kernel(own_ref, received_ref, weight_ref, grad_ref, total_ref):
    step = pl.program_id(0)
    rows, _, toks, tile = own_ref.shape
    values = (own_ref[...].astype(F32) + received_ref[...].astype(F32)).astype(BF16)
    part = dot(values.reshape(rows * toks, tile), weight_ref[...], NT)

    @pl.when(step == 0)
    def _():
        total_ref[...] = part

    @pl.when(step > 0)
    def _():
        total_ref[...] += part

    @pl.when(step == pl.num_programs(0) - 1)
    def _():
        grad_ref[...] = total_ref[...].astype(BF16).reshape(rows, toks, D)


def up_back(own, received, weight, tile=512):
    rows, _, toks, _ = own.shape
    tiles = D // tile
    keyval = pl.BlockSpec((rows, 1, toks, tile), lambda step: (0, step // tiles, 0, step % tiles))
    return pl.pallas_call(
        up_back_kernel,
        grid=(2 * tiles,),
        in_specs=[keyval, keyval, pl.BlockSpec((D, tile), lambda step: (0, step + tiles))],
        out_specs=pl.BlockSpec((rows, toks, D), lambda step: (0, 0, 0)),
        out_shape=jax.ShapeDtypeStruct((rows, toks, D), BF16),
        scratch_shapes=[pltpu.VMEM((rows * toks, D), F32)],
        compiler_params=params(40, 1),
        cost_estimate=pl.CostEstimate(
            flops=4 * rows * toks * D * D, bytes_accessed=4 * D * D + 10 * rows * toks * D, transcendentals=0
        ),
        name="up_back",
    )(own, received, weight)


def project_back_kernel(level_count, tokens_ref, gain_ref, residual_ref, query_ref, own_ref, received_ref, weight_ref, *rest):
    above_refs = rest[: level_count - 1]
    grad_ref, total_ref = rest[-2:]
    step = pl.program_id(0)
    rows, toks, tile = query_ref.shape
    count = rows * toks
    query_steps = D // tile

    @pl.when(step == 0)
    def _():
        total_ref[...] = dot(query_ref[...].reshape(count, tile), weight_ref[...], NT)

    @pl.when((step > 0) & (step < query_steps))
    def _():
        total_ref[...] += dot(query_ref[...].reshape(count, tile), weight_ref[...], NT)

    @pl.when(step >= query_steps)
    def _():
        values = (own_ref[...].astype(F32) + received_ref[...].astype(F32)).astype(BF16)
        total_ref[...] += dot(values.reshape(count, tile), weight_ref[...], NT)

    @pl.when(step == pl.num_programs(0) - 1)
    def _():
        total = total_ref[...]
        for above_ref in above_refs:
            total = total + above_ref[...].reshape(count, D).astype(F32)
        normed, scale = normalize(tokens_ref[...].reshape(count, D).astype(F32))
        grad = norm_back(total * gain_ref[...], normed, scale)
        grad_ref[...] = residual_ref[...] + grad.reshape(rows, toks, D)


def project_back(tokens, gain, grad_residual, grad_queries, own, received, weight, above, first_row, earlier, tile=512):
    row_count, toks, _ = grad_queries.shape
    count = row_count * toks
    tiles = D // tile
    at_row = first_row // row_count
    given = [] if earlier is None else [earlier]

    def keyval_map(step):
        at = jnp.maximum(step - tiles, 0)
        return (0, at // tiles, 0, at % tiles)

    some_rows = pl.BlockSpec((row_count, toks, D), lambda step: (at_row, 0, 0))
    all_rows = pl.BlockSpec((row_count, toks, D), lambda step: (0, 0, 0))
    keyval = pl.BlockSpec((row_count, 1, toks, tile), keyval_map)
    return pl.pallas_call(
        functools.partial(project_back_kernel, len(above) + 1),
        grid=(3 * tiles,),
        in_specs=[
            some_rows,
            pl.BlockSpec((1, D), lambda step: (0, 0)),
            all_rows,
            pl.BlockSpec((row_count, toks, tile), lambda step: (0, 0, jnp.minimum(step, tiles - 1))),
            keyval,
            keyval,
            pl.BlockSpec((D, tile), lambda step: (0, step)),
        ]
        + [all_rows] * len(above)
        + [pl.BlockSpec(memory_space=pl.ANY)] * len(given),
        out_specs=some_rows,
        out_shape=jax.ShapeDtypeStruct(tokens.shape, F32),
        scratch_shapes=[pltpu.VMEM((count, D), F32)],
        input_output_aliases={7 + len(above): 0} if given else {},
        compiler_params=params(40, 1),
        cost_estimate=pl.CostEstimate(
            flops=6 * count * D * D, bytes_accessed=6 * D * D + 20 * count * D, transcendentals=0
        ),
        name="project_back",
    )(tokens, gain, grad_residual, grad_queries, own, received, weight, *above, *given)


def prefix_kernel(table_ref, lift_ref, lift_bias_ref, fan_ref, fan_bias_ref, lifted_ref, keyval_ref):
    lifted = jnp.tanh(dot(table_ref[...], lift_ref[...]) + lift_bias_ref[...])
    lifted_ref[...] = jnp.zeros_like(lifted_ref)
    lifted_ref[:PREFIX, :] = lifted
    keyval_ref[...] = jnp.zeros_like(keyval_ref)
    keyval = (dot(lifted.astype(BF16), fan_ref[...]) + fan_bias_ref[...]).astype(BF16)
    keyval_ref[0, :PREFIX, :] = keyval[:, :D]
    keyval_ref[1, :PREFIX, :] = keyval[:, D:]


def prefix_forward(table, lift, lift_bias, fan, fan_bias):
    return pl.pallas_call(
        prefix_kernel,
        out_shape=[
            jax.ShapeDtypeStruct((PREFIX_PAD, lift.shape[1]), F32),
            jax.ShapeDtypeStruct((2, PREFIX_PAD, D), BF16),
        ],
        compiler_params=pltpu.CompilerParams(vmem_limit_bytes=32 * MIB),
        name="prefix_forward",
    )(table, lift, lift_bias, fan, fan_bias)


def dot_split(left, right, dims=NN):
    if left.dtype == F32:
        high = left.astype(BF16)
        return dot(high, right, dims) + dot((left - high.astype(F32)).astype(BF16), right, dims)
    high = right.astype(BF16)
    return dot(left, high, dims) + dot(left, (right - high.astype(F32)).astype(BF16), dims)


def prefix_network_back_kernel(grad_ref, table_ref, lift_ref, fan_ref, lifted_ref, grad_table_ref, grad_lift_ref, grad_lift_bias_ref, grad_fan_ref, grad_fan_bias_ref):
    lifted = lifted_ref[...]
    lifted_t = lifted.astype(BF16).T
    grad_lifted = None
    for half in range(2):
        cols = slice(half * D, (half + 1) * D)
        grad = grad_ref[half]
        grad_fan_bias_ref[:, cols] = jnp.sum(grad, axis=0, keepdims=True)
        grad_fan_ref[:, cols] = dot_split(lifted_t, grad)
        part = dot_split(grad, fan_ref[:, cols], NT)
        grad_lifted = part if grad_lifted is None else grad_lifted + part
    grad_lifted = grad_lifted * (1.0 - lifted * lifted)
    grad_lift_bias_ref[...] = jnp.sum(grad_lifted, axis=0, keepdims=True)
    table = jnp.concatenate([table_ref[...], jnp.zeros((PREFIX_PAD - PREFIX, D), F32)], axis=0)
    grad_lift_ref[...] = dot_split(table.T.astype(BF16), grad_lifted)
    grad_table_ref[...] = dot_split(grad_lifted, lift_ref[...], NT)[:PREFIX]


def prefix_network_back(grad, table, lift, fan, lifted):
    hidden = lift.shape[1]
    return pl.pallas_call(
        prefix_network_back_kernel,
        out_shape=[
            jax.ShapeDtypeStruct((PREFIX, D), F32),
            jax.ShapeDtypeStruct((D, hidden), F32),
            jax.ShapeDtypeStruct((1, hidden), F32),
            jax.ShapeDtypeStruct((hidden, 2 * D), F32),
            jax.ShapeDtypeStruct((1, 2 * D), F32),
        ],
        compiler_params=pltpu.CompilerParams(vmem_limit_bytes=40 * MIB),
        name="prefix_network_back",
    )(grad, table.astype(F32), lift, fan, lifted)


def sum_everywhere(values, axes):
    for axis in axes:
        size = lax.axis_size(axis)
        if size & (size - 1):
            values = lax.psum(values, axis)
            continue
        hop = 1
        while hop < size:
            values = values + lax.ppermute(values, axis, [(at, at ^ hop) for at in range(size)])
            hop *= 2
    return values


def per_device(tokens, cotangent, row_lengths, source_lengths, first_gain, first_shift, attend_weight, attend_bias, output_weight, output_bias, second_gain, second_shift, expand_weight, expand_bias, contract_weight, contract_bias, prefix_table, lift_weight, lift_bias, fan_weight, fan_bias):
    rows = tokens.shape[0]
    seq = lax.axis_size("seq")
    level_count = seq // 2
    levels = range(1, level_count)
    mates = [(at, at ^ 1) for at in range(seq)]
    place = lax.axis_index("seq").astype(jnp.int32).reshape(1)
    first_gain, first_shift, attend_bias, output_bias, second_gain, second_shift, expand_bias, contract_bias, lift_bias, fan_bias = [
        vector.reshape(1, -1)
        for vector in (first_gain, first_shift, attend_bias, output_bias, second_gain, second_shift, expand_bias, contract_bias, lift_bias, fan_bias)
    ]
    weights = (output_weight, output_bias, second_gain, second_shift, expand_weight, expand_bias, contract_weight, contract_bias)
    lower_tokens = [
        [lax.ppermute(tokens[row : row + 1], "seq", [(at, at + 2 * level) for at in range(seq - 2 * level)]) for level in levels]
        for row in range(rows)
    ]
    queries, keyval = project(tokens, first_gain, first_shift, attend_weight, attend_bias, True)
    mate_keyval = lax.ppermute(keyval, "seq", mates)
    lifted, prefix_keyval = prefix_forward(prefix_table, lift_weight, lift_bias, fan_weight, fan_bias)

    activations = None
    input_grad = None
    prefix_grad = None
    for row in range(rows):
        keyvals = [(keyval, row), (mate_keyval, row)]
        for level in levels:
            (lower,) = project(lower_tokens[row][level - 1], first_gain, first_shift, attend_weight, attend_bias, False)
            keyvals += [(lower, 0), (lax.ppermute(lower, "seq", mates), 0)]
        mixed, total = attend(place, row_lengths, queries, keyvals, prefix_keyval, row, 1)
        activations, grad_residual, grad_heads = feed_forward(
            place, row_lengths, source_lengths, tokens, cotangent, mixed, weights, row, activations
        )
        inner, start, row_prefix_grad = prefix_back(queries, grad_heads, mixed, total, prefix_keyval, row)
        prefix_grad = row_prefix_grad if prefix_grad is None else prefix_grad + row_prefix_grad
        grad_queries, *grads = attend_back(
            place, row_lengths, queries, grad_heads, total, inner, start, dict(enumerate(keyvals)), level_count, row, True
        )
        received = lax.ppermute(grads[1], "seq", mates)
        above = []
        for level in levels:
            from_mate = lax.ppermute(grads[2 * level + 1], "seq", mates)
            part = up_back(grads[2 * level], from_mate, attend_weight)
            above.append(lax.ppermute(part, "seq", [(at + 2 * level, at) for at in range(seq - 2 * level)]))
        input_grad = project_back(tokens, first_gain, grad_residual, grad_queries, grads[0], received, attend_weight, above, row, input_grad)
    prefix_grad = sum_everywhere(prefix_grad, ("seq", "dp"))
    grad_table, grad_lift, grad_lift_bias, grad_fan, grad_fan_bias = prefix_network_back(prefix_grad, prefix_table, lift_weight, fan_weight, lifted)
    return (activations, input_grad, grad_table, grad_lift, grad_lift_bias.reshape(-1), grad_fan, grad_fan_bias.reshape(-1))


def solution(mesh):
    batch = P("dp", "seq", None)
    return jax.shard_map(
        per_device,
        mesh=mesh,
        in_specs=(batch, batch, P("dp"), P("dp")) + (P(),) * 17,
        out_specs=(batch, batch, P(), P(), P(), P(), P()),
        check_vma=False,
    )
```

```python
import functools

import jax
import jax.numpy as jnp
from jax import lax
from jax.experimental import pallas as pl
from jax.experimental.pallas import tpu as pltpu
from jax.sharding import PartitionSpec as P

D = 1024
HEADS = 16
HEAD_DIM = 64
PAIRS = HEADS // 2
PREFIX = 10
PREFIX_PAD = 16
LEAST_LENGTH = 512
NN = (((1,), (0,)), ((), ()))
NT = (((1,), (1,)), ((), ()))
MIB = 1 << 20
VMEM_LIMIT = 62 * MIB
COST_SHARE = 50
BF16 = jnp.bfloat16
F32 = jnp.float32


def dot(left, right, dims=NN):
    return lax.dot_general(left, right, dims, preferred_element_type=F32)


ANY = pl.BlockSpec(memory_space=pl.ANY)


def kernel_call(kernel, after, operands, prefetched=0, grid=None, in_specs=(), out_specs=None, scratch_shapes=(), **rest):
    lead = prefetched + len(in_specs)

    def body(*refs):
        kernel(*refs[:lead], *refs[lead + len(after) :])

    spec = pltpu.PrefetchScalarGridSpec(
        num_scalar_prefetch=prefetched,
        grid=grid or (1,),
        in_specs=[*in_specs] + [ANY] * len(after),
        out_specs=out_specs,
        scratch_shapes=scratch_shapes,
    )
    return pl.pallas_call(
        body,
        grid_spec=spec,
        compiler_params=pltpu.CompilerParams(
            dimension_semantics=("arbitrary",) * len(grid or (1,)), vmem_limit_bytes=VMEM_LIMIT
        ),
        **rest,
    )(*operands, *after)


def cost(flops, moved, transcendentals=0):
    return pl.CostEstimate(
        flops=int(flops * COST_SHARE), bytes_accessed=int(moved * COST_SHARE), transcendentals=int(transcendentals * COST_SHARE)
    )


def normalize(values):
    centred = values - jnp.mean(values, axis=-1, keepdims=True)
    scale = lax.rsqrt(jnp.mean(centred * centred, axis=-1, keepdims=True) + 1e-05)
    return centred * scale, scale


def norm_back(grad, normed, scale):
    return scale * (
        grad
        - jnp.mean(grad, axis=-1, keepdims=True)
        - normed * jnp.mean(grad * normed, axis=-1, keepdims=True)
    )


class Copies:
    def __init__(self, semaphores):
        self.semaphores = semaphores
        self.count = 0
        self.copies = {}

    def start(self, name, source, target):
        copy = pltpu.make_async_copy(source, target, self.semaphores.at[self.count])
        copy.start()
        self.count += 1
        self.copies[name] = copy

    def wait(self, name):
        self.copies[name].wait()


HBM = pl.BlockSpec(memory_space=pltpu.HBM)


def project_kernel(first, counts, tokens_hbm, gain_ref, shift_ref, bias_ref, weight_hbm, *rest):
    outs = rest[: len(counts)]
    tokens_ref, weight_ref, normed_ref, result_ref, semaphores = rest[len(counts):]
    rows, toks, _ = tokens_hbm.shape
    count = rows * toks
    chunks, _, chunk = weight_ref.shape
    copies = Copies(semaphores)
    copies.start("tokens", tokens_hbm, tokens_ref)
    for at in range(chunks):
        copies.start(at, weight_hbm.at[:, pl.ds((first + at) * chunk, chunk)], weight_ref.at[at])
    copies.wait("tokens")
    normed, _ = normalize(tokens_ref[...].reshape(count, D).astype(F32))
    normed_ref[...] = (normed * gain_ref[...] + shift_ref[...]).astype(BF16)
    tiles = D // chunk
    for at in range(chunks):
        spot = first + at
        copies.wait(at)
        result = (dot(normed_ref[...], weight_ref[at]) + bias_ref[:, spot * chunk : (spot + 1) * chunk]).astype(BF16)
        cols = pl.ds(spot % tiles * chunk, chunk)
        if spot < tiles:
            result = result * 0.125
            target = outs[0].at[:, :, cols]
        else:
            target = outs[-1].at[:, spot // tiles - 1, :, cols]
        result_ref[at] = result.reshape(rows, toks, chunk)
        copies.start(("out", at), result_ref.at[at], target)
    for at in range(chunks):
        copies.wait(("out", at))


def project(after, tokens, gain, shift, weight, bias, has_queries, chunk=512):
    rows, toks, _ = tokens.shape
    tiles = D // chunk
    first = 0 if has_queries else tiles
    chunks = 3 * tiles - first
    out_shape = [jax.ShapeDtypeStruct((rows, 2, toks, D), BF16)]
    if has_queries:
        out_shape.insert(0, jax.ShapeDtypeStruct((rows, toks, D), BF16))
    vmem = pl.BlockSpec(memory_space=pltpu.VMEM)
    return kernel_call(
        functools.partial(project_kernel, first, (1,) * len(out_shape)),
        after,
        (tokens, gain, shift, bias, weight),
        in_specs=[ANY, vmem, vmem, vmem, HBM],
        out_specs=[HBM] * len(out_shape),
        out_shape=out_shape,
        scratch_shapes=[
            pltpu.VMEM((rows, toks, D), BF16),
            pltpu.VMEM((chunks, D, chunk), BF16),
            pltpu.VMEM((rows * toks, D), BF16),
            pltpu.VMEM((chunks, rows, toks, chunk), BF16),
            pltpu.SemaphoreType.DMA((2 * chunks + 1,)),
        ],
        cost_estimate=cost(2 * rows * toks * D * chunk * chunks, 2 * (D + rows * toks) * chunk * chunks),
        name="project_own" if has_queries else "project_up",
    )


def head_lanes(values, head):
    lanes = lax.broadcasted_iota(jnp.int32, values.shape, 1)
    keep = lanes < HEAD_DIM if head == 0 else lanes >= HEAD_DIM
    return jnp.where(keep, values, jnp.zeros_like(values))


def prefix_mask(values, fill):
    places = lax.broadcasted_iota(jnp.int32, values.shape, 0)
    return jnp.where(places < PREFIX, values, fill)


class Places:
    def __init__(self, toks, level_count):
        self.toks = toks
        self.level_count = level_count

    def masked(self, block):
        if block < 2:
            return True
        level = block // 2
        return (self.level_count - level) * 2 * self.toks > LEAST_LENGTH

    def limits(self, place, length):
        base = place * self.toks
        queries = base + lax.broadcasted_iota(jnp.int32, (1, self.toks), 1)
        return jnp.minimum(queries, length - 1)

    def visible(self, block, place, limit):
        if block == 0:
            base = place * self.toks
        else:
            base = (lax.bitwise_xor(place, block % 2) - (block // 2) * 2) * self.toks
        keys = lax.broadcasted_iota(jnp.int32, (self.toks, self.toks), 0)
        return keys <= limit - base


def spread_prefix(prefix):
    tiled = jnp.concatenate([prefix] * HEADS, axis=0)
    rows = lax.broadcasted_iota(jnp.int32, tiled.shape, 0) // PREFIX_PAD
    cols = lax.broadcasted_iota(jnp.int32, tiled.shape, 1) // HEAD_DIM
    return jnp.where(rows == cols, tiled, jnp.zeros_like(tiled))


def attend_near_kernel(places, first_row, pair_step, place_ref, length_ref, query_all_ref, query_ref, own_ref, mate_ref, prefix_all_ref, prefix_ref, mixed_ref, total_ref, spread_ref, scores_ref, hide_ref):
    place = place_ref[0]
    limit = places.limits(place, length_ref[first_row + pl.program_id(0)])
    step = pl.program_id(1)
    keyval_refs = (own_ref, mate_ref)

    @pl.when((pl.program_id(0) == 0) & (step == 0))
    def _():
        spread_ref[...] = spread_prefix(prefix_all_ref[0])

    @pl.when(step == 0)
    def _():
        scores_ref[...] = dot(spread_ref[...], query_all_ref[0], NT)
        for block in range(2):
            hide_ref[block] = jnp.where(places.visible(block, place, limit), 0.0, -jnp.inf)

    def scores_of(at):
        pair, head = at // 2, at % 2
        cols = slice(pair * 128, (pair + 1) * 128)
        queries = head_lanes(query_ref[0, :, cols], head)
        spot = pl.multiple_of((step * pair_step * 2 + at) * PREFIX_PAD, PREFIX_PAD)
        prefix_scores = prefix_mask(scores_ref[pl.ds(spot, PREFIX_PAD), :], -jnp.inf)
        highest = jnp.max(prefix_scores, axis=0, keepdims=True)
        scores = []
        for block in range(2):
            part = dot(keyval_refs[block][0, 0, :, cols], queries, NT) + hide_ref[block]
            highest = jnp.maximum(highest, jnp.max(part, axis=0, keepdims=True))
            scores.append(part)
        return prefix_scores, scores, highest

    ahead = scores_of(0)
    for at in range(2 * pair_step):
        pair, head = at // 2, at % 2
        cols = slice(pair * 128, (pair + 1) * 128)
        prefix_scores, scores, highest = ahead
        if at + 1 < 2 * pair_step:
            ahead = scores_of(at + 1)
        if head == 0:
            values_t = [keyval_refs[block][0, 1, :, cols].T for block in range(2)]
            prefix_values_t = prefix_ref[1, :, cols].T
        rows = slice(head * HEAD_DIM, (head + 1) * HEAD_DIM)
        prefix_weights = jnp.exp(prefix_scores - highest)
        total = jnp.sum(prefix_weights, axis=0, keepdims=True)
        mixed = dot(prefix_values_t[rows], prefix_weights.astype(BF16))
        for block in range(2):
            weights = jnp.exp(scores[block] - highest)
            total = total + jnp.sum(weights, axis=0, keepdims=True)
            mixed = mixed + dot(values_t[block][rows], weights.astype(BF16))
        mixed_ref[0, at * HEAD_DIM : (at + 1) * HEAD_DIM, :] = mixed * (1.0 / total)
        total_ref[0, at : at + 1, :] = highest + jnp.log(total)


def attend_far_kernel(places, first_row, pair_step, place_ref, length_ref, query_ref, near_ref, near_total_ref, *rest):
    block_count = 2 * places.level_count
    keyval_refs = dict(zip(range(2, block_count), rest))
    mixed_ref, total_ref, hide_ref = rest[-3:]
    place = place_ref[0]
    level = place // 2
    limit = places.limits(place, length_ref[first_row + pl.program_id(0)])
    masked_blocks = [block for block in range(2, block_count) if places.masked(block)]

    if masked_blocks:

        @pl.when(pl.program_id(1) == 0)
        def _():
            for at, block in enumerate(masked_blocks):
                hide_ref[at] = jnp.where(places.visible(block, place, limit), 0.0, -jnp.inf)

    def attend(blocks):
        def scores_of(at):
            pair, head = at // 2, at % 2
            cols = slice(pair * 128, (pair + 1) * 128)
            queries = head_lanes(query_ref[0, :, cols], head)
            highest = near_total_ref[0, at : at + 1, :]
            scores = []
            for block in blocks:
                part = dot(keyval_refs[block][0, 0, :, cols], queries, NT)
                if block in masked_blocks:
                    part = part + hide_ref[masked_blocks.index(block)]
                highest = jnp.maximum(highest, jnp.max(part, axis=0, keepdims=True))
                scores.append(part)
            return scores, highest

        if blocks:
            ahead = scores_of(0)
        outs = []
        for at in range(2 * pair_step):
            pair, head = at // 2, at % 2
            cols = slice(pair * 128, (pair + 1) * 128)
            near = near_ref[0, at * HEAD_DIM : (at + 1) * HEAD_DIM, :]
            near_total = near_total_ref[0, at : at + 1, :]
            if blocks:
                scores, highest = ahead
                if at + 1 < 2 * pair_step:
                    ahead = scores_of(at + 1)
                if head == 0:
                    values_t = [keyval_refs[block][0, 1, :, cols].T for block in blocks]
                rows = slice(head * HEAD_DIM, (head + 1) * HEAD_DIM)
                total = jnp.exp(near_total - highest)
                mixed = near * total
                for values, part in zip(values_t, scores):
                    weights = jnp.exp(part - highest)
                    total = total + jnp.sum(weights, axis=0, keepdims=True)
                    mixed = mixed + dot(values[rows], weights.astype(BF16))
                near = mixed * (1.0 / total)
                near_total = highest + jnp.log(total)
            outs.append(near)
            total_ref[0, at : at + 1, :] = near_total
            if head == 1:
                mixed_ref[0, :, cols] = jnp.concatenate(outs, axis=0).T.astype(BF16)
                outs = []

    for levels in range(places.level_count):

        @pl.when(level == levels)
        def _():
            attend(list(range(2, 2 * (levels + 1))))


def block_spec(shape, first_row, pair_last=True):
    if len(shape) == 3:
        return pl.BlockSpec(
            (1, shape[1], shape[2]), lambda row, pair, *_: (row + first_row, 0, pair)
        )
    return pl.BlockSpec(
        (1, shape[1], shape[2], shape[3]), lambda row, pair, *_: (row + first_row, 0, 0, pair)
    )


def attend_near(after, place, lengths, queries, own, mate, prefix_keyval, level_count, first_row, row_count, pair_step=4):
    toks = queries.shape[1]
    width = 128 * pair_step
    return kernel_call(
        functools.partial(attend_near_kernel, Places(toks, level_count), first_row, pair_step),
        after,
        (place, lengths, queries, queries, own, mate, prefix_keyval, prefix_keyval),
        prefetched=2,
        grid=(row_count, PAIRS // pair_step),
        in_specs=[
            pl.BlockSpec((1, toks, D), lambda row, pair, *_: (row + first_row, 0, 0)),
            block_spec((1, toks, width), first_row),
            block_spec((1, 2, toks, width), first_row),
            block_spec((1, 2, toks, width), first_row),
            pl.BlockSpec((2, PREFIX_PAD, D), lambda row, pair, *_: (0, 0, 0)),
            pl.BlockSpec((2, PREFIX_PAD, width), lambda row, pair, *_: (0, 0, pair)),
        ],
        out_specs=[
            pl.BlockSpec((1, width, toks), lambda row, pair, *_: (row, pair, 0)),
            pl.BlockSpec((1, 2 * pair_step, toks), lambda row, pair, *_: (row, pair, 0)),
        ],
        scratch_shapes=[
            pltpu.VMEM((HEADS * PREFIX_PAD, D), BF16),
            pltpu.VMEM((HEADS * PREFIX_PAD, toks), F32),
            pltpu.VMEM((2, toks, toks), F32),
        ],
        out_shape=[
            jax.ShapeDtypeStruct((row_count, D, toks), F32),
            jax.ShapeDtypeStruct((row_count, HEADS, toks), F32),
        ],
        cost_estimate=cost(row_count * 2048 * HEADS * toks * toks, row_count * toks * D * 14, row_count * HEADS * toks * toks * 2),
        name="attend_near",
    )


def attend_far(after, place, lengths, queries, near, near_total, keyvals, level_count, first_row, pair_step=4):
    row_count = near.shape[0]
    toks = queries.shape[1]
    width = 128 * pair_step
    places = Places(toks, level_count)
    masked = max(1, sum(places.masked(block) for block in range(2, 2 * level_count)))
    return kernel_call(
        functools.partial(attend_far_kernel, places, first_row, pair_step),
        after,
        (place, lengths, queries, near, near_total, *keyvals),
        prefetched=2,
        grid=(row_count, PAIRS // pair_step),
        in_specs=[
            block_spec((1, toks, width), first_row),
            pl.BlockSpec((1, width, toks), lambda row, pair, *_: (row, pair, 0)),
            pl.BlockSpec((1, 2 * pair_step, toks), lambda row, pair, *_: (row, pair, 0)),
        ]
        + [block_spec((1, 2, toks, width), 0)] * len(keyvals),
        out_specs=[
            block_spec((1, toks, width), 0),
            pl.BlockSpec((1, 2 * pair_step, toks), lambda row, pair, *_: (row, pair, 0)),
        ],
        scratch_shapes=[pltpu.VMEM((masked, toks, toks), F32)],
        out_shape=[
            jax.ShapeDtypeStruct((row_count, toks, D), BF16),
            jax.ShapeDtypeStruct((row_count, HEADS, toks), F32),
        ],
        cost_estimate=cost(
            row_count * 1024 * HEADS * toks * toks * len(keyvals),
            row_count * toks * D * (8 + 4 * len(keyvals)),
            row_count * HEADS * toks * toks * len(keyvals),
        ),
        name="attend_far",
    )


def prefix_back_kernel(query_ref, grad_ref, mixed_ref, total_ref, prefix_ref, inner_ref, start_ref, prefix_grad_ref, spread_ref):
    row = pl.program_id(0)
    toks = query_ref.shape[1]

    @pl.when(row == 0)
    def _():
        spread_ref[0] = spread_prefix(prefix_ref[0])
        spread_ref[1] = spread_prefix(prefix_ref[1])
        prefix_grad_ref[...] = jnp.zeros_like(prefix_grad_ref)

    queries = query_ref[0]
    grads = grad_ref[0]
    product = grads.astype(F32) * mixed_ref[0].astype(F32)
    head_of = lax.broadcasted_iota(jnp.int32, (HEADS, D), 1) // HEAD_DIM
    chosen = jnp.where(head_of == lax.broadcasted_iota(jnp.int32, (HEADS, D), 0), 1.0, 0.0).astype(BF16)
    high = product.astype(BF16)
    low = (product - high.astype(F32)).astype(BF16)
    inner = dot(chosen, high, NT) + dot(chosen, low, NT)
    inner_ref[0] = inner

    def per_head(values):
        return values.reshape(HEADS, PREFIX_PAD, toks)

    scores = per_head(dot(spread_ref[0], queries, NT))
    grad_weights = per_head(dot(spread_ref[1], grads, NT))
    weights = jnp.exp(scores - total_ref[0][:, None, :])
    valid = lax.broadcasted_iota(jnp.int32, weights.shape, 1) < PREFIX
    weights = jnp.where(valid, weights, 0.0)
    grad_scores = weights * (grad_weights - inner[:, None, :])
    weights = weights.reshape(HEADS * PREFIX_PAD, toks).astype(BF16)
    grad_scores = grad_scores.reshape(HEADS * PREFIX_PAD, toks).astype(BF16)
    start_ref[0] = dot(grad_scores.T, spread_ref[0])
    own = (
        lax.broadcasted_iota(jnp.int32, (HEADS * PREFIX_PAD, D), 0) // PREFIX_PAD
        == lax.broadcasted_iota(jnp.int32, (HEADS * PREFIX_PAD, D), 1) // HEAD_DIM
    )

    def gather(values):
        return jnp.sum(jnp.where(own, values, 0.0).reshape(HEADS, PREFIX_PAD, D), axis=0)

    prefix_grad_ref[0] += gather(dot(grad_scores, queries))
    prefix_grad_ref[1] += gather(dot(weights, grads))


def prefix_back(after, queries, grads, mixed, total, prefix_keyval, first_row):
    row_count, toks, _ = grads.shape
    row_block = pl.BlockSpec((1, toks, D), lambda row: (row, 0, 0))
    head_block = pl.BlockSpec((1, HEADS, toks), lambda row: (row, 0, 0))
    return kernel_call(
        prefix_back_kernel,
        after,
        (queries, grads, mixed, total, prefix_keyval),
        grid=(row_count,),
        in_specs=[
            pl.BlockSpec((1, toks, D), lambda row: (row + first_row, 0, 0)),
            row_block,
            row_block,
            head_block,
            pl.BlockSpec((2, PREFIX_PAD, D), lambda row: (0, 0, 0)),
        ],
        out_specs=[
            head_block,
            row_block,
            pl.BlockSpec((2, PREFIX_PAD, D), lambda row: (0, 0, 0)),
        ],
        out_shape=[
            jax.ShapeDtypeStruct((row_count, HEADS, toks), F32),
            jax.ShapeDtypeStruct((row_count, toks, D), F32),
            jax.ShapeDtypeStruct((2, PREFIX_PAD, D), F32),
        ],
        scratch_shapes=[pltpu.VMEM((2, HEADS * PREFIX_PAD, D), BF16)],
        cost_estimate=cost(row_count * 12 * toks * D * 256, row_count * toks * D * 10, row_count * toks * 256),
        name="prefix_back",
    )


def attend_back_kernel(places, blocks, first_row, pair_step, final, place_ref, length_ref, query_ref, grad_ref, total_ref, inner_ref, start_ref, *rest):
    count = len(blocks)
    keyval_refs = dict(zip(blocks, rest[:count]))
    grad_query_ref = rest[count]
    out_refs = dict(zip(blocks, rest[count + 1 : 2 * count + 1]))
    hide_ref = rest[2 * count + 1]
    place = place_ref[0]
    level = place // 2
    length = length_ref[first_row + pl.program_id(0)]
    limit = places.limits(place, length)
    masked_blocks = [block for block in blocks if places.masked(block)]

    if masked_blocks:

        @pl.when(pl.program_id(1) == 0)
        def _():
            for at, block in enumerate(masked_blocks):
                hide_ref[at] = jnp.where(places.visible(block, place, limit), 0.0, -jnp.inf)

    def back(active):
        def products_of(at):
            pair, head = at // 2, at % 2
            cols = slice(pair * 128, (pair + 1) * 128)
            queries = head_lanes(query_ref[0, :, cols], head)
            grads = head_lanes(grad_ref[0, :, cols], head)
            scores = {}
            grad_weights = {}
            for block in active:
                part = dot(keyval_refs[block][0, 0, :, cols], queries, NT)
                if block in masked_blocks:
                    part = part + hide_ref[masked_blocks.index(block)]
                scores[block] = part
                grad_weights[block] = dot(keyval_refs[block][0, 1, :, cols], grads, NT)
            return queries, grads, scores, grad_weights

        ahead = products_of(0)
        for at in range(2 * pair_step):
            pair, head = at // 2, at % 2
            cols = slice(pair * 128, (pair + 1) * 128)
            queries, grads, scores, grad_weights = ahead
            if at + 1 < 2 * pair_step:
                ahead = products_of(at + 1)
            if head == 0:
                keys_t = {block: keyval_refs[block][0, 0, :, cols].T for block in active}
                grad_keys = {}
                grad_values = {}
                outs = []
            total = total_ref[0, at : at + 1, :]
            inner = inner_ref[0, at : at + 1, :]
            rows = slice(head * HEAD_DIM, (head + 1) * HEAD_DIM)
            grad_query = None
            for block in active:
                weights = jnp.exp(scores[block] - total)
                grad_scores = (weights * (grad_weights[block] - inner)).astype(BF16)
                part_values = dot(weights.astype(BF16), grads)
                part_keys = dot(grad_scores, queries)
                part_query = dot(keys_t[block][rows], grad_scores)
                if head == 0:
                    grad_values[block], grad_keys[block] = part_values, part_keys
                else:
                    out_refs[block][0, 0, :, cols] = (grad_keys[block] + part_keys).astype(BF16)
                    out_refs[block][0, 1, :, cols] = (grad_values[block] + part_values).astype(BF16)
                grad_query = part_query if grad_query is None else grad_query + part_query
            outs.append(grad_query)
            if head == 1:
                grad_query = jnp.concatenate(outs, axis=0).T + start_ref[0, :, cols]
                if final:
                    grad_query = (grad_query * 0.125).astype(BF16)
                grad_query_ref[0, :, cols] = grad_query

    if max(blocks) < 2:
        back(blocks)
        return
    for levels in range(places.level_count):
        active = [block for block in blocks if block < 2 * (levels + 1)]

        @pl.when(level == levels)
        def _():
            if active:
                back(active)
            else:
                grad_query_ref[...] = start_ref[...]


def attend_back(after, place, lengths, queries, grads, total, inner, start, keyvals, level_count, first_row, final, pair_step=4):
    row_count, toks, _ = grads.shape
    blocks = sorted(keyvals)
    places = Places(toks, level_count)
    width = 128 * pair_step
    row_block = block_spec((1, toks, width), 0)
    head_block = pl.BlockSpec((1, 2 * pair_step, toks), lambda row, pair, *_: (row, pair, 0))
    masked = max(1, sum(places.masked(block) for block in blocks))
    return kernel_call(
        functools.partial(attend_back_kernel, places, blocks, first_row, pair_step, final),
        after,
        (place, lengths, queries, grads, total, inner, start, *[keyvals[block][0] for block in blocks]),
        prefetched=2,
        grid=(row_count, PAIRS // pair_step),
        in_specs=[block_spec((1, toks, width), first_row), row_block, head_block, head_block, row_block]
        + [block_spec((1, 2, toks, width), keyvals[block][1]) for block in blocks],
        out_specs=[row_block] + [block_spec((1, 2, toks, width), 0)] * len(blocks),
        scratch_shapes=[pltpu.VMEM((masked, toks, toks), F32)],
        out_shape=[jax.ShapeDtypeStruct((row_count, toks, D), BF16 if final else F32)]
        + [jax.ShapeDtypeStruct((row_count, 2, toks, D), BF16)] * len(blocks),
        cost_estimate=cost(
            row_count * HEADS * 10 * toks * toks * len(blocks) * 256,
            row_count * toks * D * 2 * (5 + 4 * len(blocks)),
            row_count * HEADS * toks * toks * len(blocks),
        ),
        name="attend_back",
    )


GELU_SCALE = 0.7978845608028654
GELU_CUBE = 0.044715


def feed_forward_kernel(first_row, chunk, place_ref, length_ref, source_ref, tokens_ref, cotangent_ref, mixed_ref, output_bias_ref, gain_ref, shift_ref, expand_bias_ref, contract_bias_ref, output_weight_hbm, expand_weight_hbm, contract_weight_hbm, *rest):
    activations_ref, grad_residual_ref, grad_heads_ref, output_weight_ref, expand_weight_ref, contract_weight_ref, residual_ref, normed_ref, grad_out_ref, active_ref, grad_expand_ref, result_ref, grad_normed_ref, semaphores = rest[-14:]
    rows, toks, _ = tokens_ref.shape
    count = rows * toks
    chunks = expand_weight_ref.shape[0]
    copies = Copies(semaphores)
    copies.start("output", output_weight_hbm, output_weight_ref)

    def weight_copies(at):
        span = pl.ds(pl.multiple_of(at * chunk, chunk), chunk)
        return (
            pltpu.make_async_copy(expand_weight_hbm.at[:, span], expand_weight_ref.at[at], semaphores.at[1 + at]),
            pltpu.make_async_copy(contract_weight_hbm.at[span, :], contract_weight_ref.at[at], semaphores.at[1 + chunks + at]),
        )

    def start_weights(at, carry):
        for copy in weight_copies(at):
            copy.start()
        return carry

    lax.fori_loop(0, chunks, start_weights, 0)

    spots = place_ref[0] * toks + lax.broadcasted_iota(jnp.int32, (toks, D), 0)
    for row in range(rows):
        target = (spots >= source_ref[first_row + row]) & (spots < length_ref[first_row + row])
        values = cotangent_ref[row].astype(F32)
        grad_out_ref[row * toks : (row + 1) * toks, :] = jnp.where(target, values, 0.0).astype(BF16)
    copies.wait("output")
    projected = dot(mixed_ref[...].reshape(count, D), output_weight_ref[...])
    residual = tokens_ref[...].reshape(count, D).astype(F32) + projected + output_bias_ref[...]
    residual_ref[...] = residual
    normed, _ = normalize(residual)
    normed_ref[...] = (normed * gain_ref[...] + shift_ref[...]).astype(BF16)

    def first(at, slot):
        for copy in weight_copies(at):
            copy.wait()
        bias = expand_bias_ref[:, pl.ds(pl.multiple_of(at * chunk, chunk), chunk)]
        values = dot(normed_ref[...], expand_weight_ref[at]) + bias
        grad_hidden = dot(grad_out_ref[...], contract_weight_ref[at], NT)
        square = values * values
        bend = jnp.tanh(values * (GELU_SCALE + GELU_SCALE * GELU_CUBE * square))
        half = 0.5 + 0.5 * bend
        slope = half + (0.5 * values) * (1.0 - bend * bend) * (
            GELU_SCALE + 3.0 * GELU_SCALE * GELU_CUBE * square
        )
        active_ref[slot] = (values * half).astype(BF16)
        grad_expand_ref[slot] = (grad_hidden * slope).astype(BF16)

    def second(at, slot):
        result_ref[...] += dot(active_ref[slot], contract_weight_ref[at])
        grad_normed_ref[...] += dot(grad_expand_ref[slot], expand_weight_ref[at], NT)

    result_ref[...] = jnp.zeros_like(result_ref)
    grad_normed_ref[...] = jnp.zeros_like(grad_normed_ref)
    first(0, 0)

    def body(at, carry):
        first(2 * at + 1, 1)
        second(2 * at, 0)
        first(2 * at + 2, 0)
        second(2 * at + 1, 1)
        return carry

    lax.fori_loop(0, chunks // 2 - 1, body, 0)
    first(chunks - 1, 1)
    second(chunks - 2, 0)
    second(chunks - 1, 1)

    residual = residual_ref[...]
    activations_ref[...] = (residual + result_ref[...] + contract_bias_ref[...]).astype(BF16).reshape(rows, toks, D)
    normed, scale = normalize(residual)
    grad = grad_out_ref[...].astype(F32) + norm_back(grad_normed_ref[...] * gain_ref[...], normed, scale)
    grad_residual_ref[...] = grad.reshape(rows, toks, D)
    heads = dot(grad.astype(BF16), output_weight_ref[...], NT)
    grad_heads_ref[...] = heads.astype(BF16).reshape(rows, toks, D)


def feed_forward(after, place, lengths, sources, tokens, cotangent, mixed, weights, first_row, earlier, chunk=512):
    row_count, toks, _ = mixed.shape
    count = row_count * toks
    output_weight, output_bias, gain, shift, expand_weight, expand_bias, contract_weight, contract_bias = weights
    hidden = expand_weight.shape[1]
    chunks = hidden // chunk
    given = [] if earlier is None else [earlier]
    at_row = first_row // row_count

    def whole(shape):
        return pl.BlockSpec(shape, lambda step, *_: (0,) * len(shape))

    some_rows = pl.BlockSpec((row_count, toks, D), lambda step, *_: (at_row, 0, 0))
    return kernel_call(
        functools.partial(feed_forward_kernel, first_row, chunk),
        after,
        (place, lengths, sources, tokens, cotangent, mixed, output_bias, gain, shift, expand_bias, contract_bias, output_weight, expand_weight, contract_weight, *given),
        prefetched=3,
        in_specs=[some_rows, some_rows, whole((row_count, toks, D))]
        + [whole((1, D))] * 3
        + [whole((1, hidden)), whole((1, D)), HBM, HBM, HBM]
        + [HBM] * len(given),
        out_specs=[some_rows, whole((row_count, toks, D)), whole((row_count, toks, D))],
        scratch_shapes=[
            pltpu.VMEM((D, D), BF16),
            pltpu.VMEM((chunks, D, chunk), BF16),
            pltpu.VMEM((chunks, chunk, D), BF16),
            pltpu.VMEM((count, D), F32),
            pltpu.VMEM((count, D), BF16),
            pltpu.VMEM((count, D), BF16),
            pltpu.VMEM((2, count, chunk), BF16),
            pltpu.VMEM((2, count, chunk), BF16),
            pltpu.VMEM((count, D), F32),
            pltpu.VMEM((count, D), F32),
            pltpu.SemaphoreType.DMA((2 * chunks + 1,)),
        ],
        out_shape=[
            jax.ShapeDtypeStruct(tokens.shape, BF16),
            jax.ShapeDtypeStruct((row_count, toks, D), F32),
            jax.ShapeDtypeStruct((row_count, toks, D), BF16),
        ],
        input_output_aliases={14: 0} if given else {},
        cost_estimate=cost(count * D * (8 * hidden + 4 * D), 4 * D * hidden + 2 * D * D + 16 * count * D, count * hidden),
        name="feed_forward",
    )


def up_back_kernel(own_hbm, received_hbm, weight_hbm, grad_ref, own_ref, received_ref, weight_ref, semaphores):
    rows, _, toks, _ = own_hbm.shape
    copies = Copies(semaphores)
    for half in range(2):
        copies.start(("own", half), own_hbm.at[:, half], own_ref.at[half])
        copies.start(("received", half), received_hbm.at[:, half], received_ref.at[half])
        copies.start(half, weight_hbm.at[:, pl.ds((half + 1) * D, D)], weight_ref.at[half])
    total = None
    for half in range(2):
        for name in (("own", half), ("received", half), half):
            copies.wait(name)
        values = (own_ref[half].astype(F32) + received_ref[half].astype(F32)).astype(BF16)
        part = dot(values.reshape(rows * toks, D), weight_ref[half], NT)
        total = part if total is None else total + part
    grad_ref[...] = total.astype(BF16).reshape(rows, toks, D)


def up_back(after, own, received, weight):
    rows, _, toks, _ = own.shape
    return kernel_call(
        up_back_kernel,
        after,
        (own, received, weight),
        in_specs=[ANY, ANY, HBM],
        out_specs=pl.BlockSpec(memory_space=pltpu.VMEM),
        out_shape=jax.ShapeDtypeStruct((rows, toks, D), BF16),
        scratch_shapes=[
            pltpu.VMEM((2, rows, toks, D), BF16),
            pltpu.VMEM((2, rows, toks, D), BF16),
            pltpu.VMEM((2, D, D), BF16),
            pltpu.SemaphoreType.DMA((6,)),
        ],
        cost_estimate=cost(4 * rows * toks * D * D, 4 * D * D + 10 * rows * toks * D),
        name="up_back",
    )


def project_back_kernel(rows, *refs):
    query_hbms, own_hbms, received_hbms = refs[:rows], refs[rows : 2 * rows], refs[2 * rows : 3 * rows]
    weight_hbm, total_ref, query_ref, own_ref, received_ref, weight_ref, semaphores = refs[3 * rows :]
    toks = total_ref.shape[1]
    copies = Copies(semaphores)
    for row in range(rows):
        copies.start(("query", row), query_hbms[row].at[0], query_ref.at[row])
    for at in range(3):
        copies.start(at, weight_hbm.at[:, pl.ds(at * D, D)], weight_ref.at[at])
        for row in range(rows if at else 0):
            copies.start(("own", at, row), own_hbms[row].at[0, at - 1], own_ref.at[at - 1, row])
            copies.start(("received", at, row), received_hbms[row].at[0, at - 1], received_ref.at[at - 1, row])
    for row in range(rows):
        copies.wait(("query", row))
    copies.wait(0)
    total = dot(query_ref[...].reshape(rows * toks, D), weight_ref[0], NT)
    for at in (1, 2):
        for row in range(rows):
            copies.wait(("own", at, row))
            copies.wait(("received", at, row))
        copies.wait(at)
        values = (own_ref[at - 1].astype(F32) + received_ref[at - 1].astype(F32)).astype(BF16)
        total = total + dot(values.reshape(rows * toks, D), weight_ref[at], NT)
    total_ref[...] = total.reshape(rows, toks, D)


def project_back(after, grad_queries, own, received, weight):
    rows = len(grad_queries)
    toks = grad_queries[0].shape[1]
    return kernel_call(
        functools.partial(project_back_kernel, rows),
        after,
        (*grad_queries, *own, *received, weight),
        in_specs=[ANY] * (3 * rows) + [HBM],
        out_specs=pl.BlockSpec(memory_space=pltpu.VMEM),
        out_shape=jax.ShapeDtypeStruct((rows, toks, D), F32),
        scratch_shapes=[
            pltpu.VMEM((rows, toks, D), BF16),
            pltpu.VMEM((2, rows, toks, D), BF16),
            pltpu.VMEM((2, rows, toks, D), BF16),
            pltpu.VMEM((3, D, D), BF16),
            pltpu.SemaphoreType.DMA((3 + 5 * rows,)),
        ],
        cost_estimate=cost(6 * rows * toks * D * D, 6 * D * D + 14 * rows * toks * D),
        name="project_back",
    )


def finish_kernel(above_count, tokens_ref, gain_ref, residual_ref, total_ref, *rest):
    grad_ref = rest[-1]
    total = total_ref[0]
    for above_ref in rest[:above_count]:
        total = total + above_ref[0].astype(F32)
    normed, scale = normalize(tokens_ref[0].astype(F32))
    grad_ref[0] = residual_ref[0] + norm_back(total * gain_ref[...], normed, scale)


def finish(after, tokens, gain, grad_residual, total, above, row, earlier):
    toks = tokens.shape[1]
    tile = min(128, toks)
    given = [] if earlier is None else [earlier]
    at_row = pl.BlockSpec((1, tile, D), lambda at: (row, at, 0))
    own_row = pl.BlockSpec((1, tile, D), lambda at: (0, at, 0))
    return kernel_call(
        functools.partial(finish_kernel, len(above)),
        after,
        (tokens, gain, grad_residual, total, *above, *given),
        grid=(toks // tile,),
        in_specs=[at_row, pl.BlockSpec((1, D), lambda at: (0, 0)), own_row, at_row]
        + [own_row] * len(above)
        + [HBM] * len(given),
        out_specs=at_row,
        out_shape=jax.ShapeDtypeStruct(tokens.shape, F32),
        input_output_aliases={4 + len(above): 0} if given else {},
        cost_estimate=cost(20 * toks * D, toks * D * 16),
        name="finish",
    )


def prefix_kernel(table_ref, lift_ref, lift_bias_ref, fan_ref, fan_bias_ref, lifted_ref, keyval_ref):
    lifted = jnp.tanh(dot(table_ref[...], lift_ref[...]) + lift_bias_ref[...])
    lifted_ref[...] = jnp.zeros_like(lifted_ref)
    lifted_ref[:PREFIX, :] = lifted
    keyval_ref[...] = jnp.zeros_like(keyval_ref)
    keyval = (dot(lifted.astype(BF16), fan_ref[...]) + fan_bias_ref[...]).astype(BF16)
    keyval_ref[0, :PREFIX, :] = keyval[:, :D]
    keyval_ref[1, :PREFIX, :] = keyval[:, D:]


def prefix_forward(after, table, lift, lift_bias, fan, fan_bias):
    vmem = pl.BlockSpec(memory_space=pltpu.VMEM)
    return kernel_call(
        prefix_kernel,
        after,
        (table, lift, lift_bias, fan, fan_bias),
        in_specs=[vmem] * 5,
        out_specs=[vmem] * 2,
        out_shape=[
            jax.ShapeDtypeStruct((PREFIX_PAD, lift.shape[1]), F32),
            jax.ShapeDtypeStruct((2, PREFIX_PAD, D), BF16),
        ],
        cost_estimate=cost(10**9, 10**6),
        name="prefix_forward",
    )


def split(values):
    high = values.astype(BF16)
    return high, (values - high.astype(F32)).astype(BF16)


def prefix_network_back_kernel(grad_ref, table_ref, lift_ref, fan_ref, lifted_ref, grad_table_ref, grad_lift_ref, grad_lift_bias_ref, grad_fan_ref, grad_fan_bias_ref):
    lifted = lifted_ref[...]
    lifted_t = jnp.concatenate([lifted.astype(BF16)] * 2, axis=0).T
    grad_lifted = None
    for half in range(2):
        cols = slice(half * D, (half + 1) * D)
        grad = grad_ref[half]
        grad_fan_bias_ref[:, cols] = jnp.sum(grad, axis=0, keepdims=True)
        both = jnp.concatenate(split(grad), axis=0)
        grad_fan_ref[:, cols] = dot(lifted_t, both)
        part = dot(both, fan_ref[:, cols], NT)
        grad_lifted = part if grad_lifted is None else grad_lifted + part
    grad_lifted = (grad_lifted[:PREFIX_PAD] + grad_lifted[PREFIX_PAD:]) * (1.0 - lifted * lifted)
    grad_lift_bias_ref[...] = jnp.sum(grad_lifted, axis=0, keepdims=True)
    both = jnp.concatenate(split(grad_lifted), axis=0)
    table = jnp.concatenate([table_ref[...].astype(F32), jnp.zeros((PREFIX_PAD - PREFIX, D), F32)], axis=0)
    table_t = jnp.concatenate([table.astype(BF16)] * 2, axis=0).T
    grad_lift_ref[...] = dot(table_t, both)
    grad_table = dot(both, lift_ref[...], NT)
    grad_table_ref[...] = (grad_table[:PREFIX_PAD] + grad_table[PREFIX_PAD:])[:PREFIX]


def prefix_network_back(after, grad, table, lift, fan, lifted):
    hidden = lift.shape[1]
    vmem = pl.BlockSpec(memory_space=pltpu.VMEM)
    return kernel_call(
        prefix_network_back_kernel,
        after,
        (grad, table, lift, fan, lifted),
        in_specs=[vmem] * 5,
        out_specs=[vmem] * 5,
        out_shape=[
            jax.ShapeDtypeStruct((PREFIX, D), F32),
            jax.ShapeDtypeStruct((D, hidden), F32),
            jax.ShapeDtypeStruct((1, hidden), F32),
            jax.ShapeDtypeStruct((hidden, 2 * D), F32),
            jax.ShapeDtypeStruct((1, 2 * D), F32),
        ],
        cost_estimate=cost(10**9, 10**6),
        name="prefix_network_back",
    )


def add_kernel(left_ref, right_ref, sum_ref):
    sum_ref[...] = left_ref[...] + right_ref[...]


def add(after, left, right):
    vmem = pl.BlockSpec(memory_space=pltpu.VMEM)
    return kernel_call(
        add_kernel,
        after,
        (left, right),
        in_specs=[vmem] * 2,
        out_specs=vmem,
        out_shape=jax.ShapeDtypeStruct(left.shape, left.dtype),
        cost_estimate=cost(10**8, 10**5),
        name="add",
    )


class Order:
    def __init__(self):
        self.before = ()

    def call(self, kernel, *operands):
        outs = kernel(self.before, *operands)
        self.before = (outs[-1] if isinstance(outs, (list, tuple)) else outs,)
        return outs


def sum_hops(axes):
    hops = []
    for axis in axes:
        size = lax.axis_size(axis)
        if size & (size - 1):
            return None
        hop = 1
        while hop < size:
            hops.append((axis, [(at, at ^ hop) for at in range(size)]))
            hop *= 2
    return hops


def per_device(tokens, cotangent, row_lengths, source_lengths, first_gain, first_shift, attend_weight, attend_bias, output_weight, output_bias, second_gain, second_shift, expand_weight, expand_bias, contract_weight, contract_bias, prefix_table, lift_weight, lift_bias, fan_weight, fan_bias):
    rows = tokens.shape[0]
    seq = lax.axis_size("seq")
    level_count = seq // 2
    levels = range(1, level_count)
    mates = [(at, at ^ 1) for at in range(seq)]
    place = lax.axis_index("seq").astype(jnp.int32).reshape(1)
    first_gain, first_shift, attend_bias, output_bias, second_gain, second_shift, expand_bias, contract_bias, lift_bias, fan_bias = [
        vector.reshape(1, -1)
        for vector in (first_gain, first_shift, attend_bias, output_bias, second_gain, second_shift, expand_bias, contract_bias, lift_bias, fan_bias)
    ]
    weights = (output_weight, output_bias, second_gain, second_shift, expand_weight, expand_bias, contract_weight, contract_bias)
    lower_tokens = [
        [lax.ppermute(tokens[row : row + 1], "seq", [(at, at + 2 * level) for at in range(seq - 2 * level)]) for level in levels]
        for row in range(rows)
    ]
    order = Order()
    hops = sum_hops(("seq", "dp"))
    activations = None
    input_grad = None
    prefix_grad = None
    arriving = None

    def swap(array):
        return lax.ppermute(array, "seq", mates)

    def hop():
        nonlocal prefix_grad, arriving
        if arriving is not None:
            prefix_grad = order.call(add, prefix_grad, arriving)
            arriving = None
        if hops:
            axis, pairs = hops.pop(0)
            arriving = lax.ppermute(prefix_grad, axis, pairs)

    def lower(row):
        blocks = []
        for level in levels:
            (block,) = order.call(project, lower_tokens[row][level - 1], first_gain, first_shift, attend_weight, attend_bias, False)
            blocks += [block, swap(block)]
        return blocks

    def attend_to_near(row):
        return order.call(attend_near, place, row_lengths, queries, keyval, mate_keyval, prefix_keyval, level_count, row, 1)

    def attend_to_far(row, near, blocks):
        return order.call(attend_far, place, row_lengths, queries, *near, blocks, level_count, row)

    def feed(row, mixed):
        nonlocal activations
        activations, grad_residual, grad_heads = order.call(
            feed_forward, place, row_lengths, source_lengths, tokens, cotangent, mixed, weights, row, activations
        )
        return grad_residual, grad_heads

    queries, keyval = order.call(project, tokens, first_gain, first_shift, attend_weight, attend_bias, True)
    mate_keyval = swap(keyval)
    lifted, prefix_keyval = order.call(prefix_forward, prefix_table, lift_weight, lift_bias, fan_weight, fan_bias)
    nears = [attend_to_near(0)]
    lowers = [lower(0)]
    mixed, total, grad_residual, grad_heads = [], [], [], []
    for row in range(rows):
        if row + 1 < rows:
            nears.append(attend_to_near(row + 1))
        row_mixed, row_total = attend_to_far(row, nears[row], lowers[row])
        if row + 1 < rows:
            lowers.append(lower(row + 1))
        row_residual, row_heads = feed(row, row_mixed)
        for values, value in zip((mixed, total, grad_residual, grad_heads), (row_mixed, row_total, row_residual, row_heads)):
            values.append(value)

    inners, starts = [], []
    for row in range(rows):
        inner, start, part = order.call(prefix_back, queries, grad_heads[row], mixed[row], total[row], prefix_keyval, row)
        prefix_grad = part if prefix_grad is None else order.call(add, prefix_grad, part)
        inners.append(inner)
        starts.append(start)
    if hops is None:
        prefix_grad = lax.psum(prefix_grad, ("seq", "dp"))

    own, received, grad_queries, aboves = [], [], [], []
    for row in range(rows):
        pairs = {0: (keyval, row), 1: (mate_keyval, row)}
        pairs.update({2 + at: (block, 0) for at, block in enumerate(lowers[row])})

        def back(names, final, start):
            return order.call(
                attend_back, place, row_lengths, queries, grad_heads[row], total[row], inners[row], start,
                {name: pairs[name] for name in names}, level_count, row, final,
            )

        hop()
        start = starts[row]
        above = []
        if level_count > 1:
            start, *mate_grads = back([2 * level + 1 for level in levels], False, start)
            hop()
            from_mates = [swap(grad) for grad in mate_grads]
            start, *up_grads = back([2 * level for level in levels], False, start)
            hop()
            for level in levels:
                part = order.call(up_back, up_grads[level - 1], from_mates[level - 1], attend_weight)
                above.append(lax.ppermute(part, "seq", [(at + 2 * level, at) for at in range(seq - 2 * level)]))
        row_queries, row_own, row_mate = back([0, 1], True, start)
        hop()
        received.append(swap(row_mate))
        own.append(row_own)
        grad_queries.append(row_queries)
        aboves.append(above)
    while hops or arriving is not None:
        hop()
    grad_table, grad_lift, grad_lift_bias, grad_fan, grad_fan_bias = order.call(
        prefix_network_back, prefix_grad, prefix_table, lift_weight, fan_weight, lifted
    )
    totals = order.call(project_back, grad_queries, own, received, attend_weight)
    for row in range(rows):
        input_grad = order.call(finish, tokens, first_gain, grad_residual[row], totals, aboves[row], row, input_grad)
    return (activations, input_grad, grad_table, grad_lift, grad_lift_bias.reshape(-1), grad_fan, grad_fan_bias.reshape(-1))


def solution(mesh):
    batch = P("dp", "seq", None)
    return jax.shard_map(
        per_device,
        mesh=mesh,
        in_specs=(batch, batch, P("dp"), P("dp")) + (P(),) * 17,
        out_specs=(batch, batch, P(), P(), P(), P(), P()),
        check_vma=False,
    )
```

```python
import functools

import jax
import jax.numpy as jnp
from jax import lax
from jax.experimental import pallas as pl
from jax.experimental.pallas import tpu as pltpu
from jax.sharding import PartitionSpec as P

D = 1024
HEADS = 16
HEAD_DIM = 64
PAIRS = HEADS // 2
PREFIX = 10
PREFIX_PAD = 16
LEAST_LENGTH = 512
NN = (((1,), (0,)), ((), ()))
NT = (((1,), (1,)), ((), ()))
MIB = 1 << 20
BF16 = jnp.bfloat16
F32 = jnp.float32


def dot(left, right, dims=NN):
    return lax.dot_general(left, right, dims, preferred_element_type=F32)


ANY = pl.BlockSpec(memory_space=pl.ANY)


VMEM = pl.BlockSpec(memory_space=pltpu.VMEM)
COVER = pl.CostEstimate(flops=10**12, bytes_accessed=10**9, transcendentals=0)
TOKEN = jax.ShapeDtypeStruct((8, 128), F32)


def kernel_call(kernel, after, operands, limit, in_specs, out_specs, out_shape, prefetched=0, scratch_shapes=(), **rest):
    lead = prefetched + len(in_specs)

    def body(*refs):
        outs = lead + len(after)
        token_ref = refs[outs + len(out_shape)]
        token_ref[...] = jnp.zeros_like(token_ref)
        kernel(*refs[:lead], *refs[outs : outs + len(out_shape)], *refs[outs + len(out_shape) + 1 :])

    spec = pltpu.PrefetchScalarGridSpec(
        num_scalar_prefetch=prefetched,
        grid=(1,),
        in_specs=[*in_specs] + [ANY] * len(after),
        out_specs=[*out_specs, VMEM],
        scratch_shapes=scratch_shapes,
    )
    return pl.pallas_call(
        body,
        grid_spec=spec,
        out_shape=[*(jax.ShapeDtypeStruct(out.shape, out.dtype) for out in out_shape), TOKEN],
        compiler_params=pltpu.CompilerParams(dimension_semantics=("arbitrary",), vmem_limit_bytes=limit * MIB),
        cost_estimate=COVER,
        **rest,
    )(*operands, *after)


def split(values):
    high = values.astype(BF16)
    return high, (values - high.astype(F32)).astype(BF16)


class Copies:
    def __init__(self, semaphores):
        self.semaphores = semaphores
        self.count = 0
        self.copies = {}

    def start(self, name, source, target):
        copy = pltpu.make_async_copy(source, target, self.semaphores.at[self.count])
        copy.start()
        self.count += 1
        self.copies[name] = copy

    def wait(self, name):
        self.copies[name].wait()


HBM = pl.BlockSpec(memory_space=pltpu.HBM)


def normalize(values):
    centred = values - jnp.mean(values, axis=-1, keepdims=True)
    scale = lax.rsqrt(jnp.mean(centred * centred, axis=-1, keepdims=True) + 1e-05)
    return centred * scale, scale


def norm_back(grad, normed, scale):
    return scale * (
        grad
        - jnp.mean(grad, axis=-1, keepdims=True)
        - normed * jnp.mean(grad * normed, axis=-1, keepdims=True)
    )


def project_own_kernel(tokens_hbm, gain_ref, shift_ref, bias_ref, weight_hbm, query_ref, keyval_ref, *rest):
    later_refs = rest[:-4]
    tokens_ref, weight_ref, normed_ref, semaphores = rest[-4:]
    rows, toks, _ = tokens_hbm.shape
    count = rows * toks
    chunks, _, chunk = weight_ref.shape
    tiles = D // chunk
    copies = Copies(semaphores)
    copies.start("tokens", tokens_hbm, tokens_ref)
    for at in range(chunks):
        copies.start(at, weight_hbm.at[:, pl.ds(at * chunk, chunk)], weight_ref.at[at])
    copies.wait("tokens")
    for at, later_ref in enumerate(later_refs):
        later_ref[0] = tokens_ref[at + 1]
    normed, _ = normalize(tokens_ref[...].reshape(count, D).astype(F32))
    normed_ref[...] = (normed * gain_ref[...] + shift_ref[...]).astype(BF16)
    for at in range(chunks):
        copies.wait(at)
        result = (dot(normed_ref[...], weight_ref[at]) + bias_ref[:, at * chunk : (at + 1) * chunk]).astype(BF16)
        cols = slice(at % tiles * chunk, (at % tiles + 1) * chunk)
        if at < tiles:
            query_ref[:, :, cols] = (result * 0.125).reshape(rows, toks, chunk)
        else:
            keyval_ref[:, at // tiles - 1, :, cols] = result.reshape(rows, toks, chunk)


def project_own(after, tokens, gain, shift, weight, bias, chunk=512):
    rows, toks, _ = tokens.shape
    chunks = 3 * D // chunk
    return kernel_call(
        project_own_kernel,
        after,
        (tokens, gain, shift, bias, weight),
        58,
        [ANY, VMEM, VMEM, VMEM, HBM],
        [VMEM] * (1 + rows),
        [jax.ShapeDtypeStruct((rows, toks, D), BF16), jax.ShapeDtypeStruct((rows, 2, toks, D), BF16)]
        + [jax.ShapeDtypeStruct((1, toks, D), BF16)] * (rows - 1),
        scratch_shapes=[
            pltpu.VMEM((rows, toks, D), BF16),
            pltpu.VMEM((chunks, D, chunk), BF16),
            pltpu.VMEM((rows * toks, D), BF16),
            pltpu.SemaphoreType.DMA((chunks + 1,)),
        ],
        name="project_own",
    )


def project_up_kernel(tokens_ref, gain_ref, shift_ref, bias_ref, weight_ref, keyval_ref):
    toks = tokens_ref.shape[1]
    normed, _ = normalize(tokens_ref[0].astype(F32))
    normed = (normed * gain_ref[...] + shift_ref[...]).astype(BF16)
    for half in range(2):
        cols = slice((half + 1) * D, (half + 2) * D)
        keyval_ref[0, half] = (dot(normed, weight_ref[:, cols]) + bias_ref[:, cols]).astype(BF16)


def project_up(after, tokens, gain, shift, weight, bias):
    toks = tokens.shape[1]
    return kernel_call(
        project_up_kernel,
        after,
        (tokens, gain, shift, bias, weight),
        10,
        [VMEM] * 5,
        [VMEM],
        [jax.ShapeDtypeStruct((1, 2, toks, D), BF16)],
        name="project_up",
    )


def head_lanes(values, head):
    lanes = lax.broadcasted_iota(jnp.int32, values.shape, 1)
    keep = lanes < HEAD_DIM if head == 0 else lanes >= HEAD_DIM
    return jnp.where(keep, values, jnp.zeros_like(values))


def prefix_mask(values, fill):
    places = lax.broadcasted_iota(jnp.int32, values.shape, 0)
    return jnp.where(places < PREFIX, values, fill)


class Places:
    def __init__(self, toks, level_count):
        self.toks = toks
        self.level_count = level_count

    def masked(self, block):
        if block < 2:
            return True
        level = block // 2
        return (self.level_count - level) * 2 * self.toks > LEAST_LENGTH

    def limits(self, place, length):
        base = place * self.toks
        queries = base + lax.broadcasted_iota(jnp.int32, (1, self.toks), 1)
        return jnp.minimum(queries, length - 1)

    def visible(self, block, place, limit):
        if block == 0:
            base = place * self.toks
        else:
            base = (lax.bitwise_xor(place, block % 2) - (block // 2) * 2) * self.toks
        keys = lax.broadcasted_iota(jnp.int32, (self.toks, self.toks), 0)
        return keys <= limit - base


def spread_prefix(prefix):
    tiled = jnp.concatenate([prefix] * HEADS, axis=0)
    rows = lax.broadcasted_iota(jnp.int32, tiled.shape, 0) // PREFIX_PAD
    cols = lax.broadcasted_iota(jnp.int32, tiled.shape, 1) // HEAD_DIM
    return jnp.where(rows == cols, tiled, jnp.zeros_like(tiled))


GELU_SCALE = 0.7978845608028654
GELU_CUBE = 0.044715
FAR = 1e30
ROW_LIMIT = 47


class RowRefs:
    def __init__(self, names, refs):
        for name, ref in zip(names, refs):
            setattr(self, name, ref)


def column_group(group, width):
    return pl.ds(pl.multiple_of(group * width, width), width)


def attend_rows(places, refs, place, limit, pair_step):
    blocks = range(2 * places.level_count)
    masked_blocks = [block for block in blocks if places.masked(block)]
    level = place // 2
    width = 128 * pair_step
    refs.prefix_scores[...] = dot(refs.spread[0], refs.query[...], NT)
    for at, block in enumerate(masked_blocks):
        refs.hide[at] = jnp.where(places.visible(block, place, limit), 0.0, -jnp.inf)

    def beyond(block):
        return jnp.where(level >= block // 2, 0.0, FAR) if block > 1 else None

    def body(group, carry):
        span = column_group(group, width)
        group_queries = refs.query[:, span]
        group_keys = [refs.keyval(block, 0, span) for block in blocks]

        def scores_of(at):
            pair, head = at // 2, at % 2
            cols = slice(pair * 128, (pair + 1) * 128)
            queries = head_lanes(group_queries[:, cols], head)
            spot = pl.multiple_of((group * pair_step * 2 + at) * PREFIX_PAD, PREFIX_PAD)
            prefix_scores = prefix_mask(refs.prefix_scores[pl.ds(spot, PREFIX_PAD), :], -jnp.inf)
            highest = jnp.max(prefix_scores, axis=0, keepdims=True)
            scores = []
            for block in blocks:
                part = dot(group_keys[block][:, cols], queries, NT)
                if block in masked_blocks:
                    part = part + refs.hide[masked_blocks.index(block)]
                top = jnp.max(part, axis=0, keepdims=True)
                if block > 1:
                    top = top - beyond(block)
                highest = jnp.maximum(highest, top)
                scores.append(part)
            return prefix_scores, scores, highest

        ahead = scores_of(0)
        for at in range(2 * pair_step):
            pair, head = at // 2, at % 2
            cols = slice(pair * 128, (pair + 1) * 128)
            prefix_scores, scores, highest = ahead
            if at + 1 < 2 * pair_step:
                ahead = scores_of(at + 1)
            if head == 0:
                values_t = [refs.keyval(block, 1, span)[:, cols].T for block in blocks]
                prefix_values_t = refs.prefix[1, :, span][:, cols].T
                outs = []
            rows = slice(head * HEAD_DIM, (head + 1) * HEAD_DIM)
            prefix_weights = jnp.exp(prefix_scores - highest)
            total = jnp.sum(prefix_weights, axis=0, keepdims=True)
            mixed = dot(prefix_values_t[rows], prefix_weights.astype(BF16))
            for block in blocks:
                base = highest + beyond(block) if block > 1 else highest
                weights = jnp.exp(scores[block] - base)
                total = total + jnp.sum(weights, axis=0, keepdims=True)
                mixed = mixed + dot(values_t[block][rows], weights.astype(BF16))
            outs.append(mixed * (1.0 / total))
            refs.total[group, at : at + 1, :] = highest + jnp.log(total)
            if head == 1:
                refs.mixed[:, pl.ds(pl.multiple_of(group * width + pair * 128, 128), 128)] = jnp.concatenate(outs, axis=0).T.astype(BF16)
        return carry

    lax.fori_loop(0, PAIRS // pair_step, body, 0)


def feed_rows(refs, place, length, source, weight_copies, chunks, chunk):
    toks = refs.tokens.shape[0]
    spots = place * toks + lax.broadcasted_iota(jnp.int32, (toks, D), 0)
    target = (spots >= source) & (spots < length)
    refs.grad_out[...] = jnp.where(target, refs.cotangent[...].astype(F32), 0.0).astype(BF16)
    residual = refs.tokens[...].astype(F32) + dot(refs.mixed[...], refs.output_weight[...]) + refs.output_bias[...]
    refs.residual[...] = residual
    normed, _ = normalize(residual)
    refs.normed[...] = (normed * refs.second_gain[...] + refs.second_shift[...]).astype(BF16)

    def first(at, slot):
        for copy in weight_copies(at):
            copy.wait()
        bias = refs.expand_bias[:, pl.ds(pl.multiple_of(at * chunk, chunk), chunk)]
        values = dot(refs.normed[...], refs.expand_weight[at]) + bias
        grad_hidden = dot(refs.grad_out[...], refs.contract_weight[at], NT)
        square = values * values
        bend = jnp.tanh(values * (GELU_SCALE + GELU_SCALE * GELU_CUBE * square))
        half = 0.5 + 0.5 * bend
        slope = half + (0.5 * values) * (1.0 - bend * bend) * (
            GELU_SCALE + 3.0 * GELU_SCALE * GELU_CUBE * square
        )
        refs.active[slot] = (values * half).astype(BF16)
        refs.grad_expand[slot] = (grad_hidden * slope).astype(BF16)

    def second(at, slot):
        refs.result[...] += dot(refs.active[slot], refs.contract_weight[at])
        refs.grad_normed[...] += dot(refs.grad_expand[slot], refs.expand_weight[at], NT)

    refs.result[...] = jnp.zeros_like(refs.result)
    refs.grad_normed[...] = jnp.zeros_like(refs.grad_normed)
    first(0, 0)

    def body(at, carry):
        first(2 * at + 1, 1)
        second(2 * at, 0)
        first(2 * at + 2, 0)
        second(2 * at + 1, 1)
        return carry

    lax.fori_loop(0, chunks // 2 - 1, body, 0)
    first(chunks - 1, 1)
    second(chunks - 2, 0)
    second(chunks - 1, 1)

    residual = refs.residual[...]
    refs.activations[...] = (residual + refs.result[...] + refs.contract_bias[...]).astype(BF16)
    normed, scale = normalize(residual)
    grad = refs.grad_out[...].astype(F32) + norm_back(refs.grad_normed[...] * refs.second_gain[...], normed, scale)
    refs.grad_residual[0] = grad
    refs.grad_heads[...] = dot(grad.astype(BF16), refs.output_weight[...], NT).astype(BF16)


def prefix_back_rows(refs):
    toks = refs.query.shape[0]
    queries = refs.query[...]
    grads = refs.grad_heads[...]
    product = grads.astype(F32) * refs.mixed[...].astype(F32)
    head_of = lax.broadcasted_iota(jnp.int32, (HEADS, D), 1) // HEAD_DIM
    chosen = jnp.where(head_of == lax.broadcasted_iota(jnp.int32, (HEADS, D), 0), 1.0, 0.0).astype(BF16)
    high, low = split(product)
    inner = dot(chosen, high, NT) + dot(chosen, low, NT)
    refs.inner[...] = inner.reshape(refs.inner.shape)

    def per_head(values):
        return values.reshape(HEADS, PREFIX_PAD, toks)

    scores = per_head(refs.prefix_scores[...])
    grad_weights = per_head(dot(refs.spread[1], grads, NT))
    weights = jnp.exp(scores - refs.total[...].reshape(HEADS, 1, toks))
    valid = lax.broadcasted_iota(jnp.int32, weights.shape, 1) < PREFIX
    weights = jnp.where(valid, weights, 0.0)
    grad_scores = weights * (grad_weights - inner[:, None, :])
    weights = weights.reshape(HEADS * PREFIX_PAD, toks).astype(BF16)
    grad_scores = grad_scores.reshape(HEADS * PREFIX_PAD, toks).astype(BF16)
    refs.result[...] = dot(grad_scores.T, refs.spread[0])
    own = (
        lax.broadcasted_iota(jnp.int32, (HEADS * PREFIX_PAD, D), 0) // PREFIX_PAD
        == lax.broadcasted_iota(jnp.int32, (HEADS * PREFIX_PAD, D), 1) // HEAD_DIM
    )

    def gather(values):
        return jnp.sum(jnp.where(own, values, 0.0).reshape(HEADS, PREFIX_PAD, D), axis=0)

    sums = gather(dot(grad_scores, queries)), gather(dot(weights, grads))
    for half in range(2):
        refs.prefix_grad[half] = sums[half] if refs.earlier_grad is None else sums[half] + refs.earlier_grad[half]


def attend_back_rows(places, refs, place, pair_step):
    blocks = range(2 * places.level_count)
    masked_blocks = [block for block in blocks if places.masked(block)]
    level = place // 2
    width = 128 * pair_step

    def body(group, carry):
        span = column_group(group, width)
        group_queries = refs.query[:, span]
        group_grads = refs.grad_heads[:, span]
        group_keys = [refs.keyval(block, 0, span) for block in blocks]
        group_values = [refs.keyval(block, 1, span) for block in blocks]

        def products_of(at):
            pair, head = at // 2, at % 2
            cols = slice(pair * 128, (pair + 1) * 128)
            queries = head_lanes(group_queries[:, cols], head)
            grads = head_lanes(group_grads[:, cols], head)
            scores, grad_weights = [], []
            for block in blocks:
                part = dot(group_keys[block][:, cols], queries, NT)
                if block in masked_blocks:
                    part = part + refs.hide[masked_blocks.index(block)]
                scores.append(part)
                grad_weights.append(dot(group_values[block][:, cols], grads, NT))
            return queries, grads, scores, grad_weights

        ahead = products_of(0)
        for at in range(2 * pair_step):
            pair, head = at // 2, at % 2
            cols = slice(pair * 128, (pair + 1) * 128)
            place_cols = pl.ds(pl.multiple_of(group * width + pair * 128, 128), 128)
            queries, grads, scores, grad_weights = ahead
            if at + 1 < 2 * pair_step:
                ahead = products_of(at + 1)
            if head == 0:
                keys_t = [keys[:, cols].T for keys in group_keys]
                grad_keys, grad_values, outs = [], [], []
            total = refs.total[group, at : at + 1, :]
            inner = refs.inner[group, at : at + 1, :]
            rows = slice(head * HEAD_DIM, (head + 1) * HEAD_DIM)
            grad_query = None
            for block in blocks:
                base = total + jnp.where(level >= block // 2, 0.0, FAR) if block > 1 else total
                weights = jnp.exp(scores[block] - base)
                grad_scores = (weights * (grad_weights[block] - inner)).astype(BF16)
                part_values = dot(weights.astype(BF16), grads)
                part_keys = dot(grad_scores, queries)
                part_query = dot(keys_t[block][rows], grad_scores)
                if head == 0:
                    grad_values.append(part_values)
                    grad_keys.append(part_keys)
                else:
                    refs.grad_keyval[block][0, 0, :, place_cols] = (grad_keys[block] + part_keys).astype(BF16)
                    refs.grad_keyval[block][0, 1, :, place_cols] = (grad_values[block] + part_values).astype(BF16)
                grad_query = part_query if grad_query is None else grad_query + part_query
            outs.append(grad_query)
            if head == 1:
                grad_query = jnp.concatenate(outs, axis=0).T + refs.result[:, place_cols]
                refs.grad_query[0, :, place_cols] = (grad_query * 0.125).astype(BF16)
        return carry

    lax.fori_loop(0, PAIRS // pair_step, body, 0)


ROW_NAMES = (
    "tokens", "cotangent", "output_weight", "expand_weight", "contract_weight", "spread", "prefix_scores", "hide", "total",
    "mixed", "grad_out", "residual", "normed", "active", "grad_expand", "result", "grad_normed", "activations",
    "grad_heads", "inner",
)


def row_kernel(places, row, keyval_rows, pair_step, chunk, has_earlier, place_ref, length_ref, source_ref, *rest):
    block_count = 2 * places.level_count
    query_ref, tokens_hbm, cotangent_hbm, prefix_ref = rest[:4]
    keyval_refs = rest[4 : 4 + block_count]
    rest = rest[4 + block_count :]
    output_weight_hbm, expand_weight_hbm, contract_weight_hbm = rest[:3]
    vectors = rest[3:8]
    earlier_grad_ref = rest[8] if has_earlier else None
    rest = rest[8 + 2 * has_earlier :]
    activations_hbm, grad_residual_ref, grad_query_ref = rest[:3]
    grad_keyval_refs = rest[3 : 3 + block_count]
    prefix_grad_ref = rest[3 + block_count]
    rest = rest[4 + block_count :]
    refs = RowRefs(ROW_NAMES, rest)
    refs.output_bias, refs.second_gain, refs.second_shift, refs.expand_bias, refs.contract_bias = vectors
    refs.prefix_grad, refs.earlier_grad = prefix_grad_ref, earlier_grad_ref
    refs.query, refs.prefix = query_ref.at[row], prefix_ref
    refs.keyval = lambda block, half, span: keyval_refs[block][keyval_rows[block], half, :, span]
    refs.grad_residual, refs.grad_query, refs.grad_keyval = grad_residual_ref, grad_query_ref, grad_keyval_refs
    semaphores, weight_semaphores = rest[len(ROW_NAMES) :]
    chunks = refs.expand_weight.shape[0]

    copies = Copies(semaphores)
    copies.start("output", output_weight_hbm, refs.output_weight)
    copies.start("tokens", tokens_hbm.at[row], refs.tokens)
    copies.start("cotangent", cotangent_hbm.at[row], refs.cotangent)

    def weight_copies(at):
        span = pl.ds(pl.multiple_of(at * chunk, chunk), chunk)
        return (
            pltpu.make_async_copy(expand_weight_hbm.at[:, span], refs.expand_weight.at[at], weight_semaphores.at[at]),
            pltpu.make_async_copy(contract_weight_hbm.at[span, :], refs.contract_weight.at[at], weight_semaphores.at[chunks + at]),
        )

    def start_weights(at, carry):
        for copy in weight_copies(at):
            copy.start()
        return carry

    lax.fori_loop(0, chunks, start_weights, 0)
    place = place_ref[0]
    length = length_ref[row]
    limit = places.limits(place, length)
    for half in range(2):
        refs.spread[half] = spread_prefix(refs.prefix[half])
    attend_rows(places, refs, place, limit, pair_step)
    for name in ("output", "tokens", "cotangent"):
        copies.wait(name)
    feed_rows(refs, place, length, source_ref[row], weight_copies, chunks, chunk)
    copies.start("activations", refs.activations, activations_hbm.at[row])
    prefix_back_rows(refs)
    attend_back_rows(places, refs, place, pair_step)
    copies.wait("activations")


def row_block(after, place, lengths, sources, queries, tokens, cotangent, prefix_keyval, keyvals, weights, row, earlier, earlier_grad, pair_step=4, chunk=512):
    toks = queries.shape[1]
    block_count = len(keyvals)
    places = Places(toks, block_count // 2)
    output_weight, output_bias, gain, shift, expand_weight, expand_bias, contract_weight, contract_bias = weights
    hidden = expand_weight.shape[1]
    chunks = hidden // chunk
    given = [] if earlier is None else [earlier_grad, earlier]
    masked = sum(places.masked(block) for block in range(block_count))
    per_group = 2 * pair_step
    scratch = dict(
        tokens=((toks, D), BF16), cotangent=((toks, D), BF16), output_weight=((D, D), BF16),
        expand_weight=((chunks, D, chunk), BF16), contract_weight=((chunks, chunk, D), BF16),
        spread=((2, HEADS * PREFIX_PAD, D), BF16), prefix_scores=((HEADS * PREFIX_PAD, toks), F32),
        hide=((masked, toks, toks), F32), total=((HEADS // per_group, per_group, toks), F32), mixed=((toks, D), BF16),
        grad_out=((toks, D), BF16), residual=((toks, D), F32), normed=((toks, D), BF16),
        active=((2, toks, chunk), BF16), grad_expand=((2, toks, chunk), BF16), result=((toks, D), F32),
        grad_normed=((toks, D), F32), activations=((toks, D), BF16),
        grad_heads=((toks, D), BF16), inner=((HEADS // per_group, per_group, toks), F32),
    )
    return kernel_call(
        functools.partial(row_kernel, places, row, [at for _, at in keyvals], pair_step, chunk, earlier is not None),
        after,
        (
            place, lengths, sources, queries, tokens, cotangent, prefix_keyval, *[array for array, _ in keyvals],
            output_weight, expand_weight, contract_weight, output_bias, gain, shift, expand_bias, contract_bias, *given,
        ),
        ROW_LIMIT,
        [VMEM, ANY, ANY, VMEM] + [VMEM] * block_count + [HBM] * 3 + [VMEM] * 5 + [VMEM, ANY][: len(given)],
        [HBM] + [VMEM] * (3 + block_count),
        [
            jax.ShapeDtypeStruct(tokens.shape, BF16),
            jax.ShapeDtypeStruct((1, toks, D), F32),
            jax.ShapeDtypeStruct((1, toks, D), BF16),
        ]
        + [jax.ShapeDtypeStruct((1, 2, toks, D), BF16)] * block_count
        + [jax.ShapeDtypeStruct((2, PREFIX_PAD, D), F32)],
        prefetched=3,
        scratch_shapes=[pltpu.VMEM(*scratch[name]) for name in ROW_NAMES]
        + [pltpu.SemaphoreType.DMA((4,)), pltpu.SemaphoreType.DMA((2 * chunks,))],
        input_output_aliases={16 + block_count: 0} if given else {},
        name="row_block",
    )


def up_back_kernel(own_ref, received_ref, weight_ref, grad_ref):
    total = None
    for half in range(2):
        values = (own_ref[0, half].astype(F32) + received_ref[0, half].astype(F32)).astype(BF16)
        part = dot(values, weight_ref[:, (half + 1) * D : (half + 2) * D], NT)
        total = part if total is None else total + part
    grad_ref[0] = total.astype(BF16)


def up_back(after, own, received, weight):
    toks = own.shape[2]
    return kernel_call(
        up_back_kernel,
        after,
        (own, received, weight),
        10,
        [VMEM] * 3,
        [VMEM],
        [jax.ShapeDtypeStruct((1, toks, D), BF16)],
        name="up_back",
    )


def project_back_kernel(query_ref, own_ref, received_ref, weight_ref, total_ref):
    total = dot(query_ref[0], weight_ref[:, :D], NT)
    for half in range(2):
        values = (own_ref[0, half].astype(F32) + received_ref[0, half].astype(F32)).astype(BF16)
        total = total + dot(values, weight_ref[:, (half + 1) * D : (half + 2) * D], NT)
    total_ref[0] = total


def project_back(after, grad_query, own, received, weight):
    toks = grad_query.shape[1]
    return kernel_call(
        project_back_kernel,
        after,
        (grad_query, own, received, weight),
        10,
        [VMEM] * 4,
        [VMEM],
        [jax.ShapeDtypeStruct((1, toks, D), F32)],
        name="project_back",
    )


def finish_kernel(above_count, row, tokens_hbm, gain_ref, residual_ref, total_ref, *rest):
    grad_hbm, tokens_ref, grad_ref, semaphores = rest[-4:]
    toks = tokens_ref.shape[0]
    copies = Copies(semaphores)
    copies.start("tokens", tokens_hbm.at[row], tokens_ref)
    copies.wait("tokens")
    parts = 2
    for part in range(parts):
        span = pl.ds(part * (toks // parts), toks // parts)
        total = total_ref[0, span]
        for above_ref in rest[:above_count]:
            total = total + above_ref[0, span].astype(F32)
        normed, scale = normalize(tokens_ref[span].astype(F32))
        grad_ref[span] = residual_ref[0, span] + norm_back(total * gain_ref[...], normed, scale)
        copies.start(part, grad_ref.at[span], grad_hbm.at[row, span])
    for part in range(parts):
        copies.wait(part)


def finish(after, tokens, gain, grad_residual, total, above, row, earlier):
    toks = tokens.shape[1]
    given = [] if earlier is None else [earlier]
    return kernel_call(
        functools.partial(finish_kernel, len(above), row),
        after,
        (tokens, gain, grad_residual, total, *above, *given),
        10,
        [ANY] + [VMEM] * (3 + len(above)) + [ANY] * len(given),
        [HBM],
        [jax.ShapeDtypeStruct(tokens.shape, F32)],
        scratch_shapes=[pltpu.VMEM((toks, D), BF16), pltpu.VMEM((toks, D), F32), pltpu.SemaphoreType.DMA((3,))],
        input_output_aliases={4 + len(above): 0} if given else {},
        name="finish",
    )


def prefix_kernel(table_ref, lift_ref, lift_bias_ref, fan_ref, fan_bias_ref, lifted_ref, keyval_ref):
    lifted = jnp.tanh(dot(table_ref[...], lift_ref[...]) + lift_bias_ref[...])
    lifted_ref[...] = jnp.zeros_like(lifted_ref)
    lifted_ref[:PREFIX, :] = lifted
    keyval_ref[...] = jnp.zeros_like(keyval_ref)
    keyval = (dot(lifted.astype(BF16), fan_ref[...]) + fan_bias_ref[...]).astype(BF16)
    keyval_ref[0, :PREFIX, :] = keyval[:, :D]
    keyval_ref[1, :PREFIX, :] = keyval[:, D:]


def prefix_forward(after, table, lift, lift_bias, fan, fan_bias):
    return kernel_call(
        prefix_kernel,
        after,
        (table, lift, lift_bias, fan, fan_bias),
        8,
        [VMEM] * 5,
        [VMEM] * 2,
        [
            jax.ShapeDtypeStruct((PREFIX_PAD, lift.shape[1]), F32),
            jax.ShapeDtypeStruct((2, PREFIX_PAD, D), BF16),
        ],
        name="prefix_forward",
    )


def prefix_network_back_kernel(grad_ref, table_ref, lift_ref, fan_ref, lifted_ref, grad_table_ref, grad_lift_ref, grad_lift_bias_ref, grad_fan_ref, grad_fan_bias_ref):
    lifted = lifted_ref[...]
    lifted_t = jnp.concatenate([lifted.astype(BF16)] * 2, axis=0).T
    grad_lifted = None
    for half in range(2):
        cols = slice(half * D, (half + 1) * D)
        grad = grad_ref[half]
        grad_fan_bias_ref[:, cols] = jnp.sum(grad, axis=0, keepdims=True)
        both = jnp.concatenate(split(grad), axis=0)
        grad_fan_ref[:, cols] = dot(lifted_t, both)
        part = dot(both, fan_ref[:, cols], NT)
        grad_lifted = part if grad_lifted is None else grad_lifted + part
    grad_lifted = (grad_lifted[:PREFIX_PAD] + grad_lifted[PREFIX_PAD:]) * (1.0 - lifted * lifted)
    grad_lift_bias_ref[...] = jnp.sum(grad_lifted, axis=0, keepdims=True)
    both = jnp.concatenate(split(grad_lifted), axis=0)
    table = jnp.concatenate([table_ref[...].astype(F32), jnp.zeros((PREFIX_PAD - PREFIX, D), F32)], axis=0)
    table_t = jnp.concatenate([table.astype(BF16)] * 2, axis=0).T
    grad_lift_ref[...] = dot(table_t, both)
    grad_table = dot(both, lift_ref[...], NT)
    grad_table_ref[...] = (grad_table[:PREFIX_PAD] + grad_table[PREFIX_PAD:])[:PREFIX]


def prefix_network_back(after, grad, table, lift, fan, lifted):
    hidden = lift.shape[1]
    return kernel_call(
        prefix_network_back_kernel,
        after,
        (grad, table, lift, fan, lifted),
        20,
        [VMEM] * 5,
        [VMEM] * 5,
        [
            jax.ShapeDtypeStruct((PREFIX, D), F32),
            jax.ShapeDtypeStruct((D, hidden), F32),
            jax.ShapeDtypeStruct((1, hidden), F32),
            jax.ShapeDtypeStruct((hidden, 2 * D), F32),
            jax.ShapeDtypeStruct((1, 2 * D), F32),
        ],
        name="prefix_network_back",
    )


def add_kernel(left_ref, right_ref, sum_ref):
    sum_ref[...] = left_ref[...] + right_ref[...]


def add(after, left, right):
    return kernel_call(add_kernel, after, (left, right), 2, [VMEM] * 2, [VMEM], [left], name="add")


class Order:
    def __init__(self):
        self.before = ()

    def call(self, kernel, *operands):
        *outs, token = kernel(self.before, *operands)
        self.before = (token,)
        return outs[0] if len(outs) == 1 else outs


def sum_hops(axes):
    hops = []
    for axis in axes:
        size = lax.axis_size(axis)
        if size & (size - 1):
            return None
        hop = 1
        while hop < size:
            hops.append((axis, [(at, at ^ hop) for at in range(size)]))
            hop *= 2
    return hops


def per_device(tokens, cotangent, row_lengths, source_lengths, first_gain, first_shift, attend_weight, attend_bias, output_weight, output_bias, second_gain, second_shift, expand_weight, expand_bias, contract_weight, contract_bias, prefix_table, lift_weight, lift_bias, fan_weight, fan_bias):
    rows = tokens.shape[0]
    seq = lax.axis_size("seq")
    level_count = seq // 2
    levels = range(1, level_count)
    mates = [(at, at ^ 1) for at in range(seq)]
    place = lax.axis_index("seq").astype(jnp.int32).reshape(1)
    first_gain, first_shift, attend_bias, output_bias, second_gain, second_shift, expand_bias, contract_bias, lift_bias, fan_bias = [
        vector.reshape(1, -1)
        for vector in (first_gain, first_shift, attend_bias, output_bias, second_gain, second_shift, expand_bias, contract_bias, lift_bias, fan_bias)
    ]
    weights = (output_weight, output_bias, second_gain, second_shift, expand_weight, expand_bias, contract_weight, contract_bias)
    order = Order()
    hops = sum_hops(("seq", "dp"))
    activations = None
    input_grad = None
    prefix_grad = None
    arriving = None

    def swap(array):
        return lax.ppermute(array, "seq", mates)

    def hop():
        nonlocal prefix_grad, arriving
        if arriving is not None:
            prefix_grad = order.call(add, prefix_grad, arriving)
            arriving = None
        if hops:
            axis, pairs = hops.pop(0)
            arriving = lax.ppermute(prefix_grad, axis, pairs)

    def lower(row):
        blocks = []
        for level in levels:
            block = order.call(project_up, lower_tokens[row, level], first_gain, first_shift, attend_weight, attend_bias)
            blocks += [block, swap(block)]
        return blocks

    def keyvals_of(row, blocks):
        return [(keyval, row), (mate_keyval, row)] + [(block, 0) for block in blocks]

    row_tokens = [tokens[:1]]
    lower_tokens = {}

    def raise_tokens(row):
        for level in levels:
            pairs = [(at, at + 2 * level) for at in range(seq - 2 * level)]
            lower_tokens[row, level] = lax.ppermute(row_tokens[row], "seq", pairs)

    raise_tokens(0)
    queries, keyval, *later = order.call(project_own, tokens, first_gain, first_shift, attend_weight, attend_bias)
    row_tokens += later
    for row in range(1, rows):
        raise_tokens(row)
    mate_keyval = swap(keyval)
    lifted, prefix_keyval = order.call(prefix_forward, prefix_table, lift_weight, lift_bias, fan_weight, fan_bias)
    blocks = lower(0)
    waiting = []
    for row in range(rows):
        last_row = row + 1 == rows
        activations, grad_residual, grad_query, *grads, prefix_grad = order.call(
            row_block, place, row_lengths, source_lengths, queries, tokens, cotangent, prefix_keyval,
            keyvals_of(row, blocks), weights, row, activations, prefix_grad,
        )
        received = swap(grads[1])
        from_mates = [swap(grads[2 * level + 1]) for level in levels]
        if last_row:
            if hops is None:
                prefix_grad = lax.psum(prefix_grad, ("seq", "dp"))
            hop()
            for earlier in waiting:
                earlier()
                hop()
        else:
            blocks = lower(row + 1)
        above = []
        for level in levels:
            part = order.call(up_back, grads[2 * level], from_mates[level - 1], attend_weight)
            above.append(lax.ppermute(part, "seq", [(at + 2 * level, at) for at in range(seq - 2 * level)]))
        if last_row:
            hop()
        total = order.call(project_back, grad_query, grads[0], received, attend_weight)

        def end(row=row, grad_residual=grad_residual, total=total, above=above):
            nonlocal input_grad
            input_grad = order.call(finish, tokens, first_gain, grad_residual, total, above, row, input_grad)

        waiting.append(end)
    while hops or arriving is not None:
        hop()
    grad_table, grad_lift, grad_lift_bias, grad_fan, grad_fan_bias = order.call(
        prefix_network_back, prefix_grad, prefix_table, lift_weight, fan_weight, lifted
    )
    waiting[-1]()
    return (activations, input_grad, grad_table, grad_lift, grad_lift_bias.reshape(-1), grad_fan, grad_fan_bias.reshape(-1))


def solution(mesh):
    batch = P("dp", "seq", None)
    return jax.shard_map(
        per_device,
        mesh=mesh,
        in_specs=(batch, batch, P("dp"), P("dp")) + (P(),) * 17,
        out_specs=(batch, batch, P(), P(), P(), P(), P()),
        check_vma=False,
    )
```

```python
import functools

import jax
import jax.numpy as jnp
from jax import lax
from jax.experimental import pallas as pl
from jax.experimental.pallas import tpu as pltpu
from jax.sharding import PartitionSpec as P

D = 1024
HEADS = 16
HEAD_DIM = 64
PAIRS = HEADS // 2
PREFIX = 10
PREFIX_PAD = 16
LEAST_LENGTH = 512
NN = (((1,), (0,)), ((), ()))
NT = (((1,), (1,)), ((), ()))
MIB = 1 << 20
BF16 = jnp.bfloat16
F32 = jnp.float32


def dot(left, right, dims=NN):
    return lax.dot_general(left, right, dims, preferred_element_type=F32)


ANY = pl.BlockSpec(memory_space=pl.ANY)


VMEM = pl.BlockSpec(memory_space=pltpu.VMEM)
COVER = pl.CostEstimate(flops=10**10, bytes_accessed=10**9, transcendentals=0)
TOKEN = jax.ShapeDtypeStruct((8, 128), F32)


def kernel_call(kernel, after, operands, limit, in_specs, out_specs, out_shape, prefetched=0, scratch_shapes=(), **rest):
    lead = prefetched + len(in_specs)

    def body(*refs):
        outs = lead + len(after)
        token_ref = refs[outs + len(out_shape)]
        token_ref[...] = jnp.zeros_like(token_ref)
        kernel(*refs[:lead], *refs[outs : outs + len(out_shape)], *refs[outs + len(out_shape) + 1 :])

    spec = pltpu.PrefetchScalarGridSpec(
        num_scalar_prefetch=prefetched,
        grid=(1,),
        in_specs=[*in_specs] + [ANY] * len(after),
        out_specs=[*out_specs, VMEM],
        scratch_shapes=scratch_shapes,
    )
    return pl.pallas_call(
        body,
        grid_spec=spec,
        out_shape=[*(jax.ShapeDtypeStruct(out.shape, out.dtype) for out in out_shape), TOKEN],
        compiler_params=pltpu.CompilerParams(dimension_semantics=("arbitrary",), vmem_limit_bytes=limit * MIB),
        cost_estimate=COVER,
        **rest,
    )(*operands, *after)


def split(values):
    high = values.astype(BF16)
    return high, (values - high.astype(F32)).astype(BF16)


class Copies:
    def __init__(self, semaphores):
        self.semaphores = semaphores
        self.count = 0
        self.copies = {}

    def start(self, name, source, target):
        copy = pltpu.make_async_copy(source, target, self.semaphores.at[self.count])
        copy.start()
        self.count += 1
        self.copies[name] = copy

    def wait(self, name):
        self.copies[name].wait()


HBM = pl.BlockSpec(memory_space=pltpu.HBM)


def normalize(values):
    centred = values - jnp.mean(values, axis=-1, keepdims=True)
    scale = lax.rsqrt(jnp.mean(centred * centred, axis=-1, keepdims=True) + 1e-05)
    return centred * scale, scale


def norm_back(grad, normed, scale):
    return scale * (
        grad
        - jnp.mean(grad, axis=-1, keepdims=True)
        - normed * jnp.mean(grad * normed, axis=-1, keepdims=True)
    )


def project_own_kernel(tokens_ref, gain_ref, shift_ref, bias_ref, weight_ref, query_ref, keyval_ref, *rest):
    later_refs, normed_ref = rest[:-1], rest[-1]
    rows, toks, _ = tokens_ref.shape
    for at, later_ref in enumerate(later_refs):
        later_ref[0] = tokens_ref[at + 1]
    normed, _ = normalize(tokens_ref[...].reshape(rows * toks, D).astype(F32))
    normed_ref[...] = (normed * gain_ref[...] + shift_ref[...]).astype(BF16)
    chunk = D // 2
    for at in range(6):
        span = slice(at * chunk, (at + 1) * chunk)
        result = (dot(normed_ref[...], weight_ref[:, span]) + bias_ref[:, span]).astype(BF16)
        cols = slice(at % 2 * chunk, (at % 2 + 1) * chunk)
        if at < 2:
            query_ref[:, :, cols] = (result * 0.125).reshape(rows, toks, chunk)
        else:
            keyval_ref[:, at // 2 - 1, :, cols] = result.reshape(rows, toks, chunk)


def project_own(after, tokens, gain, shift, weight, bias):
    rows, toks, _ = tokens.shape
    return kernel_call(
        project_own_kernel,
        after,
        (tokens, gain, shift, bias, weight),
        14,
        [VMEM] * 5,
        [VMEM] * (1 + rows),
        [jax.ShapeDtypeStruct((rows, toks, D), BF16), jax.ShapeDtypeStruct((rows, 2, toks, D), BF16)]
        + [jax.ShapeDtypeStruct((1, toks, D), BF16)] * (rows - 1),
        scratch_shapes=[pltpu.VMEM((rows * toks, D), BF16)],
        name="project_own",
    )


def project_up_kernel(tokens_ref, gain_ref, shift_ref, bias_ref, weight_ref, keyval_ref):
    toks = tokens_ref.shape[1]
    normed, _ = normalize(tokens_ref[0].astype(F32))
    normed = (normed * gain_ref[...] + shift_ref[...]).astype(BF16)
    for half in range(2):
        cols = slice((half + 1) * D, (half + 2) * D)
        keyval_ref[0, half] = (dot(normed, weight_ref[:, cols]) + bias_ref[:, cols]).astype(BF16)


def project_up(after, tokens, gain, shift, weight, bias):
    toks = tokens.shape[1]
    return kernel_call(
        project_up_kernel,
        after,
        (tokens, gain, shift, bias, weight),
        10,
        [VMEM] * 5,
        [VMEM],
        [jax.ShapeDtypeStruct((1, 2, toks, D), BF16)],
        name="project_up",
    )


def head_lanes(values, head):
    lanes = lax.broadcasted_iota(jnp.int32, values.shape, 1)
    keep = lanes < HEAD_DIM if head == 0 else lanes >= HEAD_DIM
    return jnp.where(keep, values, jnp.zeros_like(values))


def prefix_mask(values, fill):
    places = lax.broadcasted_iota(jnp.int32, values.shape, 0)
    return jnp.where(places < PREFIX, values, fill)


class Places:
    def __init__(self, toks, level_count):
        self.toks = toks
        self.level_count = level_count

    def masked(self, block):
        if block < 2:
            return True
        level = block // 2
        return (self.level_count - level) * 2 * self.toks > LEAST_LENGTH

    def limits(self, place, length):
        base = place * self.toks
        queries = base + lax.broadcasted_iota(jnp.int32, (1, self.toks), 1)
        return jnp.minimum(queries, length - 1)

    def visible(self, block, place, limit):
        if block == 0:
            base = place * self.toks
        else:
            base = (lax.bitwise_xor(place, block % 2) - (block // 2) * 2) * self.toks
        keys = lax.broadcasted_iota(jnp.int32, (self.toks, self.toks), 0)
        return keys <= limit - base


def spread_prefix(prefix):
    tiled = jnp.concatenate([prefix] * HEADS, axis=0)
    rows = lax.broadcasted_iota(jnp.int32, tiled.shape, 0) // PREFIX_PAD
    cols = lax.broadcasted_iota(jnp.int32, tiled.shape, 1) // HEAD_DIM
    return jnp.where(rows == cols, tiled, jnp.zeros_like(tiled))


GELU_SCALE = 0.7978845608028654
GELU_CUBE = 0.044715
FAR = 1e30
ROW_LIMIT = 32


class RowRefs:
    def __init__(self, names, refs):
        for name, ref in zip(names, refs):
            setattr(self, name, ref)


def column_group(group, width):
    return pl.ds(pl.multiple_of(group * width, width), width)


def attend_rows(places, refs, place, limit, pair_step):
    blocks = range(2 * places.level_count)
    masked_blocks = [block for block in blocks if places.masked(block)]
    level = place // 2
    width = 128 * pair_step
    refs.prefix_scores[...] = dot(refs.spread[0], refs.query[...], NT)
    for at, block in enumerate(masked_blocks):
        refs.hide[at] = jnp.where(places.visible(block, place, limit), 0.0, -jnp.inf)

    def beyond(block):
        return jnp.where(level >= block // 2, 0.0, FAR) if block > 1 else None

    def body(group, carry):
        span = column_group(group, width)
        group_queries = refs.query[:, span]
        group_keys = [refs.keyval(block, 0, span) for block in blocks]

        def scores_of(at):
            pair, head = at // 2, at % 2
            cols = slice(pair * 128, (pair + 1) * 128)
            queries = head_lanes(group_queries[:, cols], head)
            spot = pl.multiple_of((group * pair_step * 2 + at) * PREFIX_PAD, PREFIX_PAD)
            prefix_scores = prefix_mask(refs.prefix_scores[pl.ds(spot, PREFIX_PAD), :], -jnp.inf)
            highest = jnp.max(prefix_scores, axis=0, keepdims=True)
            scores = []
            for block in blocks:
                part = dot(group_keys[block][:, cols], queries, NT)
                if block in masked_blocks:
                    part = part + refs.hide[masked_blocks.index(block)]
                top = jnp.max(part, axis=0, keepdims=True)
                if block > 1:
                    top = top - beyond(block)
                highest = jnp.maximum(highest, top)
                scores.append(part)
            return prefix_scores, scores, highest

        ahead = scores_of(0)
        for at in range(2 * pair_step):
            pair, head = at // 2, at % 2
            cols = slice(pair * 128, (pair + 1) * 128)
            prefix_scores, scores, highest = ahead
            if at + 1 < 2 * pair_step:
                ahead = scores_of(at + 1)
            if head == 0:
                values_t = [refs.keyval(block, 1, span)[:, cols].T for block in blocks]
                prefix_values_t = refs.prefix[1, :, span][:, cols].T
                outs = []
            rows = slice(head * HEAD_DIM, (head + 1) * HEAD_DIM)
            prefix_weights = jnp.exp(prefix_scores - highest)
            total = jnp.sum(prefix_weights, axis=0, keepdims=True)
            mixed = dot(prefix_values_t[rows], prefix_weights.astype(BF16))
            for block in blocks:
                base = highest + beyond(block) if block > 1 else highest
                weights = jnp.exp(scores[block] - base)
                total = total + jnp.sum(weights, axis=0, keepdims=True)
                mixed = mixed + dot(values_t[block][rows], weights.astype(BF16))
            outs.append(mixed * (1.0 / total))
            refs.total[group, at : at + 1, :] = highest + jnp.log(total)
            if head == 1:
                refs.mixed[:, pl.ds(pl.multiple_of(group * width + pair * 128, 128), 128)] = jnp.concatenate(outs, axis=0).T.astype(BF16)
        return carry

    lax.fori_loop(0, PAIRS // pair_step, body, 0)


def feed_rows(refs, place, length, source, weight_copies, chunks, chunk, slots):
    toks = refs.tokens.shape[0]
    spots = place * toks + lax.broadcasted_iota(jnp.int32, (toks, D), 0)
    target = (spots >= source) & (spots < length)
    refs.grad_out[...] = jnp.where(target, refs.cotangent[...].astype(F32), 0.0).astype(BF16)
    residual = refs.tokens[...].astype(F32) + dot(refs.mixed[...], refs.output_weight[...]) + refs.output_bias[...]
    refs.residual[...] = residual
    normed, _ = normalize(residual)
    refs.normed[...] = (normed * refs.second_gain[...] + refs.second_shift[...]).astype(BF16)

    def first(at, slot):
        for copy in weight_copies(at):
            copy.wait()
        bias = refs.expand_bias[:, pl.ds(pl.multiple_of(at * chunk, chunk), chunk)]
        values = dot(refs.normed[...], refs.expand_weight[at % slots]) + bias
        grad_hidden = dot(refs.grad_out[...], refs.contract_weight[at % slots], NT)
        square = values * values
        bend = jnp.tanh(values * (GELU_SCALE + GELU_SCALE * GELU_CUBE * square))
        half = 0.5 + 0.5 * bend
        slope = half + (0.5 * values) * (1.0 - bend * bend) * (
            GELU_SCALE + 3.0 * GELU_SCALE * GELU_CUBE * square
        )
        refs.active[slot] = (values * half).astype(BF16)
        refs.grad_expand[slot] = (grad_hidden * slope).astype(BF16)

    def second(at, slot):
        refs.result[...] += dot(refs.active[slot], refs.contract_weight[at % slots])
        refs.grad_normed[...] += dot(refs.grad_expand[slot], refs.expand_weight[at % slots], NT)

    def refill(at):
        @pl.when(at + slots < chunks)
        def _():
            for copy in weight_copies(at + slots):
                copy.start()

    refs.result[...] = jnp.zeros_like(refs.result)
    refs.grad_normed[...] = jnp.zeros_like(refs.grad_normed)
    first(0, 0)

    def body(at, carry):
        first(2 * at + 1, 1)
        second(2 * at, 0)
        refill(2 * at)
        first(2 * at + 2, 0)
        second(2 * at + 1, 1)
        refill(2 * at + 1)
        return carry

    lax.fori_loop(0, chunks // 2 - 1, body, 0)
    first(chunks - 1, 1)
    second(chunks - 2, 0)
    second(chunks - 1, 1)

    residual = refs.residual[...]
    refs.activations[...] = (residual + refs.result[...] + refs.contract_bias[...]).astype(BF16)
    normed, scale = normalize(residual)
    grad = refs.grad_out[...].astype(F32) + norm_back(refs.grad_normed[...] * refs.second_gain[...], normed, scale)
    refs.grad_residual[0] = grad
    refs.grad_heads[...] = dot(grad.astype(BF16), refs.output_weight[...], NT).astype(BF16)


def prefix_back_rows(refs):
    toks = refs.query.shape[0]
    queries = refs.query[...]
    grads = refs.grad_heads[...]
    product = grads.astype(F32) * refs.mixed[...].astype(F32)
    head_of = lax.broadcasted_iota(jnp.int32, (HEADS, D), 1) // HEAD_DIM
    chosen = jnp.where(head_of == lax.broadcasted_iota(jnp.int32, (HEADS, D), 0), 1.0, 0.0).astype(BF16)
    high, low = split(product)
    inner = dot(chosen, high, NT) + dot(chosen, low, NT)
    refs.inner[...] = inner.reshape(refs.inner.shape)

    def per_head(values):
        return values.reshape(HEADS, PREFIX_PAD, toks)

    scores = per_head(refs.prefix_scores[...])
    grad_weights = per_head(dot(refs.spread[1], grads, NT))
    weights = jnp.exp(scores - refs.total[...].reshape(HEADS, 1, toks))
    valid = lax.broadcasted_iota(jnp.int32, weights.shape, 1) < PREFIX
    weights = jnp.where(valid, weights, 0.0)
    grad_scores = weights * (grad_weights - inner[:, None, :])
    weights = weights.reshape(HEADS * PREFIX_PAD, toks).astype(BF16)
    grad_scores = grad_scores.reshape(HEADS * PREFIX_PAD, toks).astype(BF16)
    refs.result[...] = dot(grad_scores.T, refs.spread[0])
    own = (
        lax.broadcasted_iota(jnp.int32, (HEADS * PREFIX_PAD, D), 0) // PREFIX_PAD
        == lax.broadcasted_iota(jnp.int32, (HEADS * PREFIX_PAD, D), 1) // HEAD_DIM
    )

    def gather(values):
        return jnp.sum(jnp.where(own, values, 0.0).reshape(HEADS, PREFIX_PAD, D), axis=0)

    sums = gather(dot(grad_scores, queries)), gather(dot(weights, grads))
    for half in range(2):
        refs.prefix_grad[half] = sums[half] if refs.earlier_grad is None else sums[half] + refs.earlier_grad[half]


def attend_back_rows(places, refs, place, pair_step):
    blocks = range(2 * places.level_count)
    masked_blocks = [block for block in blocks if places.masked(block)]
    level = place // 2
    width = 128 * pair_step

    def body(group, carry):
        span = column_group(group, width)
        group_queries = refs.query[:, span]
        group_grads = refs.grad_heads[:, span]
        group_keys = [refs.keyval(block, 0, span) for block in blocks]
        group_values = [refs.keyval(block, 1, span) for block in blocks]

        def products_of(at):
            pair, head = at // 2, at % 2
            cols = slice(pair * 128, (pair + 1) * 128)
            queries = head_lanes(group_queries[:, cols], head)
            grads = head_lanes(group_grads[:, cols], head)
            scores, grad_weights = [], []
            for block in blocks:
                part = dot(group_keys[block][:, cols], queries, NT)
                if block in masked_blocks:
                    part = part + refs.hide[masked_blocks.index(block)]
                scores.append(part)
                grad_weights.append(dot(group_values[block][:, cols], grads, NT))
            return queries, grads, scores, grad_weights

        ahead = products_of(0)
        for at in range(2 * pair_step):
            pair, head = at // 2, at % 2
            cols = slice(pair * 128, (pair + 1) * 128)
            place_cols = pl.ds(pl.multiple_of(group * width + pair * 128, 128), 128)
            queries, grads, scores, grad_weights = ahead
            if at + 1 < 2 * pair_step:
                ahead = products_of(at + 1)
            if head == 0:
                keys_t = [keys[:, cols].T for keys in group_keys]
                grad_keys, grad_values, outs = [], [], []
            total = refs.total[group, at : at + 1, :]
            inner = refs.inner[group, at : at + 1, :]
            rows = slice(head * HEAD_DIM, (head + 1) * HEAD_DIM)
            grad_query = None
            for block in blocks:
                base = total + jnp.where(level >= block // 2, 0.0, FAR) if block > 1 else total
                weights = jnp.exp(scores[block] - base)
                grad_scores = (weights * (grad_weights[block] - inner)).astype(BF16)
                part_values = dot(weights.astype(BF16), grads)
                part_keys = dot(grad_scores, queries)
                part_query = dot(keys_t[block][rows], grad_scores)
                if head == 0:
                    grad_values.append(part_values)
                    grad_keys.append(part_keys)
                else:
                    refs.grad_keyval[block][0, 0, :, place_cols] = (grad_keys[block] + part_keys).astype(BF16)
                    refs.grad_keyval[block][0, 1, :, place_cols] = (grad_values[block] + part_values).astype(BF16)
                grad_query = part_query if grad_query is None else grad_query + part_query
            outs.append(grad_query)
            if head == 1:
                grad_query = jnp.concatenate(outs, axis=0).T + refs.result[:, place_cols]
                refs.grad_query[0, :, place_cols] = (grad_query * 0.125).astype(BF16)
        return carry

    lax.fori_loop(0, PAIRS // pair_step, body, 0)


ROW_NAMES = (
    "expand_weight", "contract_weight", "spread", "prefix_scores", "hide", "total",
    "mixed", "grad_out", "residual", "normed", "active", "grad_expand", "result", "grad_normed", "activations",
    "grad_heads", "inner",
)


def row_kernel(places, row, keyval_rows, pair_step, chunk, has_earlier, place_ref, length_ref, source_ref, *rest):
    block_count = 2 * places.level_count
    query_ref, tokens_ref, cotangent_ref, prefix_ref = rest[:4]
    keyval_refs = rest[4 : 4 + block_count]
    rest = rest[4 + block_count :]
    output_weight_ref, expand_weight_hbm, contract_weight_hbm = rest[:3]
    vectors = rest[3:8]
    earlier_grad_ref = rest[8] if has_earlier else None
    rest = rest[8 + 2 * has_earlier :]
    activations_hbm, grad_residual_ref, grad_query_ref = rest[:3]
    grad_keyval_refs = rest[3 : 3 + block_count]
    prefix_grad_ref = rest[3 + block_count]
    rest = rest[4 + block_count :]
    refs = RowRefs(ROW_NAMES, rest)
    refs.output_bias, refs.second_gain, refs.second_shift, refs.expand_bias, refs.contract_bias = vectors
    refs.prefix_grad, refs.earlier_grad = prefix_grad_ref, earlier_grad_ref
    refs.query, refs.prefix = query_ref.at[row], prefix_ref
    refs.keyval = lambda block, half, span: keyval_refs[block][keyval_rows[block], half, :, span]
    refs.grad_residual, refs.grad_query, refs.grad_keyval = grad_residual_ref, grad_query_ref, grad_keyval_refs
    semaphores, weight_semaphores = rest[len(ROW_NAMES) :]
    slots = refs.expand_weight.shape[0]
    chunks = expand_weight_hbm.shape[1] // chunk

    copies = Copies(semaphores)
    refs.output_weight, refs.tokens, refs.cotangent = output_weight_ref, tokens_ref.at[row], cotangent_ref.at[row]

    def weight_copies(at):
        span = pl.ds(pl.multiple_of(at * chunk, chunk), chunk)
        return (
            pltpu.make_async_copy(expand_weight_hbm.at[:, span], refs.expand_weight.at[at % slots], weight_semaphores.at[at]),
            pltpu.make_async_copy(contract_weight_hbm.at[span, :], refs.contract_weight.at[at % slots], weight_semaphores.at[chunks + at]),
        )

    def start_weights(at, carry):
        for copy in weight_copies(at):
            copy.start()
        return carry

    lax.fori_loop(0, slots, start_weights, 0)
    place = place_ref[0]
    length = length_ref[row]
    limit = places.limits(place, length)
    for half in range(2):
        refs.spread[half] = spread_prefix(refs.prefix[half])
    attend_rows(places, refs, place, limit, pair_step)
    feed_rows(refs, place, length, source_ref[row], weight_copies, chunks, chunk, slots)
    copies.start("activations", refs.activations, activations_hbm.at[row])
    prefix_back_rows(refs)
    attend_back_rows(places, refs, place, pair_step)
    copies.wait("activations")


def row_block(after, place, lengths, sources, queries, tokens, cotangent, prefix_keyval, keyvals, weights, row, earlier, earlier_grad, pair_step=2, chunk=512, slots=4):
    toks = queries.shape[1]
    block_count = len(keyvals)
    places = Places(toks, block_count // 2)
    output_weight, output_bias, gain, shift, expand_weight, expand_bias, contract_weight, contract_bias = weights
    hidden = expand_weight.shape[1]
    chunks = hidden // chunk
    given = [] if earlier is None else [earlier_grad, earlier]
    masked = sum(places.masked(block) for block in range(block_count))
    per_group = 2 * pair_step
    scratch = dict(
        expand_weight=((slots, D, chunk), BF16), contract_weight=((slots, chunk, D), BF16),
        spread=((2, HEADS * PREFIX_PAD, D), BF16), prefix_scores=((HEADS * PREFIX_PAD, toks), F32),
        hide=((masked, toks, toks), F32), total=((HEADS // per_group, per_group, toks), F32), mixed=((toks, D), BF16),
        grad_out=((toks, D), BF16), residual=((toks, D), F32), normed=((toks, D), BF16),
        active=((2, toks, chunk), BF16), grad_expand=((2, toks, chunk), BF16), result=((toks, D), F32),
        grad_normed=((toks, D), F32), activations=((toks, D), BF16),
        grad_heads=((toks, D), BF16), inner=((HEADS // per_group, per_group, toks), F32),
    )
    return kernel_call(
        functools.partial(row_kernel, places, row, [at for _, at in keyvals], pair_step, chunk, earlier is not None),
        after,
        (
            place, lengths, sources, queries, tokens, cotangent, prefix_keyval, *[array for array, _ in keyvals],
            output_weight, expand_weight, contract_weight, output_bias, gain, shift, expand_bias, contract_bias, *given,
        ),
        ROW_LIMIT,
        [VMEM] * (4 + block_count) + [VMEM, HBM, HBM] + [VMEM] * 5 + [VMEM, ANY][: len(given)],
        [HBM] + [VMEM] * (3 + block_count),
        [
            jax.ShapeDtypeStruct(tokens.shape, BF16),
            jax.ShapeDtypeStruct((1, toks, D), F32),
            jax.ShapeDtypeStruct((1, toks, D), BF16),
        ]
        + [jax.ShapeDtypeStruct((1, 2, toks, D), BF16)] * block_count
        + [jax.ShapeDtypeStruct((2, PREFIX_PAD, D), F32)],
        prefetched=3,
        scratch_shapes=[pltpu.VMEM(*scratch[name]) for name in ROW_NAMES]
        + [pltpu.SemaphoreType.DMA((1,)), pltpu.SemaphoreType.DMA((2 * chunks,))],
        input_output_aliases={16 + block_count: 0} if given else {},
        name="row_block",
    )


def up_back_kernel(own_ref, received_ref, weight_ref, grad_ref):
    total = None
    for half in range(2):
        values = (own_ref[0, half].astype(F32) + received_ref[0, half].astype(F32)).astype(BF16)
        part = dot(values, weight_ref[:, (half + 1) * D : (half + 2) * D], NT)
        total = part if total is None else total + part
    grad_ref[0] = total.astype(BF16)


def up_back(after, own, received, weight):
    toks = own.shape[2]
    return kernel_call(
        up_back_kernel,
        after,
        (own, received, weight),
        10,
        [VMEM] * 3,
        [VMEM],
        [jax.ShapeDtypeStruct((1, toks, D), BF16)],
        name="up_back",
    )


def project_back_kernel(query_ref, own_ref, received_ref, weight_ref, total_ref):
    total = dot(query_ref[0], weight_ref[:, :D], NT)
    for half in range(2):
        values = (own_ref[0, half].astype(F32) + received_ref[0, half].astype(F32)).astype(BF16)
        total = total + dot(values, weight_ref[:, (half + 1) * D : (half + 2) * D], NT)
    total_ref[0] = total


def project_back(after, grad_query, own, received, weight):
    toks = grad_query.shape[1]
    return kernel_call(
        project_back_kernel,
        after,
        (grad_query, own, received, weight),
        10,
        [VMEM] * 4,
        [VMEM],
        [jax.ShapeDtypeStruct((1, toks, D), F32)],
        name="project_back",
    )


def finish_kernel(above_count, row, tokens_ref, gain_ref, residual_ref, total_ref, *rest):
    grad_hbm, grad_ref, semaphores = rest[-3:]
    toks = grad_ref.shape[0]
    copies = Copies(semaphores)
    parts = 2
    for part in range(parts):
        span = pl.ds(part * (toks // parts), toks // parts)
        total = total_ref[0, span]
        for above_ref in rest[:above_count]:
            total = total + above_ref[0, span].astype(F32)
        normed, scale = normalize(tokens_ref[row, span].astype(F32))
        grad_ref[span] = residual_ref[0, span] + norm_back(total * gain_ref[...], normed, scale)
        copies.start(part, grad_ref.at[span], grad_hbm.at[row, span])
    for part in range(parts):
        copies.wait(part)


def finish(after, tokens, gain, grad_residual, total, above, row, earlier):
    toks = tokens.shape[1]
    given = [] if earlier is None else [earlier]
    return kernel_call(
        functools.partial(finish_kernel, len(above), row),
        after,
        (tokens, gain, grad_residual, total, *above, *given),
        10,
        [VMEM] * (4 + len(above)) + [ANY] * len(given),
        [HBM],
        [jax.ShapeDtypeStruct(tokens.shape, F32)],
        scratch_shapes=[pltpu.VMEM((toks, D), F32), pltpu.SemaphoreType.DMA((2,))],
        input_output_aliases={4 + len(above): 0} if given else {},
        name="finish",
    )


def prefix_kernel(table_ref, lift_ref, lift_bias_ref, fan_ref, fan_bias_ref, lifted_ref, keyval_ref):
    lifted = jnp.tanh(dot(table_ref[...], lift_ref[...]) + lift_bias_ref[...])
    lifted_ref[...] = jnp.zeros_like(lifted_ref)
    lifted_ref[:PREFIX, :] = lifted
    keyval_ref[...] = jnp.zeros_like(keyval_ref)
    keyval = (dot(lifted.astype(BF16), fan_ref[...]) + fan_bias_ref[...]).astype(BF16)
    keyval_ref[0, :PREFIX, :] = keyval[:, :D]
    keyval_ref[1, :PREFIX, :] = keyval[:, D:]


def prefix_forward(after, table, lift, lift_bias, fan, fan_bias):
    return kernel_call(
        prefix_kernel,
        after,
        (table, lift, lift_bias, fan, fan_bias),
        8,
        [VMEM] * 5,
        [VMEM] * 2,
        [
            jax.ShapeDtypeStruct((PREFIX_PAD, lift.shape[1]), F32),
            jax.ShapeDtypeStruct((2, PREFIX_PAD, D), BF16),
        ],
        name="prefix_forward",
    )


def prefix_network_back_kernel(grad_ref, table_ref, lift_ref, fan_ref, lifted_ref, grad_table_ref, grad_lift_ref, grad_lift_bias_ref, grad_fan_ref, grad_fan_bias_ref):
    lifted = lifted_ref[...]
    lifted_t = jnp.concatenate([lifted.astype(BF16)] * 2, axis=0).T
    grad_lifted = None
    for half in range(2):
        cols = slice(half * D, (half + 1) * D)
        grad = grad_ref[half]
        grad_fan_bias_ref[:, cols] = jnp.sum(grad, axis=0, keepdims=True)
        both = jnp.concatenate(split(grad), axis=0)
        grad_fan_ref[:, cols] = dot(lifted_t, both)
        part = dot(both, fan_ref[:, cols], NT)
        grad_lifted = part if grad_lifted is None else grad_lifted + part
    grad_lifted = (grad_lifted[:PREFIX_PAD] + grad_lifted[PREFIX_PAD:]) * (1.0 - lifted * lifted)
    grad_lift_bias_ref[...] = jnp.sum(grad_lifted, axis=0, keepdims=True)
    both = jnp.concatenate(split(grad_lifted), axis=0)
    table = jnp.concatenate([table_ref[...].astype(F32), jnp.zeros((PREFIX_PAD - PREFIX, D), F32)], axis=0)
    table_t = jnp.concatenate([table.astype(BF16)] * 2, axis=0).T
    grad_lift_ref[...] = dot(table_t, both)
    grad_table = dot(both, lift_ref[...], NT)
    grad_table_ref[...] = (grad_table[:PREFIX_PAD] + grad_table[PREFIX_PAD:])[:PREFIX]


def prefix_network_back(after, grad, table, lift, fan, lifted):
    hidden = lift.shape[1]
    return kernel_call(
        prefix_network_back_kernel,
        after,
        (grad, table, lift, fan, lifted),
        20,
        [VMEM] * 5,
        [VMEM] * 5,
        [
            jax.ShapeDtypeStruct((PREFIX, D), F32),
            jax.ShapeDtypeStruct((D, hidden), F32),
            jax.ShapeDtypeStruct((1, hidden), F32),
            jax.ShapeDtypeStruct((hidden, 2 * D), F32),
            jax.ShapeDtypeStruct((1, 2 * D), F32),
        ],
        name="prefix_network_back",
    )


def add_kernel(left_ref, right_ref, sum_ref):
    sum_ref[...] = left_ref[...] + right_ref[...]


def add(after, left, right):
    return kernel_call(add_kernel, after, (left, right), 2, [VMEM] * 2, [VMEM], [left], name="add")


def mark_kernel(*refs):
    pass


def mark(after):
    return kernel_call(mark_kernel, after, (), 1, [], [], [], name="mark")


class Order:
    def __init__(self):
        self.before = ()

    def call(self, kernel, *operands):
        *outs, token = kernel(self.before, *operands)
        self.before = (token,)
        return outs[0] if len(outs) == 1 else outs


def sum_hops(axes):
    hops = []
    for axis in axes:
        size = lax.axis_size(axis)
        if size & (size - 1):
            return None
        hop = 1
        while hop < size:
            hops.append((axis, [(at, at ^ hop) for at in range(size)]))
            hop *= 2
    return hops


def per_device(tokens, cotangent, row_lengths, source_lengths, first_gain, first_shift, attend_weight, attend_bias, output_weight, output_bias, second_gain, second_shift, expand_weight, expand_bias, contract_weight, contract_bias, prefix_table, lift_weight, lift_bias, fan_weight, fan_bias):
    rows = tokens.shape[0]
    seq = lax.axis_size("seq")
    level_count = seq // 2
    levels = range(1, level_count)
    mates = [(at, at ^ 1) for at in range(seq)]
    place = lax.axis_index("seq").astype(jnp.int32).reshape(1)
    first_gain, first_shift, attend_bias, output_bias, second_gain, second_shift, expand_bias, contract_bias, lift_bias, fan_bias = [
        vector.reshape(1, -1)
        for vector in (first_gain, first_shift, attend_bias, output_bias, second_gain, second_shift, expand_bias, contract_bias, lift_bias, fan_bias)
    ]
    weights = (output_weight, output_bias, second_gain, second_shift, expand_weight, expand_bias, contract_weight, contract_bias)
    order = Order()
    hops = sum_hops(("seq", "dp"))
    activations = None
    input_grad = None
    prefix_grad = None
    arriving = None

    def swap(array):
        return lax.ppermute(array, "seq", mates)

    def hop():
        nonlocal prefix_grad, arriving
        if arriving is not None:
            prefix_grad = order.call(add, prefix_grad, arriving)
            arriving = None
        if hops:
            axis, pairs = hops.pop(0)
            arriving = lax.ppermute(prefix_grad, axis, pairs)

    def lower(row):
        blocks = []
        for level in levels:
            block = order.call(project_up, lower_tokens[row, level], first_gain, first_shift, attend_weight, attend_bias)
            blocks += [block, swap(block)]
        return blocks

    def keyvals_of(row, blocks):
        return [(keyval, row), (mate_keyval, row)] + [(block, 0) for block in blocks]

    row_tokens = [tokens[:1]]
    lower_tokens = {}

    def raise_tokens(row):
        for level in levels:
            pairs = [(at, at + 2 * level) for at in range(seq - 2 * level)]
            lower_tokens[row, level] = lax.ppermute(row_tokens[row], "seq", pairs)

    raise_tokens(0)
    queries, keyval, *later = order.call(project_own, tokens, first_gain, first_shift, attend_weight, attend_bias)
    row_tokens += later
    for row in range(1, rows):
        raise_tokens(row)
    mate_keyval = swap(keyval)
    lifted, prefix_keyval = order.call(prefix_forward, prefix_table, lift_weight, lift_bias, fan_weight, fan_bias)
    blocks = lower(0)
    waiting = []
    for row in range(rows):
        last_row = row + 1 == rows
        activations, grad_residual, grad_query, *grads, prefix_grad = order.call(
            row_block, place, row_lengths, source_lengths, queries, tokens, cotangent, prefix_keyval,
            keyvals_of(row, blocks), weights, row, activations, prefix_grad,
        )
        received = swap(grads[1])
        from_mates = [swap(grads[2 * level + 1]) for level in levels]
        if last_row:
            if hops is None:
                prefix_grad = lax.psum(prefix_grad, ("seq", "dp"))
            hop()
            for earlier in waiting:
                earlier()
                hop()
        else:
            blocks = lower(row + 1)
        above = []
        for level in levels:
            part = order.call(up_back, grads[2 * level], from_mates[level - 1], attend_weight)
            above.append(lax.ppermute(part, "seq", [(at + 2 * level, at) for at in range(seq - 2 * level)]))
        if last_row:
            hop()
        total = order.call(project_back, grad_query, grads[0], received, attend_weight)

        def end(row=row, grad_residual=grad_residual, total=total, above=above):
            nonlocal input_grad
            input_grad = order.call(finish, tokens, first_gain, grad_residual, total, above, row, input_grad)

        waiting.append(end)
    while hops or arriving is not None:
        hop()
        if arriving is not None:
            order.call(mark)
    grad_table, grad_lift, grad_lift_bias, grad_fan, grad_fan_bias = order.call(
        prefix_network_back, prefix_grad, prefix_table, lift_weight, fan_weight, lifted
    )
    waiting[-1]()
    return (activations, input_grad, grad_table, grad_lift, grad_lift_bias.reshape(-1), grad_fan, grad_fan_bias.reshape(-1))


def solution(mesh):
    batch = P("dp", "seq", None)
    return jax.shard_map(
        per_device,
        mesh=mesh,
        in_specs=(batch, batch, P("dp"), P("dp")) + (P(),) * 17,
        out_specs=(batch, batch, P(), P(), P(), P(), P()),
        check_vma=False,
    )
```

```python
import functools

import jax
import jax.numpy as jnp
from jax import lax
from jax.experimental import pallas as pl
from jax.experimental.pallas import tpu as pltpu
from jax.sharding import PartitionSpec as P

D = 1024
HEADS = 16
HEAD_DIM = 64
PAIRS = HEADS // 2
PREFIX = 10
PREFIX_PAD = 16
LEAST_LENGTH = 512
NN = (((1,), (0,)), ((), ()))
NT = (((1,), (1,)), ((), ()))
MIB = 1 << 20
BF16 = jnp.bfloat16
F32 = jnp.float32


def dot(left, right, dims=NN):
    return lax.dot_general(left, right, dims, preferred_element_type=F32)


ANY = pl.BlockSpec(memory_space=pl.ANY)


VMEM = pl.BlockSpec(memory_space=pltpu.VMEM)
COVER = pl.CostEstimate(flops=10**10, bytes_accessed=10**9, transcendentals=0)
TOKEN = jax.ShapeDtypeStruct((8, 128), F32)


def kernel_call(kernel, after, operands, limit, in_specs, out_specs, out_shape, prefetched=0, scratch_shapes=(), **rest):
    lead = prefetched + len(in_specs)

    def body(*refs):
        outs = lead + len(after)
        token_ref = refs[outs + len(out_shape)]
        token_ref[...] = jnp.zeros_like(token_ref)
        kernel(*refs[:lead], *refs[outs : outs + len(out_shape)], *refs[outs + len(out_shape) + 1 :])

    spec = pltpu.PrefetchScalarGridSpec(
        num_scalar_prefetch=prefetched,
        grid=(1,),
        in_specs=[*in_specs] + [ANY] * len(after),
        out_specs=[*out_specs, VMEM],
        scratch_shapes=scratch_shapes,
    )
    return pl.pallas_call(
        body,
        grid_spec=spec,
        out_shape=[*(jax.ShapeDtypeStruct(out.shape, out.dtype) for out in out_shape), TOKEN],
        compiler_params=pltpu.CompilerParams(dimension_semantics=("arbitrary",), vmem_limit_bytes=limit * MIB),
        cost_estimate=COVER,
        **rest,
    )(*operands, *after)


def split(values):
    high = values.astype(BF16)
    return high, (values - high.astype(F32)).astype(BF16)


class Copies:
    def __init__(self, semaphores):
        self.semaphores = semaphores
        self.count = 0
        self.copies = {}

    def start(self, name, source, target):
        copy = pltpu.make_async_copy(source, target, self.semaphores.at[self.count])
        copy.start()
        self.count += 1
        self.copies[name] = copy

    def wait(self, name):
        self.copies[name].wait()


HBM = pl.BlockSpec(memory_space=pltpu.HBM)


def normalize(values):
    centred = values - jnp.mean(values, axis=-1, keepdims=True)
    scale = lax.rsqrt(jnp.mean(centred * centred, axis=-1, keepdims=True) + 1e-05)
    return centred * scale, scale


def norm_back(grad, normed, scale):
    return scale * (
        grad
        - jnp.mean(grad, axis=-1, keepdims=True)
        - normed * jnp.mean(grad * normed, axis=-1, keepdims=True)
    )


def project_own_kernel(tokens_ref, gain_ref, shift_ref, bias_ref, weight_ref, query_ref, keyval_ref, *rest):
    later_refs, normed_ref = rest[:-1], rest[-1]
    rows, toks, _ = tokens_ref.shape
    for at, later_ref in enumerate(later_refs):
        later_ref[0] = tokens_ref[at + 1]
    normed, _ = normalize(tokens_ref[...].reshape(rows * toks, D).astype(F32))
    normed_ref[...] = (normed * gain_ref[...] + shift_ref[...]).astype(BF16)
    chunk = D // 2
    for at in range(6):
        span = slice(at * chunk, (at + 1) * chunk)
        result = (dot(normed_ref[...], weight_ref[:, span]) + bias_ref[:, span]).astype(BF16)
        cols = slice(at % 2 * chunk, (at % 2 + 1) * chunk)
        if at < 2:
            query_ref[:, :, cols] = (result * 0.125).reshape(rows, toks, chunk)
        else:
            keyval_ref[:, at // 2 - 1, :, cols] = result.reshape(rows, toks, chunk)


def project_own(after, tokens, gain, shift, weight, bias):
    rows, toks, _ = tokens.shape
    return kernel_call(
        project_own_kernel,
        after,
        (tokens, gain, shift, bias, weight),
        14,
        [VMEM] * 5,
        [VMEM] * (1 + rows),
        [jax.ShapeDtypeStruct((rows, toks, D), BF16), jax.ShapeDtypeStruct((rows, 2, toks, D), BF16)]
        + [jax.ShapeDtypeStruct((1, toks, D), BF16)] * (rows - 1),
        scratch_shapes=[pltpu.VMEM((rows * toks, D), BF16)],
        name="project_own",
    )


def project_up_kernel(tokens_ref, gain_ref, shift_ref, bias_ref, weight_ref, keyval_ref):
    toks = tokens_ref.shape[1]
    normed, _ = normalize(tokens_ref[0].astype(F32))
    normed = (normed * gain_ref[...] + shift_ref[...]).astype(BF16)
    for half in range(2):
        cols = slice((half + 1) * D, (half + 2) * D)
        keyval_ref[0, half] = (dot(normed, weight_ref[:, cols]) + bias_ref[:, cols]).astype(BF16)


def project_up(after, tokens, gain, shift, weight, bias):
    toks = tokens.shape[1]
    return kernel_call(
        project_up_kernel,
        after,
        (tokens, gain, shift, bias, weight),
        10,
        [VMEM] * 5,
        [VMEM],
        [jax.ShapeDtypeStruct((1, 2, toks, D), BF16)],
        name="project_up",
    )


def head_lanes(values, head):
    lanes = lax.broadcasted_iota(jnp.int32, values.shape, 1)
    keep = lanes < HEAD_DIM if head == 0 else lanes >= HEAD_DIM
    return jnp.where(keep, values, jnp.zeros_like(values))


def prefix_mask(values, fill):
    places = lax.broadcasted_iota(jnp.int32, values.shape, 0)
    return jnp.where(places < PREFIX, values, fill)


class Places:
    def __init__(self, toks, level_count):
        self.toks = toks
        self.level_count = level_count

    def masked(self, block):
        if block < 2:
            return True
        level = block // 2
        return (self.level_count - level) * 2 * self.toks > LEAST_LENGTH

    def limits(self, place, length):
        base = place * self.toks
        queries = base + lax.broadcasted_iota(jnp.int32, (1, self.toks), 1)
        return jnp.minimum(queries, length - 1)

    def visible(self, block, place, limit):
        if block == 0:
            base = place * self.toks
        else:
            base = (lax.bitwise_xor(place, block % 2) - (block // 2) * 2) * self.toks
        keys = lax.broadcasted_iota(jnp.int32, (self.toks, self.toks), 0)
        return keys <= limit - base


def spread_prefix(prefix):
    tiled = jnp.concatenate([prefix] * HEADS, axis=0)
    rows = lax.broadcasted_iota(jnp.int32, tiled.shape, 0) // PREFIX_PAD
    cols = lax.broadcasted_iota(jnp.int32, tiled.shape, 1) // HEAD_DIM
    return jnp.where(rows == cols, tiled, jnp.zeros_like(tiled))


GELU_SCALE = 0.7978845608028654
GELU_CUBE = 0.044715
FAR = 1e30
ROW_LIMIT = 32


class RowRefs:
    def __init__(self, names, refs):
        for name, ref in zip(names, refs):
            setattr(self, name, ref)


def column_group(group, width):
    return pl.ds(pl.multiple_of(group * width, width), width)


def attend_rows(places, refs, place, limit, pair_step):
    blocks = range(2 * places.level_count)
    masked_blocks = [block for block in blocks if places.masked(block)]
    level = place // 2
    width = 128 * pair_step
    refs.prefix_scores[...] = dot(refs.spread[0], refs.query[...], NT)
    for at, block in enumerate(masked_blocks):
        refs.hide[at] = jnp.where(places.visible(block, place, limit), 0.0, -jnp.inf)

    def beyond(block):
        return jnp.where(level >= block // 2, 0.0, FAR) if block > 1 else None

    def body(group, carry):
        span = column_group(group, width)
        group_queries = refs.query[:, span]
        group_keys = [refs.keyval(block, 0, span) for block in blocks]

        def scores_of(at):
            pair, head = at // 2, at % 2
            cols = slice(pair * 128, (pair + 1) * 128)
            queries = head_lanes(group_queries[:, cols], head)
            spot = pl.multiple_of((group * pair_step * 2 + at) * PREFIX_PAD, PREFIX_PAD)
            prefix_scores = prefix_mask(refs.prefix_scores[pl.ds(spot, PREFIX_PAD), :], -jnp.inf)
            highest = jnp.max(prefix_scores, axis=0, keepdims=True)
            scores = []
            for block in blocks:
                part = dot(group_keys[block][:, cols], queries, NT)
                if block in masked_blocks:
                    part = part + refs.hide[masked_blocks.index(block)]
                top = jnp.max(part, axis=0, keepdims=True)
                if block > 1:
                    top = top - beyond(block)
                highest = jnp.maximum(highest, top)
                scores.append(part)
            return prefix_scores, scores, highest

        ahead = scores_of(0)
        for at in range(2 * pair_step):
            pair, head = at // 2, at % 2
            cols = slice(pair * 128, (pair + 1) * 128)
            prefix_scores, scores, highest = ahead
            if at + 1 < 2 * pair_step:
                ahead = scores_of(at + 1)
            if head == 0:
                values_t = [refs.keyval(block, 1, span)[:, cols].T for block in blocks]
                prefix_values_t = refs.prefix[1, :, span][:, cols].T
                outs = []
            rows = slice(head * HEAD_DIM, (head + 1) * HEAD_DIM)
            prefix_weights = jnp.exp(prefix_scores - highest)
            total = jnp.sum(prefix_weights, axis=0, keepdims=True)
            mixed = dot(prefix_values_t[rows], prefix_weights.astype(BF16))
            for block in blocks:
                base = highest + beyond(block) if block > 1 else highest
                weights = jnp.exp(scores[block] - base)
                total = total + jnp.sum(weights, axis=0, keepdims=True)
                mixed = mixed + dot(values_t[block][rows], weights.astype(BF16))
            outs.append(mixed * (1.0 / total))
            refs.total[group, at : at + 1, :] = highest + jnp.log(total)
            if head == 1:
                refs.mixed[:, pl.ds(pl.multiple_of(group * width + pair * 128, 128), 128)] = jnp.concatenate(outs, axis=0).T.astype(BF16)
        return carry

    lax.fori_loop(0, PAIRS // pair_step, body, 0)


def feed_rows(refs, place, length, source, weight_copies, chunks, chunk, slots):
    toks = refs.tokens.shape[0]
    spots = place * toks + lax.broadcasted_iota(jnp.int32, (toks, D), 0)
    target = (spots >= source) & (spots < length)
    refs.grad_out[...] = jnp.where(target, refs.cotangent[...].astype(F32), 0.0).astype(BF16)
    residual = refs.tokens[...].astype(F32) + dot(refs.mixed[...], refs.output_weight[...]) + refs.output_bias[...]
    refs.residual[...] = residual
    normed, _ = normalize(residual)
    refs.normed[...] = (normed * refs.second_gain[...] + refs.second_shift[...]).astype(BF16)

    def first(at, slot):
        for copy in weight_copies(at):
            copy.wait()
        bias = refs.expand_bias[:, pl.ds(pl.multiple_of(at * chunk, chunk), chunk)]
        values = dot(refs.normed[...], refs.expand_weight[at % slots]) + bias
        grad_hidden = dot(refs.grad_out[...], refs.contract_weight[at % slots], NT)
        square = values * values
        bend = jnp.tanh(values * (GELU_SCALE + GELU_SCALE * GELU_CUBE * square))
        half = 0.5 + 0.5 * bend
        slope = half + (0.5 * values) * (1.0 - bend * bend) * (
            GELU_SCALE + 3.0 * GELU_SCALE * GELU_CUBE * square
        )
        refs.active[slot] = (values * half).astype(BF16)
        refs.grad_expand[slot] = (grad_hidden * slope).astype(BF16)

    def second(at, slot):
        refs.result[...] += dot(refs.active[slot], refs.contract_weight[at % slots])
        refs.grad_normed[...] += dot(refs.grad_expand[slot], refs.expand_weight[at % slots], NT)

    def refill(at):
        @pl.when(at + slots < chunks)
        def _():
            for copy in weight_copies(at + slots):
                copy.start()

    refs.result[...] = jnp.zeros_like(refs.result)
    refs.grad_normed[...] = jnp.zeros_like(refs.grad_normed)
    first(0, 0)

    def body(at, carry):
        first(2 * at + 1, 1)
        second(2 * at, 0)
        refill(2 * at)
        first(2 * at + 2, 0)
        second(2 * at + 1, 1)
        refill(2 * at + 1)
        return carry

    lax.fori_loop(0, chunks // 2 - 1, body, 0)
    first(chunks - 1, 1)
    second(chunks - 2, 0)
    second(chunks - 1, 1)

    residual = refs.residual[...]
    refs.activations[...] = (residual + refs.result[...] + refs.contract_bias[...]).astype(BF16)
    normed, scale = normalize(residual)
    grad = refs.grad_out[...].astype(F32) + norm_back(refs.grad_normed[...] * refs.second_gain[...], normed, scale)
    refs.grad_residual[0] = grad
    refs.grad_heads[...] = dot(grad.astype(BF16), refs.output_weight[...], NT).astype(BF16)


def prefix_back_rows(refs):
    toks = refs.query.shape[0]
    queries = refs.query[...]
    grads = refs.grad_heads[...]
    product = grads.astype(F32) * refs.mixed[...].astype(F32)
    head_of = lax.broadcasted_iota(jnp.int32, (HEADS, D), 1) // HEAD_DIM
    chosen = jnp.where(head_of == lax.broadcasted_iota(jnp.int32, (HEADS, D), 0), 1.0, 0.0).astype(BF16)
    high, low = split(product)
    inner = dot(chosen, high, NT) + dot(chosen, low, NT)
    refs.inner[...] = inner.reshape(refs.inner.shape)

    def per_head(values):
        return values.reshape(HEADS, PREFIX_PAD, toks)

    scores = per_head(refs.prefix_scores[...])
    grad_weights = per_head(dot(refs.spread[1], grads, NT))
    weights = jnp.exp(scores - refs.total[...].reshape(HEADS, 1, toks))
    valid = lax.broadcasted_iota(jnp.int32, weights.shape, 1) < PREFIX
    weights = jnp.where(valid, weights, 0.0)
    grad_scores = weights * (grad_weights - inner[:, None, :])
    weights = weights.reshape(HEADS * PREFIX_PAD, toks).astype(BF16)
    grad_scores = grad_scores.reshape(HEADS * PREFIX_PAD, toks).astype(BF16)
    refs.result[...] = dot(grad_scores.T, refs.spread[0])
    own = (
        lax.broadcasted_iota(jnp.int32, (HEADS * PREFIX_PAD, D), 0) // PREFIX_PAD
        == lax.broadcasted_iota(jnp.int32, (HEADS * PREFIX_PAD, D), 1) // HEAD_DIM
    )

    def gather(values):
        return jnp.sum(jnp.where(own, values, 0.0).reshape(HEADS, PREFIX_PAD, D), axis=0)

    sums = gather(dot(grad_scores, queries)), gather(dot(weights, grads))
    for half in range(2):
        refs.prefix_grad[half] = sums[half] if refs.earlier_grad is None else sums[half] + refs.earlier_grad[half]


def attend_back_rows(places, refs, place, pair_step):
    blocks = range(2 * places.level_count)
    masked_blocks = [block for block in blocks if places.masked(block)]
    level = place // 2
    width = 128 * pair_step

    def body(group, carry):
        span = column_group(group, width)
        group_queries = refs.query[:, span]
        group_grads = refs.grad_heads[:, span]
        group_keys = [refs.keyval(block, 0, span) for block in blocks]
        group_values = [refs.keyval(block, 1, span) for block in blocks]

        def products_of(at):
            pair, head = at // 2, at % 2
            cols = slice(pair * 128, (pair + 1) * 128)
            queries = head_lanes(group_queries[:, cols], head)
            grads = head_lanes(group_grads[:, cols], head)
            scores, grad_weights = [], []
            for block in blocks:
                part = dot(group_keys[block][:, cols], queries, NT)
                if block in masked_blocks:
                    part = part + refs.hide[masked_blocks.index(block)]
                scores.append(part)
                grad_weights.append(dot(group_values[block][:, cols], grads, NT))
            return queries, grads, scores, grad_weights

        ahead = products_of(0)
        for at in range(2 * pair_step):
            pair, head = at // 2, at % 2
            cols = slice(pair * 128, (pair + 1) * 128)
            place_cols = pl.ds(pl.multiple_of(group * width + pair * 128, 128), 128)
            queries, grads, scores, grad_weights = ahead
            if at + 1 < 2 * pair_step:
                ahead = products_of(at + 1)
            if head == 0:
                keys_t = [keys[:, cols].T for keys in group_keys]
                grad_keys, grad_values, outs = [], [], []
            total = refs.total[group, at : at + 1, :]
            inner = refs.inner[group, at : at + 1, :]
            rows = slice(head * HEAD_DIM, (head + 1) * HEAD_DIM)
            grad_query = None
            for block in blocks:
                base = total + jnp.where(level >= block // 2, 0.0, FAR) if block > 1 else total
                weights = jnp.exp(scores[block] - base)
                grad_scores = (weights * (grad_weights[block] - inner)).astype(BF16)
                part_values = dot(weights.astype(BF16), grads)
                part_keys = dot(grad_scores, queries)
                part_query = dot(keys_t[block][rows], grad_scores)
                if head == 0:
                    grad_values.append(part_values)
                    grad_keys.append(part_keys)
                else:
                    refs.grad_keyval[block][0, 0, :, place_cols] = (grad_keys[block] + part_keys).astype(BF16)
                    refs.grad_keyval[block][0, 1, :, place_cols] = (grad_values[block] + part_values).astype(BF16)
                grad_query = part_query if grad_query is None else grad_query + part_query
            outs.append(grad_query)
            if head == 1:
                grad_query = jnp.concatenate(outs, axis=0).T + refs.result[:, place_cols]
                refs.grad_query[0, :, place_cols] = (grad_query * 0.125).astype(BF16)
        return carry

    lax.fori_loop(0, PAIRS // pair_step, body, 0)


ROW_NAMES = (
    "expand_weight", "contract_weight", "spread", "prefix_scores", "hide", "total",
    "mixed", "grad_out", "residual", "normed", "active", "grad_expand", "result", "grad_normed", "activations",
    "grad_heads", "inner",
)


def row_kernel(places, row, keyval_rows, pair_step, chunk, has_earlier, place_ref, length_ref, source_ref, *rest):
    block_count = 2 * places.level_count
    query_ref, tokens_ref, cotangent_ref, prefix_ref = rest[:4]
    keyval_refs = rest[4 : 4 + block_count]
    rest = rest[4 + block_count :]
    output_weight_ref, expand_weight_hbm, contract_weight_hbm = rest[:3]
    vectors = rest[3:8]
    earlier_grad_ref = rest[8] if has_earlier else None
    rest = rest[8 + 2 * has_earlier :]
    activations_hbm, grad_residual_ref, grad_query_ref = rest[:3]
    grad_keyval_refs = rest[3 : 3 + block_count]
    prefix_grad_ref = rest[3 + block_count]
    rest = rest[4 + block_count :]
    refs = RowRefs(ROW_NAMES, rest)
    refs.output_bias, refs.second_gain, refs.second_shift, refs.expand_bias, refs.contract_bias = vectors
    refs.prefix_grad, refs.earlier_grad = prefix_grad_ref, earlier_grad_ref
    refs.query, refs.prefix = query_ref.at[row], prefix_ref
    refs.keyval = lambda block, half, span: keyval_refs[block][keyval_rows[block], half, :, span]
    refs.grad_residual, refs.grad_query, refs.grad_keyval = grad_residual_ref, grad_query_ref, grad_keyval_refs
    semaphores, weight_semaphores = rest[len(ROW_NAMES) :]
    slots = refs.expand_weight.shape[0]
    chunks = expand_weight_hbm.shape[1] // chunk

    copies = Copies(semaphores)
    refs.output_weight, refs.tokens, refs.cotangent = output_weight_ref, tokens_ref.at[row], cotangent_ref.at[row]

    def weight_copies(at):
        span = pl.ds(pl.multiple_of(at * chunk, chunk), chunk)
        return (
            pltpu.make_async_copy(expand_weight_hbm.at[:, span], refs.expand_weight.at[at % slots], weight_semaphores.at[at]),
            pltpu.make_async_copy(contract_weight_hbm.at[span, :], refs.contract_weight.at[at % slots], weight_semaphores.at[chunks + at]),
        )

    def start_weights(at, carry):
        for copy in weight_copies(at):
            copy.start()
        return carry

    lax.fori_loop(0, slots, start_weights, 0)
    place = place_ref[0]
    length = length_ref[row]
    limit = places.limits(place, length)
    for half in range(2):
        refs.spread[half] = spread_prefix(refs.prefix[half])
    attend_rows(places, refs, place, limit, pair_step)
    feed_rows(refs, place, length, source_ref[row], weight_copies, chunks, chunk, slots)
    copies.start("activations", refs.activations, activations_hbm.at[row])
    prefix_back_rows(refs)
    attend_back_rows(places, refs, place, pair_step)
    copies.wait("activations")


def row_block(after, place, lengths, sources, queries, tokens, cotangent, prefix_keyval, keyvals, weights, row, earlier, earlier_grad, pair_step=4, chunk=512, slots=4):
    toks = queries.shape[1]
    block_count = len(keyvals)
    places = Places(toks, block_count // 2)
    output_weight, output_bias, gain, shift, expand_weight, expand_bias, contract_weight, contract_bias = weights
    hidden = expand_weight.shape[1]
    chunks = hidden // chunk
    given = [] if earlier is None else [earlier_grad, earlier]
    masked = sum(places.masked(block) for block in range(block_count))
    per_group = 2 * pair_step
    scratch = dict(
        expand_weight=((slots, D, chunk), BF16), contract_weight=((slots, chunk, D), BF16),
        spread=((2, HEADS * PREFIX_PAD, D), BF16), prefix_scores=((HEADS * PREFIX_PAD, toks), F32),
        hide=((masked, toks, toks), F32), total=((HEADS // per_group, per_group, toks), F32), mixed=((toks, D), BF16),
        grad_out=((toks, D), BF16), residual=((toks, D), F32), normed=((toks, D), BF16),
        active=((2, toks, chunk), BF16), grad_expand=((2, toks, chunk), BF16), result=((toks, D), F32),
        grad_normed=((toks, D), F32), activations=((toks, D), BF16),
        grad_heads=((toks, D), BF16), inner=((HEADS // per_group, per_group, toks), F32),
    )
    return kernel_call(
        functools.partial(row_kernel, places, row, [at for _, at in keyvals], pair_step, chunk, earlier is not None),
        after,
        (
            place, lengths, sources, queries, tokens, cotangent, prefix_keyval, *[array for array, _ in keyvals],
            output_weight, expand_weight, contract_weight, output_bias, gain, shift, expand_bias, contract_bias, *given,
        ),
        ROW_LIMIT,
        [VMEM] * (4 + block_count) + [VMEM, HBM, HBM] + [VMEM] * 5 + [VMEM, ANY][: len(given)],
        [HBM] + [VMEM] * (3 + block_count),
        [
            jax.ShapeDtypeStruct(tokens.shape, BF16),
            jax.ShapeDtypeStruct((1, toks, D), F32),
            jax.ShapeDtypeStruct((1, toks, D), BF16),
        ]
        + [jax.ShapeDtypeStruct((1, 2, toks, D), BF16)] * block_count
        + [jax.ShapeDtypeStruct((2, PREFIX_PAD, D), F32)],
        prefetched=3,
        scratch_shapes=[pltpu.VMEM(*scratch[name]) for name in ROW_NAMES]
        + [pltpu.SemaphoreType.DMA((1,)), pltpu.SemaphoreType.DMA((2 * chunks,))],
        input_output_aliases={16 + block_count: 0} if given else {},
        name="row_block",
    )


def up_back_kernel(own_ref, received_ref, weight_ref, grad_ref):
    total = None
    for half in range(2):
        values = (own_ref[0, half].astype(F32) + received_ref[0, half].astype(F32)).astype(BF16)
        part = dot(values, weight_ref[:, (half + 1) * D : (half + 2) * D], NT)
        total = part if total is None else total + part
    grad_ref[0] = total.astype(BF16)


def up_back(after, own, received, weight):
    toks = own.shape[2]
    return kernel_call(
        up_back_kernel,
        after,
        (own, received, weight),
        10,
        [VMEM] * 3,
        [VMEM],
        [jax.ShapeDtypeStruct((1, toks, D), BF16)],
        name="up_back",
    )


def project_back_kernel(query_ref, own_ref, received_ref, weight_ref, total_ref):
    total = dot(query_ref[0], weight_ref[:, :D], NT)
    for half in range(2):
        values = (own_ref[0, half].astype(F32) + received_ref[0, half].astype(F32)).astype(BF16)
        total = total + dot(values, weight_ref[:, (half + 1) * D : (half + 2) * D], NT)
    total_ref[0] = total


def project_back(after, grad_query, own, received, weight):
    toks = grad_query.shape[1]
    return kernel_call(
        project_back_kernel,
        after,
        (grad_query, own, received, weight),
        10,
        [VMEM] * 4,
        [VMEM],
        [jax.ShapeDtypeStruct((1, toks, D), F32)],
        name="project_back",
    )


def finish_kernel(above_count, row, tokens_ref, gain_ref, residual_ref, total_ref, *rest):
    grad_hbm, grad_ref, semaphores = rest[-3:]
    toks = grad_ref.shape[0]
    copies = Copies(semaphores)
    parts = 2
    for part in range(parts):
        span = pl.ds(part * (toks // parts), toks // parts)
        total = total_ref[0, span]
        for above_ref in rest[:above_count]:
            total = total + above_ref[0, span].astype(F32)
        normed, scale = normalize(tokens_ref[row, span].astype(F32))
        grad_ref[span] = residual_ref[0, span] + norm_back(total * gain_ref[...], normed, scale)
        copies.start(part, grad_ref.at[span], grad_hbm.at[row, span])
    for part in range(parts):
        copies.wait(part)


def finish(after, tokens, gain, grad_residual, total, above, row, earlier):
    toks = tokens.shape[1]
    given = [] if earlier is None else [earlier]
    return kernel_call(
        functools.partial(finish_kernel, len(above), row),
        after,
        (tokens, gain, grad_residual, total, *above, *given),
        10,
        [VMEM] * (4 + len(above)) + [ANY] * len(given),
        [HBM],
        [jax.ShapeDtypeStruct(tokens.shape, F32)],
        scratch_shapes=[pltpu.VMEM((toks, D), F32), pltpu.SemaphoreType.DMA((2,))],
        input_output_aliases={4 + len(above): 0} if given else {},
        name="finish",
    )


def prefix_kernel(table_ref, lift_ref, lift_bias_ref, fan_ref, fan_bias_ref, lifted_ref, keyval_ref):
    lifted = jnp.tanh(dot(table_ref[...], lift_ref[...]) + lift_bias_ref[...])
    lifted_ref[...] = jnp.zeros_like(lifted_ref)
    lifted_ref[:PREFIX, :] = lifted
    keyval_ref[...] = jnp.zeros_like(keyval_ref)
    keyval = (dot(lifted.astype(BF16), fan_ref[...]) + fan_bias_ref[...]).astype(BF16)
    keyval_ref[0, :PREFIX, :] = keyval[:, :D]
    keyval_ref[1, :PREFIX, :] = keyval[:, D:]


def prefix_forward(after, table, lift, lift_bias, fan, fan_bias):
    return kernel_call(
        prefix_kernel,
        after,
        (table, lift, lift_bias, fan, fan_bias),
        8,
        [VMEM] * 5,
        [VMEM] * 2,
        [
            jax.ShapeDtypeStruct((PREFIX_PAD, lift.shape[1]), F32),
            jax.ShapeDtypeStruct((2, PREFIX_PAD, D), BF16),
        ],
        name="prefix_forward",
    )


def prefix_network_back_kernel(grad_ref, table_ref, lift_ref, fan_ref, lifted_ref, grad_table_ref, grad_lift_ref, grad_lift_bias_ref, grad_fan_ref, grad_fan_bias_ref):
    lifted = lifted_ref[...]
    lifted_t = jnp.concatenate([lifted.astype(BF16)] * 2, axis=0).T
    grad_lifted = None
    for half in range(2):
        cols = slice(half * D, (half + 1) * D)
        grad = grad_ref[half]
        grad_fan_bias_ref[:, cols] = jnp.sum(grad, axis=0, keepdims=True)
        both = jnp.concatenate(split(grad), axis=0)
        grad_fan_ref[:, cols] = dot(lifted_t, both)
        part = dot(both, fan_ref[:, cols], NT)
        grad_lifted = part if grad_lifted is None else grad_lifted + part
    grad_lifted = (grad_lifted[:PREFIX_PAD] + grad_lifted[PREFIX_PAD:]) * (1.0 - lifted * lifted)
    grad_lift_bias_ref[...] = jnp.sum(grad_lifted, axis=0, keepdims=True)
    both = jnp.concatenate(split(grad_lifted), axis=0)
    table = jnp.concatenate([table_ref[...].astype(F32), jnp.zeros((PREFIX_PAD - PREFIX, D), F32)], axis=0)
    table_t = jnp.concatenate([table.astype(BF16)] * 2, axis=0).T
    grad_lift_ref[...] = dot(table_t, both)
    grad_table = dot(both, lift_ref[...], NT)
    grad_table_ref[...] = (grad_table[:PREFIX_PAD] + grad_table[PREFIX_PAD:])[:PREFIX]


def prefix_network_back(after, grad, table, lift, fan, lifted):
    hidden = lift.shape[1]
    return kernel_call(
        prefix_network_back_kernel,
        after,
        (grad, table, lift, fan, lifted),
        20,
        [VMEM] * 5,
        [VMEM] * 5,
        [
            jax.ShapeDtypeStruct((PREFIX, D), F32),
            jax.ShapeDtypeStruct((D, hidden), F32),
            jax.ShapeDtypeStruct((1, hidden), F32),
            jax.ShapeDtypeStruct((hidden, 2 * D), F32),
            jax.ShapeDtypeStruct((1, 2 * D), F32),
        ],
        name="prefix_network_back",
    )


def add_kernel(left_ref, right_ref, sum_ref):
    sum_ref[...] = left_ref[...] + right_ref[...]


def add(after, left, right):
    return kernel_call(add_kernel, after, (left, right), 2, [VMEM] * 2, [VMEM], [left], name="add")


def mark_kernel(*refs):
    pass


def mark(after):
    return kernel_call(mark_kernel, after, (), 1, [], [], [], name="mark")


class Order:
    def __init__(self):
        self.before = ()

    def call(self, kernel, *operands):
        *outs, token = kernel(self.before, *operands)
        self.before = (token,)
        return outs[0] if len(outs) == 1 else outs


def sum_hops(axes):
    hops = []
    for axis in axes:
        size = lax.axis_size(axis)
        if size & (size - 1):
            return None
        hop = 1
        while hop < size:
            hops.append((axis, [(at, at ^ hop) for at in range(size)]))
            hop *= 2
    return hops


def per_device(tokens, cotangent, row_lengths, source_lengths, first_gain, first_shift, attend_weight, attend_bias, output_weight, output_bias, second_gain, second_shift, expand_weight, expand_bias, contract_weight, contract_bias, prefix_table, lift_weight, lift_bias, fan_weight, fan_bias):
    rows = tokens.shape[0]
    seq = lax.axis_size("seq")
    level_count = seq // 2
    levels = range(1, level_count)
    mates = [(at, at ^ 1) for at in range(seq)]
    place = lax.axis_index("seq").astype(jnp.int32).reshape(1)
    first_gain, first_shift, attend_bias, output_bias, second_gain, second_shift, expand_bias, contract_bias, lift_bias, fan_bias = [
        vector.reshape(1, -1)
        for vector in (first_gain, first_shift, attend_bias, output_bias, second_gain, second_shift, expand_bias, contract_bias, lift_bias, fan_bias)
    ]
    weights = (output_weight, output_bias, second_gain, second_shift, expand_weight, expand_bias, contract_weight, contract_bias)
    order = Order()
    hops = sum_hops(("seq", "dp"))
    activations = None
    input_grad = None
    prefix_grad = None
    arriving = None

    def swap(array):
        return lax.ppermute(array, "seq", mates)

    def hop():
        nonlocal prefix_grad, arriving
        if arriving is not None:
            prefix_grad = order.call(add, prefix_grad, arriving)
            arriving = None
        if hops:
            axis, pairs = hops.pop(0)
            arriving = lax.ppermute(prefix_grad, axis, pairs)

    def lower(row):
        blocks = []
        for level in levels:
            block = order.call(project_up, lower_tokens[row, level], first_gain, first_shift, attend_weight, attend_bias)
            blocks += [block, swap(block)]
        return blocks

    def keyvals_of(row, blocks):
        return [(keyval, row), (mate_keyval, row)] + [(block, 0) for block in blocks]

    row_tokens = [tokens[:1]]
    lower_tokens = {}

    def raise_tokens(row):
        for level in levels:
            pairs = [(at, at + 2 * level) for at in range(seq - 2 * level)]
            lower_tokens[row, level] = lax.ppermute(row_tokens[row], "seq", pairs)

    raise_tokens(0)
    queries, keyval, *later = order.call(project_own, tokens, first_gain, first_shift, attend_weight, attend_bias)
    row_tokens += later
    for row in range(1, rows):
        raise_tokens(row)
    mate_keyval = swap(keyval)
    lifted, prefix_keyval = order.call(prefix_forward, prefix_table, lift_weight, lift_bias, fan_weight, fan_bias)
    blocks = lower(0)
    waiting = []
    for row in range(rows):
        last_row = row + 1 == rows
        activations, grad_residual, grad_query, *grads, prefix_grad = order.call(
            row_block, place, row_lengths, source_lengths, queries, tokens, cotangent, prefix_keyval,
            keyvals_of(row, blocks), weights, row, activations, prefix_grad,
        )
        received = swap(grads[1])
        from_mates = [swap(grads[2 * level + 1]) for level in levels]
        if last_row:
            if hops is None:
                prefix_grad = lax.psum(prefix_grad, ("seq", "dp"))
            hop()
            for earlier in waiting:
                earlier()
                hop()
        else:
            blocks = lower(row + 1)
        above = []
        for level in levels:
            part = order.call(up_back, grads[2 * level], from_mates[level - 1], attend_weight)
            above.append(lax.ppermute(part, "seq", [(at + 2 * level, at) for at in range(seq - 2 * level)]))
        if last_row:
            hop()
        total = order.call(project_back, grad_query, grads[0], received, attend_weight)

        def end(row=row, grad_residual=grad_residual, total=total, above=above):
            nonlocal input_grad
            input_grad = order.call(finish, tokens, first_gain, grad_residual, total, above, row, input_grad)

        waiting.append(end)
    while hops or arriving is not None:
        hop()
        if arriving is not None:
            order.call(mark)
    grad_table, grad_lift, grad_lift_bias, grad_fan, grad_fan_bias = order.call(
        prefix_network_back, prefix_grad, prefix_table, lift_weight, fan_weight, lifted
    )
    waiting[-1]()
    return (activations, input_grad, grad_table, grad_lift, grad_lift_bias.reshape(-1), grad_fan, grad_fan_bias.reshape(-1))


def solution(mesh):
    batch = P("dp", "seq", None)
    return jax.shard_map(
        per_device,
        mesh=mesh,
        in_specs=(batch, batch, P("dp"), P("dp")) + (P(),) * 17,
        out_specs=(batch, batch, P(), P(), P(), P(), P()),
        check_vma=False,
    )
```

```python
import functools

import jax
import jax.numpy as jnp
from jax import lax
from jax.experimental import pallas as pl
from jax.experimental.pallas import tpu as pltpu
from jax.sharding import PartitionSpec as P

D = 1024
HEADS = 16
HEAD_DIM = 64
PAIRS = HEADS // 2
PREFIX = 10
PREFIX_PAD = 16
LEAST_LENGTH = 512
NN = (((1,), (0,)), ((), ()))
NT = (((1,), (1,)), ((), ()))
MIB = 1 << 20
BF16 = jnp.bfloat16
F32 = jnp.float32


def dot(left, right, dims=NN):
    return lax.dot_general(left, right, dims, preferred_element_type=F32)


ANY = pl.BlockSpec(memory_space=pl.ANY)


VMEM = pl.BlockSpec(memory_space=pltpu.VMEM)
COVER = pl.CostEstimate(flops=10**10, bytes_accessed=10**9, transcendentals=0)
TOKEN = jax.ShapeDtypeStruct((8, 128), F32)


def kernel_call(kernel, after, operands, limit, in_specs, out_specs, out_shape, prefetched=0, scratch_shapes=(), warm=(), **rest):
    lead = prefetched + len(in_specs)

    def body(*refs):
        outs = lead + len(after) + len(warm)
        token_ref = refs[outs + len(out_shape)]
        token_ref[...] = jnp.zeros_like(token_ref)
        kernel(*refs[:lead], *refs[outs : outs + len(out_shape)], *refs[outs + len(out_shape) + 1 :])

    spec = pltpu.PrefetchScalarGridSpec(
        num_scalar_prefetch=prefetched,
        grid=(1,),
        in_specs=[*in_specs] + [ANY] * len(after) + [VMEM] * len(warm),
        out_specs=[*out_specs, VMEM],
        scratch_shapes=scratch_shapes,
    )
    return pl.pallas_call(
        body,
        grid_spec=spec,
        out_shape=[*(jax.ShapeDtypeStruct(out.shape, out.dtype) for out in out_shape), TOKEN],
        compiler_params=pltpu.CompilerParams(dimension_semantics=("arbitrary",), vmem_limit_bytes=limit * MIB),
        cost_estimate=COVER,
        **rest,
    )(*operands, *after, *warm)


def split(values):
    high = values.astype(BF16)
    return high, (values - high.astype(F32)).astype(BF16)


class Copies:
    def __init__(self, semaphores):
        self.semaphores = semaphores
        self.count = 0
        self.copies = {}

    def start(self, name, source, target):
        copy = pltpu.make_async_copy(source, target, self.semaphores.at[self.count])
        copy.start()
        self.count += 1
        self.copies[name] = copy

    def wait(self, name):
        self.copies[name].wait()


HBM = pl.BlockSpec(memory_space=pltpu.HBM)


def normalize(values):
    centred = values - jnp.mean(values, axis=-1, keepdims=True)
    scale = lax.rsqrt(jnp.mean(centred * centred, axis=-1, keepdims=True) + 1e-05)
    return centred * scale, scale


def norm_back(grad, normed, scale):
    return scale * (
        grad
        - jnp.mean(grad, axis=-1, keepdims=True)
        - normed * jnp.mean(grad * normed, axis=-1, keepdims=True)
    )


def project_own_kernel(tokens_ref, gain_ref, shift_ref, bias_ref, weight_ref, query_ref, keyval_ref, *rest):
    later_refs, normed_ref = rest[:-1], rest[-1]
    rows, toks, _ = tokens_ref.shape
    for at, later_ref in enumerate(later_refs):
        later_ref[0] = tokens_ref[at + 1]
    normed, _ = normalize(tokens_ref[...].reshape(rows * toks, D).astype(F32))
    normed_ref[...] = (normed * gain_ref[...] + shift_ref[...]).astype(BF16)
    chunk = D // 2
    for at in range(6):
        span = slice(at * chunk, (at + 1) * chunk)
        result = (dot(normed_ref[...], weight_ref[:, span]) + bias_ref[:, span]).astype(BF16)
        cols = slice(at % 2 * chunk, (at % 2 + 1) * chunk)
        if at < 2:
            query_ref[:, :, cols] = (result * 0.125).reshape(rows, toks, chunk)
        else:
            keyval_ref[:, at // 2 - 1, :, cols] = result.reshape(rows, toks, chunk)


def project_own(after, tokens, gain, shift, weight, bias):
    rows, toks, _ = tokens.shape
    return kernel_call(
        project_own_kernel,
        after,
        (tokens, gain, shift, bias, weight),
        14,
        [VMEM] * 5,
        [VMEM] * (1 + rows),
        [jax.ShapeDtypeStruct((rows, toks, D), BF16), jax.ShapeDtypeStruct((rows, 2, toks, D), BF16)]
        + [jax.ShapeDtypeStruct((1, toks, D), BF16)] * (rows - 1),
        scratch_shapes=[pltpu.VMEM((rows * toks, D), BF16)],
        name="project_own",
    )


def project_up_kernel(tokens_ref, gain_ref, shift_ref, bias_ref, weight_ref, keyval_ref):
    toks = tokens_ref.shape[1]
    normed, _ = normalize(tokens_ref[0].astype(F32))
    normed = (normed * gain_ref[...] + shift_ref[...]).astype(BF16)
    for half in range(2):
        cols = slice((half + 1) * D, (half + 2) * D)
        keyval_ref[0, half] = (dot(normed, weight_ref[:, cols]) + bias_ref[:, cols]).astype(BF16)


def project_up(after, tokens, gain, shift, weight, bias, warm=()):
    toks = tokens.shape[1]
    return kernel_call(
        project_up_kernel,
        after,
        (tokens, gain, shift, bias, weight),
        10,
        [VMEM] * 5,
        [VMEM],
        [jax.ShapeDtypeStruct((1, 2, toks, D), BF16)],
        warm=warm,
        name="project_up",
    )


def head_lanes(values, head):
    lanes = lax.broadcasted_iota(jnp.int32, values.shape, 1)
    keep = lanes < HEAD_DIM if head == 0 else lanes >= HEAD_DIM
    return jnp.where(keep, values, jnp.zeros_like(values))


def prefix_mask(values, fill):
    places = lax.broadcasted_iota(jnp.int32, values.shape, 0)
    return jnp.where(places < PREFIX, values, fill)


class Places:
    def __init__(self, toks, level_count):
        self.toks = toks
        self.level_count = level_count

    def masked(self, block):
        if block < 2:
            return True
        level = block // 2
        return (self.level_count - level) * 2 * self.toks > LEAST_LENGTH

    def limits(self, place, length):
        base = place * self.toks
        queries = base + lax.broadcasted_iota(jnp.int32, (1, self.toks), 1)
        return jnp.minimum(queries, length - 1)

    def visible(self, block, place, limit):
        if block == 0:
            base = place * self.toks
        else:
            base = (lax.bitwise_xor(place, block % 2) - (block // 2) * 2) * self.toks
        keys = lax.broadcasted_iota(jnp.int32, (self.toks, self.toks), 0)
        return keys <= limit - base


def spread_prefix(prefix):
    tiled = jnp.concatenate([prefix] * HEADS, axis=0)
    rows = lax.broadcasted_iota(jnp.int32, tiled.shape, 0) // PREFIX_PAD
    cols = lax.broadcasted_iota(jnp.int32, tiled.shape, 1) // HEAD_DIM
    return jnp.where(rows == cols, tiled, jnp.zeros_like(tiled))


GELU_SCALE = 0.7978845608028654
GELU_CUBE = 0.044715
FAR = 1e30
ROW_LIMIT = 30


class RowRefs:
    def __init__(self, names, refs):
        for name, ref in zip(names, refs):
            setattr(self, name, ref)


def column_group(group, width):
    return pl.ds(pl.multiple_of(group * width, width), width)


def attend_rows(places, refs, place, limit, pair_step):
    blocks = range(2 * places.level_count)
    masked_blocks = [block for block in blocks if places.masked(block)]
    level = place // 2
    width = 128 * pair_step
    refs.prefix_scores[...] = dot(refs.spread[0], refs.query[...], NT)
    for at, block in enumerate(masked_blocks):
        refs.hide[at] = jnp.where(places.visible(block, place, limit), 0.0, -jnp.inf)

    def beyond(block):
        return jnp.where(level >= block // 2, 0.0, FAR) if block > 1 else None

    def body(group, carry):
        span = column_group(group, width)
        group_queries = refs.query[:, span]
        group_keys = [refs.keyval(block, 0, span) for block in blocks]

        def scores_of(at):
            pair, head = at // 2, at % 2
            cols = slice(pair * 128, (pair + 1) * 128)
            queries = head_lanes(group_queries[:, cols], head)
            spot = pl.multiple_of((group * pair_step * 2 + at) * PREFIX_PAD, PREFIX_PAD)
            prefix_scores = prefix_mask(refs.prefix_scores[pl.ds(spot, PREFIX_PAD), :], -jnp.inf)
            highest = jnp.max(prefix_scores, axis=0, keepdims=True)
            scores = []
            for block in blocks:
                part = dot(group_keys[block][:, cols], queries, NT)
                if block in masked_blocks:
                    part = part + refs.hide[masked_blocks.index(block)]
                top = jnp.max(part, axis=0, keepdims=True)
                if block > 1:
                    top = top - beyond(block)
                highest = jnp.maximum(highest, top)
                scores.append(part)
            return prefix_scores, scores, highest

        ahead = scores_of(0)
        for at in range(2 * pair_step):
            pair, head = at // 2, at % 2
            cols = slice(pair * 128, (pair + 1) * 128)
            prefix_scores, scores, highest = ahead
            if at + 1 < 2 * pair_step:
                ahead = scores_of(at + 1)
            if head == 0:
                values_t = [refs.keyval(block, 1, span)[:, cols].T for block in blocks]
                prefix_values_t = refs.prefix[1, :, span][:, cols].T
                ones = jnp.ones((PREFIX_PAD, values_t[0].shape[1]), BF16)
                outs = []
            rows = slice(head * HEAD_DIM, (head + 1) * HEAD_DIM)
            prefix_weights = jnp.exp(prefix_scores - highest)
            total = jnp.sum(prefix_weights, axis=0, keepdims=True)
            mixed = dot(prefix_values_t[rows], prefix_weights.astype(BF16))
            for block in blocks:
                base = highest + beyond(block) if block > 1 else highest
                weights = jnp.exp(scores[block] - base)
                part = dot(jnp.concatenate([values_t[block][rows], ones], axis=0), weights.astype(BF16))
                total = total + part[HEAD_DIM : HEAD_DIM + 1]
                mixed = mixed + part[:HEAD_DIM]
            outs.append(mixed * (1.0 / total))
            refs.total[group, at : at + 1, :] = highest + jnp.log(total)
            if head == 1:
                refs.mixed[:, pl.ds(pl.multiple_of(group * width + pair * 128, 128), 128)] = jnp.concatenate(outs, axis=0).T.astype(BF16)
        return carry

    lax.fori_loop(0, PAIRS // pair_step, body, 0)


def feed_rows(refs, place, length, source, weight_copies, chunks, chunk, slots):
    toks = refs.tokens.shape[0]
    spots = place * toks + lax.broadcasted_iota(jnp.int32, (toks, D), 0)
    target = (spots >= source) & (spots < length)
    refs.grad_out[...] = jnp.where(target, refs.cotangent[...].astype(F32), 0.0).astype(BF16)
    residual = refs.tokens[...].astype(F32) + dot(refs.mixed[...], refs.output_weight[...]) + refs.output_bias[...]
    refs.residual[...] = residual
    normed, _ = normalize(residual)
    refs.normed[...] = (normed * refs.second_gain[...] + refs.second_shift[...]).astype(BF16)

    def first(at, slot):
        for copy in weight_copies(at):
            copy.wait()
        bias = refs.expand_bias[:, pl.ds(pl.multiple_of(at * chunk, chunk), chunk)]
        values = dot(refs.normed[...], refs.expand_weight[at % slots]) + bias
        grad_hidden = dot(refs.grad_out[...], refs.contract_weight[at % slots], NT)
        square = values * values
        bend = jnp.tanh(values * (GELU_SCALE + GELU_SCALE * GELU_CUBE * square))
        half = 0.5 + 0.5 * bend
        slope = half + (0.5 * values) * (1.0 - bend * bend) * (
            GELU_SCALE + 3.0 * GELU_SCALE * GELU_CUBE * square
        )
        refs.active[slot] = (values * half).astype(BF16)
        refs.grad_expand[slot] = (grad_hidden * slope).astype(BF16)

    def second(at, slot):
        refs.result[...] += dot(refs.active[slot], refs.contract_weight[at % slots])
        refs.grad_normed[...] += dot(refs.grad_expand[slot], refs.expand_weight[at % slots], NT)

    def refill(at):
        @pl.when(at + slots < chunks)
        def _():
            for copy in weight_copies(at + slots):
                copy.start()

    refs.result[...] = jnp.zeros_like(refs.result)
    refs.grad_normed[...] = jnp.zeros_like(refs.grad_normed)
    first(0, 0)

    def body(at, carry):
        first(2 * at + 1, 1)
        second(2 * at, 0)
        refill(2 * at)
        first(2 * at + 2, 0)
        second(2 * at + 1, 1)
        refill(2 * at + 1)
        return carry

    lax.fori_loop(0, chunks // 2 - 1, body, 0)
    first(chunks - 1, 1)
    second(chunks - 2, 0)
    second(chunks - 1, 1)

    residual = refs.residual[...]
    refs.activations[...] = (residual + refs.result[...] + refs.contract_bias[...]).astype(BF16)
    normed, scale = normalize(residual)
    grad = refs.grad_out[...].astype(F32) + norm_back(refs.grad_normed[...] * refs.second_gain[...], normed, scale)
    refs.grad_residual[0] = grad
    refs.grad_heads[...] = dot(grad.astype(BF16), refs.output_weight[...], NT).astype(BF16)


def prefix_back_rows(refs):
    toks = refs.query.shape[0]
    queries = refs.query[...]
    grads = refs.grad_heads[...]
    product = grads.astype(F32) * refs.mixed[...].astype(F32)
    head_of = lax.broadcasted_iota(jnp.int32, (HEADS, D), 1) // HEAD_DIM
    chosen = jnp.where(head_of == lax.broadcasted_iota(jnp.int32, (HEADS, D), 0), 1.0, 0.0).astype(BF16)
    high, low = split(product)
    inner = dot(chosen, high, NT) + dot(chosen, low, NT)
    refs.inner[...] = inner.reshape(refs.inner.shape)

    def per_head(values):
        return values.reshape(HEADS, PREFIX_PAD, toks)

    scores = per_head(refs.prefix_scores[...])
    grad_weights = per_head(dot(refs.spread[1], grads, NT))
    weights = jnp.exp(scores - refs.total[...].reshape(HEADS, 1, toks))
    valid = lax.broadcasted_iota(jnp.int32, weights.shape, 1) < PREFIX
    weights = jnp.where(valid, weights, 0.0)
    grad_scores = weights * (grad_weights - inner[:, None, :])
    weights = weights.reshape(HEADS * PREFIX_PAD, toks).astype(BF16)
    grad_scores = grad_scores.reshape(HEADS * PREFIX_PAD, toks).astype(BF16)
    refs.result[...] = dot(grad_scores.T, refs.spread[0])
    own = (
        lax.broadcasted_iota(jnp.int32, (HEADS * PREFIX_PAD, D), 0) // PREFIX_PAD
        == lax.broadcasted_iota(jnp.int32, (HEADS * PREFIX_PAD, D), 1) // HEAD_DIM
    )

    def gather(values):
        return jnp.sum(jnp.where(own, values, 0.0).reshape(HEADS, PREFIX_PAD, D), axis=0)

    sums = gather(dot(grad_scores, queries)), gather(dot(weights, grads))
    for half in range(2):
        refs.prefix_grad[half] = sums[half] if refs.earlier_grad is None else sums[half] + refs.earlier_grad[half]


def attend_back_rows(places, refs, place, pair_step):
    blocks = range(2 * places.level_count)
    masked_blocks = [block for block in blocks if places.masked(block)]
    level = place // 2
    width = 128 * pair_step

    def body(group, carry):
        span = column_group(group, width)
        group_queries = refs.query[:, span]
        group_grads = refs.grad_heads[:, span]
        group_keys = [refs.keyval(block, 0, span) for block in blocks]
        group_values = [refs.keyval(block, 1, span) for block in blocks]

        sides = {}

        def side(at):
            if at not in sides:
                cols = slice(at // 2 * 128, (at // 2 + 1) * 128)
                sides[at] = head_lanes(group_queries[:, cols], at % 2), head_lanes(group_grads[:, cols], at % 2)
            return sides[at]

        def products_of(item):
            at, block = item
            cols = slice(at // 2 * 128, (at // 2 + 1) * 128)
            queries, grads = side(at)
            part = dot(group_keys[block][:, cols], queries, NT)
            if block in masked_blocks:
                part = part + refs.hide[masked_blocks.index(block)]
            return part, dot(group_values[block][:, cols], grads, NT)

        items = [(at, block) for at in range(2 * pair_step) for block in blocks]
        ahead = [products_of(item) for item in items[:2]]
        for spot, (at, block) in enumerate(items):
            pair, head = at // 2, at % 2
            cols = slice(pair * 128, (pair + 1) * 128)
            place_cols = pl.ds(pl.multiple_of(group * width + pair * 128, 128), 128)
            scores, grad_weights = ahead.pop(0)
            if spot + 2 < len(items):
                ahead.append(products_of(items[spot + 2]))
            queries, grads = side(at)
            if block == 0:
                if head == 0:
                    keys_t = [keys[:, cols].T for keys in group_keys]
                    grad_keys, grad_values, outs = [], [], []
                total = refs.total[group, at : at + 1, :]
                inner = refs.inner[group, at : at + 1, :]
                grad_query = None
            rows = slice(head * HEAD_DIM, (head + 1) * HEAD_DIM)
            base = total + jnp.where(level >= block // 2, 0.0, FAR) if block > 1 else total
            weights = jnp.exp(scores - base)
            grad_scores = (weights * (grad_weights - inner)).astype(BF16)
            part_values = dot(weights.astype(BF16), grads)
            part_keys = dot(grad_scores, queries)
            part_query = dot(keys_t[block][rows], grad_scores)
            if head == 0:
                grad_values.append(part_values)
                grad_keys.append(part_keys)
            else:
                refs.grad_keyval[block][0, 0, :, place_cols] = (grad_keys[block] + part_keys).astype(BF16)
                refs.grad_keyval[block][0, 1, :, place_cols] = (grad_values[block] + part_values).astype(BF16)
            grad_query = part_query if grad_query is None else grad_query + part_query
            if block == blocks[-1]:
                outs.append(grad_query)
                if head == 1:
                    grad_query = jnp.concatenate(outs, axis=0).T + refs.result[:, place_cols]
                    refs.grad_query[0, :, place_cols] = (grad_query * 0.125).astype(BF16)
        return carry

    lax.fori_loop(0, PAIRS // pair_step, body, 0)


ROW_NAMES = (
    "expand_weight", "contract_weight", "spread", "prefix_scores", "hide", "total",
    "mixed", "grad_out", "residual", "normed", "active", "grad_expand", "result", "grad_normed", "activations",
    "grad_heads", "inner",
)


def row_kernel(places, row, keyval_rows, pair_step, chunk, has_earlier, place_ref, length_ref, source_ref, *rest):
    block_count = 2 * places.level_count
    query_ref, tokens_ref, cotangent_ref, prefix_ref = rest[:4]
    keyval_refs = rest[4 : 4 + block_count]
    rest = rest[4 + block_count :]
    output_weight_ref, expand_weight_hbm, contract_weight_hbm = rest[:3]
    vectors = rest[3:8]
    earlier_grad_ref = rest[8] if has_earlier else None
    rest = rest[8 + 2 * has_earlier :]
    activations_hbm, grad_residual_ref, grad_query_ref = rest[:3]
    grad_keyval_refs = rest[3 : 3 + block_count]
    prefix_grad_ref = rest[3 + block_count]
    rest = rest[4 + block_count :]
    refs = RowRefs(ROW_NAMES, rest)
    refs.output_bias, refs.second_gain, refs.second_shift, refs.expand_bias, refs.contract_bias = vectors
    refs.prefix_grad, refs.earlier_grad = prefix_grad_ref, earlier_grad_ref
    refs.query, refs.prefix = query_ref.at[row], prefix_ref
    refs.keyval = lambda block, half, span: keyval_refs[block][keyval_rows[block], half, :, span]
    refs.grad_residual, refs.grad_query, refs.grad_keyval = grad_residual_ref, grad_query_ref, grad_keyval_refs
    semaphores, weight_semaphores = rest[len(ROW_NAMES) :]
    slots = refs.expand_weight.shape[0]
    chunks = expand_weight_hbm.shape[1] // chunk

    copies = Copies(semaphores)
    refs.output_weight, refs.tokens, refs.cotangent = output_weight_ref, tokens_ref.at[row], cotangent_ref.at[row]

    def weight_copies(at):
        span = pl.ds(pl.multiple_of(at * chunk, chunk), chunk)
        return (
            pltpu.make_async_copy(expand_weight_hbm.at[:, span], refs.expand_weight.at[at % slots], weight_semaphores.at[at]),
            pltpu.make_async_copy(contract_weight_hbm.at[span, :], refs.contract_weight.at[at % slots], weight_semaphores.at[chunks + at]),
        )

    def start_weights(at, carry):
        for copy in weight_copies(at):
            copy.start()
        return carry

    lax.fori_loop(0, slots, start_weights, 0)
    place = place_ref[0]
    length = length_ref[row]
    limit = places.limits(place, length)
    for half in range(2):
        refs.spread[half] = spread_prefix(refs.prefix[half])
    attend_rows(places, refs, place, limit, pair_step)
    feed_rows(refs, place, length, source_ref[row], weight_copies, chunks, chunk, slots)
    copies.start("activations", refs.activations, activations_hbm.at[row])
    prefix_back_rows(refs)
    attend_back_rows(places, refs, place, pair_step)
    copies.wait("activations")


def row_block(after, place, lengths, sources, queries, tokens, cotangent, prefix_keyval, keyvals, weights, row, earlier, earlier_grad, warm=(), pair_step=4, chunk=512, slots=3):
    toks = queries.shape[1]
    block_count = len(keyvals)
    places = Places(toks, block_count // 2)
    output_weight, output_bias, gain, shift, expand_weight, expand_bias, contract_weight, contract_bias = weights
    hidden = expand_weight.shape[1]
    chunks = hidden // chunk
    given = [] if earlier is None else [earlier_grad, earlier]
    masked = sum(places.masked(block) for block in range(block_count))
    per_group = 2 * pair_step
    scratch = dict(
        expand_weight=((slots, D, chunk), BF16), contract_weight=((slots, chunk, D), BF16),
        spread=((2, HEADS * PREFIX_PAD, D), BF16), prefix_scores=((HEADS * PREFIX_PAD, toks), F32),
        hide=((masked, toks, toks), F32), total=((HEADS // per_group, per_group, toks), F32), mixed=((toks, D), BF16),
        grad_out=((toks, D), BF16), residual=((toks, D), F32), normed=((toks, D), BF16),
        active=((2, toks, chunk), BF16), grad_expand=((2, toks, chunk), BF16), result=((toks, D), F32),
        grad_normed=((toks, D), F32), activations=((toks, D), BF16),
        grad_heads=((toks, D), BF16), inner=((HEADS // per_group, per_group, toks), F32),
    )
    return kernel_call(
        functools.partial(row_kernel, places, row, [at for _, at in keyvals], pair_step, chunk, earlier is not None),
        after,
        (
            place, lengths, sources, queries, tokens, cotangent, prefix_keyval, *[array for array, _ in keyvals],
            output_weight, expand_weight, contract_weight, output_bias, gain, shift, expand_bias, contract_bias, *given,
        ),
        ROW_LIMIT,
        [VMEM] * (4 + block_count) + [VMEM, HBM, HBM] + [VMEM] * 5 + [VMEM, ANY][: len(given)],
        [HBM] + [VMEM] * (3 + block_count),
        [
            jax.ShapeDtypeStruct(tokens.shape, BF16),
            jax.ShapeDtypeStruct((1, toks, D), F32),
            jax.ShapeDtypeStruct((1, toks, D), BF16),
        ]
        + [jax.ShapeDtypeStruct((1, 2, toks, D), BF16)] * block_count
        + [jax.ShapeDtypeStruct((2, PREFIX_PAD, D), F32)],
        prefetched=3,
        scratch_shapes=[pltpu.VMEM(*scratch[name]) for name in ROW_NAMES]
        + [pltpu.SemaphoreType.DMA((1,)), pltpu.SemaphoreType.DMA((2 * chunks,))],
        input_output_aliases={16 + block_count: 0} if given else {},
        warm=warm,
        name="row_block",
    )


def up_back_kernel(own_ref, received_ref, weight_ref, grad_ref):
    total = None
    for half in range(2):
        values = (own_ref[0, half].astype(F32) + received_ref[0, half].astype(F32)).astype(BF16)
        part = dot(values, weight_ref[:, (half + 1) * D : (half + 2) * D], NT)
        total = part if total is None else total + part
    grad_ref[0] = total.astype(BF16)


def up_back(after, own, received, weight):
    toks = own.shape[2]
    return kernel_call(
        up_back_kernel,
        after,
        (own, received, weight),
        10,
        [VMEM] * 3,
        [VMEM],
        [jax.ShapeDtypeStruct((1, toks, D), BF16)],
        name="up_back",
    )


def project_back_kernel(query_ref, own_ref, received_ref, weight_ref, total_ref):
    total = dot(query_ref[0], weight_ref[:, :D], NT)
    for half in range(2):
        values = (own_ref[0, half].astype(F32) + received_ref[0, half].astype(F32)).astype(BF16)
        total = total + dot(values, weight_ref[:, (half + 1) * D : (half + 2) * D], NT)
    total_ref[0] = total


def project_back(after, grad_query, own, received, weight):
    toks = grad_query.shape[1]
    return kernel_call(
        project_back_kernel,
        after,
        (grad_query, own, received, weight),
        10,
        [VMEM] * 4,
        [VMEM],
        [jax.ShapeDtypeStruct((1, toks, D), F32)],
        name="project_back",
    )


def finish_kernel(above_count, row, tokens_ref, gain_ref, residual_ref, total_ref, *rest):
    grad_hbm, grad_ref, semaphores = rest[-3:]
    toks = grad_ref.shape[0]
    copies = Copies(semaphores)
    parts = 2
    for part in range(parts):
        span = pl.ds(part * (toks // parts), toks // parts)
        total = total_ref[0, span]
        for above_ref in rest[:above_count]:
            total = total + above_ref[0, span].astype(F32)
        normed, scale = normalize(tokens_ref[row, span].astype(F32))
        grad_ref[span] = residual_ref[0, span] + norm_back(total * gain_ref[...], normed, scale)
        copies.start(part, grad_ref.at[span], grad_hbm.at[row, span])
    for part in range(parts):
        copies.wait(part)


def finish(after, tokens, gain, grad_residual, total, above, row, earlier):
    toks = tokens.shape[1]
    given = [] if earlier is None else [earlier]
    return kernel_call(
        functools.partial(finish_kernel, len(above), row),
        after,
        (tokens, gain, grad_residual, total, *above, *given),
        10,
        [VMEM] * (4 + len(above)) + [ANY] * len(given),
        [HBM],
        [jax.ShapeDtypeStruct(tokens.shape, F32)],
        scratch_shapes=[pltpu.VMEM((toks, D), F32), pltpu.SemaphoreType.DMA((2,))],
        input_output_aliases={4 + len(above): 0} if given else {},
        name="finish",
    )


def prefix_kernel(table_ref, lift_ref, lift_bias_ref, fan_ref, fan_bias_ref, lifted_ref, keyval_ref):
    lifted = jnp.tanh(dot(table_ref[...], lift_ref[...]) + lift_bias_ref[...])
    lifted_ref[...] = jnp.zeros_like(lifted_ref)
    lifted_ref[:PREFIX, :] = lifted
    keyval_ref[...] = jnp.zeros_like(keyval_ref)
    keyval = (dot(lifted.astype(BF16), fan_ref[...]) + fan_bias_ref[...]).astype(BF16)
    keyval_ref[0, :PREFIX, :] = keyval[:, :D]
    keyval_ref[1, :PREFIX, :] = keyval[:, D:]


def prefix_forward(after, table, lift, lift_bias, fan, fan_bias):
    return kernel_call(
        prefix_kernel,
        after,
        (table, lift, lift_bias, fan, fan_bias),
        8,
        [VMEM] * 5,
        [VMEM] * 2,
        [
            jax.ShapeDtypeStruct((PREFIX_PAD, lift.shape[1]), F32),
            jax.ShapeDtypeStruct((2, PREFIX_PAD, D), BF16),
        ],
        name="prefix_forward",
    )


def prefix_network_back_kernel(grad_ref, table_ref, lift_ref, fan_ref, lifted_ref, grad_table_ref, grad_lift_ref, grad_lift_bias_ref, grad_fan_ref, grad_fan_bias_ref):
    lifted = lifted_ref[...]
    lifted_t = jnp.concatenate([lifted.astype(BF16)] * 2, axis=0).T
    grad_lifted = None
    for half in range(2):
        cols = slice(half * D, (half + 1) * D)
        grad = grad_ref[half]
        grad_fan_bias_ref[:, cols] = jnp.sum(grad, axis=0, keepdims=True)
        both = jnp.concatenate(split(grad), axis=0)
        grad_fan_ref[:, cols] = dot(lifted_t, both)
        part = dot(both, fan_ref[:, cols], NT)
        grad_lifted = part if grad_lifted is None else grad_lifted + part
    grad_lifted = (grad_lifted[:PREFIX_PAD] + grad_lifted[PREFIX_PAD:]) * (1.0 - lifted * lifted)
    grad_lift_bias_ref[...] = jnp.sum(grad_lifted, axis=0, keepdims=True)
    both = jnp.concatenate(split(grad_lifted), axis=0)
    table = jnp.concatenate([table_ref[...].astype(F32), jnp.zeros((PREFIX_PAD - PREFIX, D), F32)], axis=0)
    table_t = jnp.concatenate([table.astype(BF16)] * 2, axis=0).T
    grad_lift_ref[...] = dot(table_t, both)
    grad_table = dot(both, lift_ref[...], NT)
    grad_table_ref[...] = (grad_table[:PREFIX_PAD] + grad_table[PREFIX_PAD:])[:PREFIX]


def prefix_network_back(after, grad, table, lift, fan, lifted):
    hidden = lift.shape[1]
    return kernel_call(
        prefix_network_back_kernel,
        after,
        (grad, table, lift, fan, lifted),
        20,
        [VMEM] * 5,
        [VMEM] * 5,
        [
            jax.ShapeDtypeStruct((PREFIX, D), F32),
            jax.ShapeDtypeStruct((D, hidden), F32),
            jax.ShapeDtypeStruct((1, hidden), F32),
            jax.ShapeDtypeStruct((hidden, 2 * D), F32),
            jax.ShapeDtypeStruct((1, 2 * D), F32),
        ],
        name="prefix_network_back",
    )


def add_kernel(left_ref, right_ref, sum_ref):
    sum_ref[...] = left_ref[...] + right_ref[...]


def add(after, left, right):
    return kernel_call(add_kernel, after, (left, right), 2, [VMEM] * 2, [VMEM], [left], name="add")


def mark_kernel(*refs):
    pass


def mark(after):
    return kernel_call(mark_kernel, after, (), 1, [], [], [], name="mark")


class Order:
    def __init__(self):
        self.before = ()

    def call(self, kernel, *operands):
        *outs, token = kernel(self.before, *operands)
        self.before = (token,)
        return outs[0] if len(outs) == 1 else outs


def sum_hops(axes):
    hops = []
    for axis in axes:
        size = lax.axis_size(axis)
        if size & (size - 1):
            return None
        hop = 1
        while hop < size:
            hops.append((axis, [(at, at ^ hop) for at in range(size)]))
            hop *= 2
    return hops


def per_device(tokens, cotangent, row_lengths, source_lengths, first_gain, first_shift, attend_weight, attend_bias, output_weight, output_bias, second_gain, second_shift, expand_weight, expand_bias, contract_weight, contract_bias, prefix_table, lift_weight, lift_bias, fan_weight, fan_bias):
    rows = tokens.shape[0]
    seq = lax.axis_size("seq")
    level_count = seq // 2
    levels = range(1, level_count)
    mates = [(at, at ^ 1) for at in range(seq)]
    place = lax.axis_index("seq").astype(jnp.int32).reshape(1)
    first_gain, first_shift, attend_bias, output_bias, second_gain, second_shift, expand_bias, contract_bias, lift_bias, fan_bias = [
        vector.reshape(1, -1)
        for vector in (first_gain, first_shift, attend_bias, output_bias, second_gain, second_shift, expand_bias, contract_bias, lift_bias, fan_bias)
    ]
    weights = (output_weight, output_bias, second_gain, second_shift, expand_weight, expand_bias, contract_weight, contract_bias)
    order = Order()
    hops = sum_hops(("seq", "dp"))
    activations = None
    input_grad = None
    prefix_grad = None
    arriving = None

    def swap(array):
        return lax.ppermute(array, "seq", mates)

    def hop():
        nonlocal prefix_grad, arriving
        if arriving is not None:
            prefix_grad = order.call(add, prefix_grad, arriving)
            arriving = None
        if hops:
            axis, pairs = hops.pop(0)
            arriving = lax.ppermute(prefix_grad, axis, pairs)

    def lower(row):
        blocks = []
        for level in levels:
            block = order.call(project_up, lower_tokens[row, level], first_gain, first_shift, attend_weight, attend_bias, (queries, cotangent) if row == 0 else ())
            blocks += [block, swap(block)]
        return blocks

    def keyvals_of(row, blocks):
        return [(keyval, row), (mate_keyval, row)] + [(block, 0) for block in blocks]

    row_tokens = [tokens[:1]]
    lower_tokens = {}

    def raise_tokens(row):
        for level in levels:
            pairs = [(at, at + 2 * level) for at in range(seq - 2 * level)]
            lower_tokens[row, level] = lax.ppermute(row_tokens[row], "seq", pairs)

    raise_tokens(0)
    queries, keyval, *later = order.call(project_own, tokens, first_gain, first_shift, attend_weight, attend_bias)
    row_tokens += later
    for row in range(1, rows):
        raise_tokens(row)
    mate_keyval = swap(keyval)
    lifted, prefix_keyval = order.call(prefix_forward, prefix_table, lift_weight, lift_bias, fan_weight, fan_bias)
    blocks = lower(0)
    waiting = []
    input_grad_rows = 0
    for row in range(rows):
        last_row = row + 1 == rows
        activations, grad_residual, grad_query, *grads, prefix_grad = order.call(
            row_block, place, row_lengths, source_lengths, queries, tokens, cotangent, prefix_keyval,
            keyvals_of(row, blocks), weights, row, activations, prefix_grad, (attend_weight,),
        )
        received = swap(grads[1])
        from_mates = [swap(grads[2 * level + 1]) for level in levels]
        if last_row:
            if hops is None:
                prefix_grad = lax.psum(prefix_grad, ("seq", "dp"))
            hop()
            for earlier in waiting:
                earlier()
                hop()
        else:
            blocks = lower(row + 1)
        above = []
        for level in levels:
            part = order.call(up_back, grads[2 * level], from_mates[level - 1], attend_weight)
            above.append(lax.ppermute(part, "seq", [(at + 2 * level, at) for at in range(seq - 2 * level)]))
        if last_row:
            hop()
        total = order.call(project_back, grad_query, grads[0], received, attend_weight)

        def end(row=row, grad_residual=grad_residual, total=total, above=above):
            nonlocal input_grad, input_grad_rows
            input_grad_rows += 1
            input_grad = order.call(finish, tokens, first_gain, grad_residual, total, above, row, input_grad)

        waiting.append(end)
    while hops or arriving is not None:
        hop()
        if arriving is not None:
            if hops:
                order.call(mark)
            else:
                waiting[-1]()
    grad_table, grad_lift, grad_lift_bias, grad_fan, grad_fan_bias = order.call(
        prefix_network_back, prefix_grad, prefix_table, lift_weight, fan_weight, lifted
    )
    if input_grad_rows < rows:
        waiting[-1]()
    return (activations, input_grad, grad_table, grad_lift, grad_lift_bias.reshape(-1), grad_fan, grad_fan_bias.reshape(-1))


def solution(mesh):
    batch = P("dp", "seq", None)
    return jax.shard_map(
        per_device,
        mesh=mesh,
        in_specs=(batch, batch, P("dp"), P("dp")) + (P(),) * 17,
        out_specs=(batch, batch, P(), P(), P(), P(), P()),
        check_vma=False,
    )
```

```python
import functools

import jax
import jax.numpy as jnp
from jax import lax
from jax.experimental import pallas as pl
from jax.experimental.pallas import tpu as pltpu
from jax.sharding import PartitionSpec as P

D = 1024
HEADS = 16
HEAD_DIM = 64
PAIRS = HEADS // 2
PREFIX = 10
PREFIX_PAD = 16
LEAST_LENGTH = 512
NN = (((1,), (0,)), ((), ()))
NT = (((1,), (1,)), ((), ()))
MIB = 1 << 20
BF16 = jnp.bfloat16
F32 = jnp.float32


def dot(left, right, dims=NN):
    return lax.dot_general(left, right, dims, preferred_element_type=F32)


ANY = pl.BlockSpec(memory_space=pl.ANY)


VMEM = pl.BlockSpec(memory_space=pltpu.VMEM)
COVER = pl.CostEstimate(flops=10**10, bytes_accessed=10**9, transcendentals=0)
TOKEN = jax.ShapeDtypeStruct((8, 128), F32)


def kernel_call(kernel, after, operands, limit, in_specs, out_specs, out_shape, prefetched=0, scratch_shapes=(), warm=(), **rest):
    lead = prefetched + len(in_specs)

    def body(*refs):
        outs = lead + len(after) + len(warm)
        token_ref = refs[outs + len(out_shape)]
        token_ref[...] = jnp.zeros_like(token_ref)
        kernel(*refs[:lead], *refs[outs : outs + len(out_shape)], *refs[outs + len(out_shape) + 1 :])

    spec = pltpu.PrefetchScalarGridSpec(
        num_scalar_prefetch=prefetched,
        grid=(1,),
        in_specs=[*in_specs] + [ANY] * len(after) + [VMEM] * len(warm),
        out_specs=[*out_specs, VMEM],
        scratch_shapes=scratch_shapes,
    )
    return pl.pallas_call(
        body,
        grid_spec=spec,
        out_shape=[*(jax.ShapeDtypeStruct(out.shape, out.dtype) for out in out_shape), TOKEN],
        compiler_params=pltpu.CompilerParams(dimension_semantics=("arbitrary",), vmem_limit_bytes=limit * MIB),
        cost_estimate=COVER,
        **rest,
    )(*operands, *after, *warm)


def split(values):
    high = values.astype(BF16)
    return high, (values - high.astype(F32)).astype(BF16)


class Copies:
    def __init__(self, semaphores):
        self.semaphores = semaphores
        self.count = 0
        self.copies = {}

    def start(self, name, source, target):
        copy = pltpu.make_async_copy(source, target, self.semaphores.at[self.count])
        copy.start()
        self.count += 1
        self.copies[name] = copy

    def wait(self, name):
        self.copies[name].wait()


HBM = pl.BlockSpec(memory_space=pltpu.HBM)


def normalize(values):
    centred = values - jnp.mean(values, axis=-1, keepdims=True)
    scale = lax.rsqrt(jnp.mean(centred * centred, axis=-1, keepdims=True) + 1e-05)
    return centred * scale, scale


def norm_back(grad, normed, scale):
    return scale * (
        grad
        - jnp.mean(grad, axis=-1, keepdims=True)
        - normed * jnp.mean(grad * normed, axis=-1, keepdims=True)
    )


def project_own_kernel(tokens_ref, gain_ref, shift_ref, bias_ref, weight_ref, query_ref, keyval_ref, *rest):
    later_refs, normed_ref = rest[:-1], rest[-1]
    rows, toks, _ = tokens_ref.shape
    for at, later_ref in enumerate(later_refs):
        later_ref[0] = tokens_ref[at + 1]
    normed, _ = normalize(tokens_ref[...].reshape(rows * toks, D).astype(F32))
    normed_ref[...] = (normed * gain_ref[...] + shift_ref[...]).astype(BF16)
    chunk = D // 2
    for at in range(6):
        span = slice(at * chunk, (at + 1) * chunk)
        result = (dot(normed_ref[...], weight_ref[:, span]) + bias_ref[:, span]).astype(BF16)
        cols = slice(at % 2 * chunk, (at % 2 + 1) * chunk)
        if at < 2:
            query_ref[:, :, cols] = (result * 0.125).reshape(rows, toks, chunk)
        else:
            keyval_ref[:, at // 2 - 1, :, cols] = result.reshape(rows, toks, chunk)


def project_own(after, tokens, gain, shift, weight, bias):
    rows, toks, _ = tokens.shape
    return kernel_call(
        project_own_kernel,
        after,
        (tokens, gain, shift, bias, weight),
        14,
        [VMEM] * 5,
        [VMEM] * (1 + rows),
        [jax.ShapeDtypeStruct((rows, toks, D), BF16), jax.ShapeDtypeStruct((rows, 2, toks, D), BF16)]
        + [jax.ShapeDtypeStruct((1, toks, D), BF16)] * (rows - 1),
        scratch_shapes=[pltpu.VMEM((rows * toks, D), BF16)],
        name="project_own",
    )


def project_up_kernel(tokens_ref, gain_ref, shift_ref, bias_ref, weight_ref, keyval_ref):
    toks = tokens_ref.shape[1]
    normed, _ = normalize(tokens_ref[0].astype(F32))
    normed = (normed * gain_ref[...] + shift_ref[...]).astype(BF16)
    for half in range(2):
        cols = slice((half + 1) * D, (half + 2) * D)
        keyval_ref[0, half] = (dot(normed, weight_ref[:, cols]) + bias_ref[:, cols]).astype(BF16)


def project_up(after, tokens, gain, shift, weight, bias, warm=()):
    toks = tokens.shape[1]
    return kernel_call(
        project_up_kernel,
        after,
        (tokens, gain, shift, bias, weight),
        10,
        [VMEM] * 5,
        [VMEM],
        [jax.ShapeDtypeStruct((1, 2, toks, D), BF16)],
        warm=warm,
        name="project_up",
    )


def head_lanes(values, head):
    lanes = lax.broadcasted_iota(jnp.int32, values.shape, 1)
    keep = lanes < HEAD_DIM if head == 0 else lanes >= HEAD_DIM
    return jnp.where(keep, values, jnp.zeros_like(values))


def prefix_mask(values, fill):
    places = lax.broadcasted_iota(jnp.int32, values.shape, 0)
    return jnp.where(places < PREFIX, values, fill)


class Places:
    def __init__(self, toks, level_count):
        self.toks = toks
        self.level_count = level_count

    def masked(self, block):
        if block < 2:
            return True
        level = block // 2
        return (self.level_count - level) * 2 * self.toks > LEAST_LENGTH

    def limits(self, place, length):
        base = place * self.toks
        queries = base + lax.broadcasted_iota(jnp.int32, (1, self.toks), 1)
        return jnp.minimum(queries, length - 1)

    def visible(self, block, place, limit):
        if block == 0:
            base = place * self.toks
        else:
            base = (lax.bitwise_xor(place, block % 2) - (block // 2) * 2) * self.toks
        keys = lax.broadcasted_iota(jnp.int32, (self.toks, self.toks), 0)
        return keys <= limit - base


def spread_prefix(prefix):
    tiled = jnp.concatenate([prefix] * HEADS, axis=0)
    rows = lax.broadcasted_iota(jnp.int32, tiled.shape, 0) // PREFIX_PAD
    cols = lax.broadcasted_iota(jnp.int32, tiled.shape, 1) // HEAD_DIM
    return jnp.where(rows == cols, tiled, jnp.zeros_like(tiled))


GELU_SCALE = 0.7978845608028654
GELU_CUBE = 0.044715
FAR = 1e30
ROW_LIMIT = 30


PACKED = (8, 2 * D + D // 2)


def pack_prefix(ref, halves):
    for half, values in enumerate(halves):
        ref[:, half * D : (half + 1) * D] = values[:8]
        for row in range(8, PREFIX):
            for part in range(2):
                at = (half * (PREFIX - 8) + row - 8) * 2 + part
                ref[at : at + 1, 2 * D :] = values[row : row + 1, part * (D // 2) : (part + 1) * (D // 2)]


def unpack_prefix(ref, half):
    rest = jnp.concatenate([ref[:, 2 * D :], jnp.zeros((8, D // 2), F32)], axis=0)
    rows = []
    for row in range(8, PREFIX):
        at = (half * (PREFIX - 8) + row - 8) * 2
        rows.append(jnp.concatenate([rest[at : at + 1], rest[at + 1 : at + 2]], axis=1))
    rows.append(jnp.zeros((PREFIX_PAD - PREFIX, D), F32))
    return jnp.concatenate([ref[:, half * D : (half + 1) * D]] + rows, axis=0)


class RowRefs:
    def __init__(self, names, refs):
        for name, ref in zip(names, refs):
            setattr(self, name, ref)


def column_group(group, width):
    return pl.ds(pl.multiple_of(group * width, width), width)


def attend_rows(places, refs, place, limit, pair_step):
    blocks = range(2 * places.level_count)
    masked_blocks = [block for block in blocks if places.masked(block)]
    level = place // 2
    width = 128 * pair_step
    refs.prefix_scores[...] = dot(refs.spread[0], refs.query[...], NT)
    for at, block in enumerate(masked_blocks):
        refs.hide[at] = jnp.where(places.visible(block, place, limit), 0.0, -jnp.inf)

    def beyond(block):
        return jnp.where(level >= block // 2, 0.0, FAR) if block > 1 else None

    def body(group, carry):
        span = column_group(group, width)
        group_queries = refs.query[:, span]
        group_keys = [refs.keyval(block, 0, span) for block in blocks]

        def scores_of(at):
            pair, head = at // 2, at % 2
            cols = slice(pair * 128, (pair + 1) * 128)
            queries = head_lanes(group_queries[:, cols], head)
            spot = pl.multiple_of((group * pair_step * 2 + at) * PREFIX_PAD, PREFIX_PAD)
            prefix_scores = prefix_mask(refs.prefix_scores[pl.ds(spot, PREFIX_PAD), :], -jnp.inf)
            highest = jnp.max(prefix_scores, axis=0, keepdims=True)
            scores = []
            for block in blocks:
                part = dot(group_keys[block][:, cols], queries, NT)
                if block in masked_blocks:
                    part = part + refs.hide[masked_blocks.index(block)]
                top = jnp.max(part, axis=0, keepdims=True)
                if block > 1:
                    top = top - beyond(block)
                highest = jnp.maximum(highest, top)
                scores.append(part)
            return prefix_scores, scores, highest

        ahead = scores_of(0)
        for at in range(2 * pair_step):
            pair, head = at // 2, at % 2
            cols = slice(pair * 128, (pair + 1) * 128)
            prefix_scores, scores, highest = ahead
            if at + 1 < 2 * pair_step:
                ahead = scores_of(at + 1)
            if head == 0:
                values_t = [refs.keyval(block, 1, span)[:, cols].T for block in blocks]
                prefix_values_t = refs.prefix[1, :, span][:, cols].T
                ones = jnp.ones((PREFIX_PAD, values_t[0].shape[1]), BF16)
                outs = []
            rows = slice(head * HEAD_DIM, (head + 1) * HEAD_DIM)
            prefix_weights = jnp.exp(prefix_scores - highest)
            total = jnp.sum(prefix_weights, axis=0, keepdims=True)
            mixed = dot(prefix_values_t[rows], prefix_weights.astype(BF16))
            for block in blocks:
                base = highest + beyond(block) if block > 1 else highest
                weights = jnp.exp(scores[block] - base)
                part = dot(jnp.concatenate([values_t[block][rows], ones], axis=0), weights.astype(BF16))
                total = total + part[HEAD_DIM : HEAD_DIM + 1]
                mixed = mixed + part[:HEAD_DIM]
            outs.append(mixed * (1.0 / total))
            refs.total[group, at : at + 1, :] = highest + jnp.log(total)
            if head == 1:
                refs.mixed[:, pl.ds(pl.multiple_of(group * width + pair * 128, 128), 128)] = jnp.concatenate(outs, axis=0).T.astype(BF16)
        return carry

    lax.fori_loop(0, PAIRS // pair_step, body, 0)


def feed_rows(refs, place, length, source, weight_copies, chunks, chunk, slots):
    toks = refs.tokens.shape[0]
    spots = place * toks + lax.broadcasted_iota(jnp.int32, (toks, D), 0)
    target = (spots >= source) & (spots < length)
    refs.grad_out[...] = jnp.where(target, refs.cotangent[...].astype(F32), 0.0).astype(BF16)
    residual = refs.tokens[...].astype(F32) + dot(refs.mixed[...], refs.output_weight[...]) + refs.output_bias[...]
    refs.residual[...] = residual
    normed, _ = normalize(residual)
    refs.normed[...] = (normed * refs.second_gain[...] + refs.second_shift[...]).astype(BF16)

    def first(at, slot):
        for copy in weight_copies(at):
            copy.wait()
        bias = refs.expand_bias[:, pl.ds(pl.multiple_of(at * chunk, chunk), chunk)]
        values = dot(refs.normed[...], refs.expand_weight[at % slots]) + bias
        grad_hidden = dot(refs.grad_out[...], refs.contract_weight[at % slots], NT)
        square = values * values
        bend = jnp.tanh(values * (GELU_SCALE + GELU_SCALE * GELU_CUBE * square))
        half = 0.5 + 0.5 * bend
        slope = half + (0.5 * values) * (1.0 - bend * bend) * (
            GELU_SCALE + 3.0 * GELU_SCALE * GELU_CUBE * square
        )
        refs.active[slot] = (values * half).astype(BF16)
        refs.grad_expand[slot] = (grad_hidden * slope).astype(BF16)

    def second(at, slot):
        refs.result[...] += dot(refs.active[slot], refs.contract_weight[at % slots])
        refs.grad_normed[...] += dot(refs.grad_expand[slot], refs.expand_weight[at % slots], NT)

    def refill(at):
        @pl.when(at + slots < chunks)
        def _():
            for copy in weight_copies(at + slots):
                copy.start()

    refs.result[...] = jnp.zeros_like(refs.result)
    refs.grad_normed[...] = jnp.zeros_like(refs.grad_normed)
    first(0, 0)

    def body(at, carry):
        first(2 * at + 1, 1)
        second(2 * at, 0)
        refill(2 * at)
        first(2 * at + 2, 0)
        second(2 * at + 1, 1)
        refill(2 * at + 1)
        return carry

    lax.fori_loop(0, chunks // 2 - 1, body, 0)
    first(chunks - 1, 1)
    second(chunks - 2, 0)
    second(chunks - 1, 1)

    residual = refs.residual[...]
    refs.activations[...] = (residual + refs.result[...] + refs.contract_bias[...]).astype(BF16)
    normed, scale = normalize(residual)
    grad = refs.grad_out[...].astype(F32) + norm_back(refs.grad_normed[...] * refs.second_gain[...], normed, scale)
    refs.grad_residual[0] = grad
    refs.grad_heads[...] = dot(grad.astype(BF16), refs.output_weight[...], NT).astype(BF16)


def prefix_back_rows(refs):
    toks = refs.query.shape[0]
    queries = refs.query[...]
    grads = refs.grad_heads[...]
    product = grads.astype(F32) * refs.mixed[...].astype(F32)
    head_of = lax.broadcasted_iota(jnp.int32, (HEADS, D), 1) // HEAD_DIM
    chosen = jnp.where(head_of == lax.broadcasted_iota(jnp.int32, (HEADS, D), 0), 1.0, 0.0).astype(BF16)
    high, low = split(product)
    inner = dot(chosen, high, NT) + dot(chosen, low, NT)
    refs.inner[...] = inner.reshape(refs.inner.shape)

    def per_head(values):
        return values.reshape(HEADS, PREFIX_PAD, toks)

    scores = per_head(refs.prefix_scores[...])
    grad_weights = per_head(dot(refs.spread[1], grads, NT))
    weights = jnp.exp(scores - refs.total[...].reshape(HEADS, 1, toks))
    valid = lax.broadcasted_iota(jnp.int32, weights.shape, 1) < PREFIX
    weights = jnp.where(valid, weights, 0.0)
    grad_scores = weights * (grad_weights - inner[:, None, :])
    weights = weights.reshape(HEADS * PREFIX_PAD, toks).astype(BF16)
    grad_scores = grad_scores.reshape(HEADS * PREFIX_PAD, toks).astype(BF16)
    refs.result[...] = dot(grad_scores.T, refs.spread[0])
    own = (
        lax.broadcasted_iota(jnp.int32, (HEADS * PREFIX_PAD, D), 0) // PREFIX_PAD
        == lax.broadcasted_iota(jnp.int32, (HEADS * PREFIX_PAD, D), 1) // HEAD_DIM
    )

    def gather(values):
        return jnp.sum(jnp.where(own, values, 0.0).reshape(HEADS, PREFIX_PAD, D), axis=0)

    sums = gather(dot(grad_scores, queries)), gather(dot(weights, grads))
    pack_prefix(refs.prefix_grad, sums)
    refs.prefix_grad[...] += refs.earlier_grad[...]


def attend_back_rows(places, refs, place, pair_step):
    blocks = range(2 * places.level_count)
    masked_blocks = [block for block in blocks if places.masked(block)]
    level = place // 2
    width = 128 * pair_step

    def body(group, carry):
        span = column_group(group, width)
        group_queries = refs.query[:, span]
        group_grads = refs.grad_heads[:, span]
        group_keys = [refs.keyval(block, 0, span) for block in blocks]
        group_values = [refs.keyval(block, 1, span) for block in blocks]

        sides = {}

        def side(at):
            if at not in sides:
                cols = slice(at // 2 * 128, (at // 2 + 1) * 128)
                sides[at] = head_lanes(group_queries[:, cols], at % 2), head_lanes(group_grads[:, cols], at % 2)
            return sides[at]

        def products_of(item):
            at, block = item
            cols = slice(at // 2 * 128, (at // 2 + 1) * 128)
            queries, grads = side(at)
            part = dot(group_keys[block][:, cols], queries, NT)
            if block in masked_blocks:
                part = part + refs.hide[masked_blocks.index(block)]
            return part, dot(group_values[block][:, cols], grads, NT)

        items = [(at, block) for at in range(2 * pair_step) for block in blocks]
        ahead = [products_of(item) for item in items[:2]]
        for spot, (at, block) in enumerate(items):
            pair, head = at // 2, at % 2
            cols = slice(pair * 128, (pair + 1) * 128)
            place_cols = pl.ds(pl.multiple_of(group * width + pair * 128, 128), 128)
            scores, grad_weights = ahead.pop(0)
            if spot + 2 < len(items):
                ahead.append(products_of(items[spot + 2]))
            queries, grads = side(at)
            if block == 0:
                if head == 0:
                    keys_t = [keys[:, cols].T for keys in group_keys]
                    grad_keys, grad_values, outs = [], [], []
                total = refs.total[group, at : at + 1, :]
                inner = refs.inner[group, at : at + 1, :]
                grad_query = None
            rows = slice(head * HEAD_DIM, (head + 1) * HEAD_DIM)
            base = total + jnp.where(level >= block // 2, 0.0, FAR) if block > 1 else total
            weights = jnp.exp(scores - base)
            grad_scores = (weights * (grad_weights - inner)).astype(BF16)
            part_values = dot(weights.astype(BF16), grads)
            part_keys = dot(grad_scores, queries)
            part_query = dot(keys_t[block][rows], grad_scores)
            if head == 0:
                grad_values.append(part_values)
                grad_keys.append(part_keys)
            else:
                refs.grad_keyval[block][0, 0, :, place_cols] = (grad_keys[block] + part_keys).astype(BF16)
                refs.grad_keyval[block][0, 1, :, place_cols] = (grad_values[block] + part_values).astype(BF16)
            grad_query = part_query if grad_query is None else grad_query + part_query
            if block == blocks[-1]:
                outs.append(grad_query)
                if head == 1:
                    grad_query = jnp.concatenate(outs, axis=0).T + refs.result[:, place_cols]
                    refs.grad_query[0, :, place_cols] = (grad_query * 0.125).astype(BF16)
        return carry

    lax.fori_loop(0, PAIRS // pair_step, body, 0)


ROW_NAMES = (
    "expand_weight", "contract_weight", "spread", "prefix_scores", "hide", "total",
    "mixed", "grad_out", "residual", "normed", "active", "grad_expand", "result", "grad_normed",
    "grad_heads", "inner",
)


def row_kernel(places, keyval_rows, pair_step, chunk, row_ref, place_ref, length_ref, source_ref, *rest):
    block_count = 2 * places.level_count
    row = row_ref[0]
    query_ref, tokens_ref, cotangent_ref, prefix_ref = rest[:4]
    keyval_refs = rest[4 : 4 + block_count]
    rest = rest[4 + block_count :]
    output_weight_ref, expand_weight_hbm, contract_weight_hbm = rest[:3]
    vectors = rest[3:8]
    earlier_grad_ref = rest[8]
    rest = rest[9:]
    activations_ref, grad_residual_ref, grad_query_ref = rest[:3]
    grad_keyval_refs = rest[3 : 3 + block_count]
    prefix_grad_ref = rest[3 + block_count]
    rest = rest[4 + block_count :]
    refs = RowRefs(ROW_NAMES, rest)
    refs.output_bias, refs.second_gain, refs.second_shift, refs.expand_bias, refs.contract_bias = vectors
    refs.prefix_grad, refs.earlier_grad = prefix_grad_ref, earlier_grad_ref
    refs.activations = activations_ref.at[0]
    refs.query, refs.prefix = query_ref.at[row], prefix_ref
    refs.keyval = lambda block, half, span: keyval_refs[block][row if keyval_rows[block] is None else keyval_rows[block], half, :, span]
    refs.grad_residual, refs.grad_query, refs.grad_keyval = grad_residual_ref, grad_query_ref, grad_keyval_refs
    (weight_semaphores,) = rest[len(ROW_NAMES) :]
    slots = refs.expand_weight.shape[0]
    chunks = expand_weight_hbm.shape[1] // chunk

    refs.output_weight, refs.tokens, refs.cotangent = output_weight_ref, tokens_ref.at[row], cotangent_ref.at[row]

    def weight_copies(at):
        span = pl.ds(pl.multiple_of(at * chunk, chunk), chunk)
        return (
            pltpu.make_async_copy(expand_weight_hbm.at[:, span], refs.expand_weight.at[at % slots], weight_semaphores.at[at]),
            pltpu.make_async_copy(contract_weight_hbm.at[span, :], refs.contract_weight.at[at % slots], weight_semaphores.at[chunks + at]),
        )

    def start_weights(at, carry):
        for copy in weight_copies(at):
            copy.start()
        return carry

    lax.fori_loop(0, slots, start_weights, 0)
    place = place_ref[0]
    length = length_ref[row]
    limit = places.limits(place, length)
    for half in range(2):
        refs.spread[half] = spread_prefix(refs.prefix[half])
    attend_rows(places, refs, place, limit, pair_step)
    feed_rows(refs, place, length, source_ref[row], weight_copies, chunks, chunk, slots)
    prefix_back_rows(refs)
    attend_back_rows(places, refs, place, pair_step)


def row_block(after, place, lengths, sources, queries, tokens, cotangent, prefix_keyval, keyvals, weights, row, earlier_grad, warm=(), pair_step=4, chunk=512, slots=3):
    toks = queries.shape[1]
    block_count = len(keyvals)
    places = Places(toks, block_count // 2)
    output_weight, output_bias, gain, shift, expand_weight, expand_bias, contract_weight, contract_bias = weights
    hidden = expand_weight.shape[1]
    chunks = hidden // chunk
    masked = sum(places.masked(block) for block in range(block_count))
    per_group = 2 * pair_step
    scratch = dict(
        expand_weight=((slots, D, chunk), BF16), contract_weight=((slots, chunk, D), BF16),
        spread=((2, HEADS * PREFIX_PAD, D), BF16), prefix_scores=((HEADS * PREFIX_PAD, toks), F32),
        hide=((masked, toks, toks), F32), total=((HEADS // per_group, per_group, toks), F32), mixed=((toks, D), BF16),
        grad_out=((toks, D), BF16), residual=((toks, D), F32), normed=((toks, D), BF16),
        active=((2, toks, chunk), BF16), grad_expand=((2, toks, chunk), BF16), result=((toks, D), F32),
        grad_normed=((toks, D), F32),
        grad_heads=((toks, D), BF16), inner=((HEADS // per_group, per_group, toks), F32),
    )
    return kernel_call(
        functools.partial(row_kernel, places, [at for _, at in keyvals], pair_step, chunk),
        after,
        (
            jnp.full((1,), row, jnp.int32), place, lengths, sources, queries, tokens, cotangent, prefix_keyval, *[array for array, _ in keyvals],
            output_weight, expand_weight, contract_weight, output_bias, gain, shift, expand_bias, contract_bias, earlier_grad,
        ),
        ROW_LIMIT,
        [VMEM] * (4 + block_count) + [VMEM, HBM, HBM] + [VMEM] * 6,
        [VMEM] * (4 + block_count),
        [
            jax.ShapeDtypeStruct((1, toks, D), BF16),
            jax.ShapeDtypeStruct((1, toks, D), F32),
            jax.ShapeDtypeStruct((1, toks, D), BF16),
        ]
        + [jax.ShapeDtypeStruct((1, 2, toks, D), BF16)] * block_count
        + [jax.ShapeDtypeStruct(PACKED, F32)],
        prefetched=4,
        scratch_shapes=[pltpu.VMEM(*scratch[name]) for name in ROW_NAMES]
        + [pltpu.SemaphoreType.DMA((2 * chunks,))],
        warm=warm,
        name="row_block",
    )


def up_back_kernel(own_ref, received_ref, weight_ref, grad_ref):
    total = None
    for half in range(2):
        values = (own_ref[0, half].astype(F32) + received_ref[0, half].astype(F32)).astype(BF16)
        part = dot(values, weight_ref[:, (half + 1) * D : (half + 2) * D], NT)
        total = part if total is None else total + part
    grad_ref[0] = total.astype(BF16)


def up_back(after, own, received, weight):
    toks = own.shape[2]
    return kernel_call(
        up_back_kernel,
        after,
        (own, received, weight),
        10,
        [VMEM] * 3,
        [VMEM],
        [jax.ShapeDtypeStruct((1, toks, D), BF16)],
        name="up_back",
    )


def project_back_kernel(query_ref, own_ref, received_ref, weight_ref, total_ref):
    total = dot(query_ref[0], weight_ref[:, :D], NT)
    for half in range(2):
        values = (own_ref[0, half].astype(F32) + received_ref[0, half].astype(F32)).astype(BF16)
        total = total + dot(values, weight_ref[:, (half + 1) * D : (half + 2) * D], NT)
    total_ref[0] = total


def project_back(after, grad_query, own, received, weight):
    toks = grad_query.shape[1]
    return kernel_call(
        project_back_kernel,
        after,
        (grad_query, own, received, weight),
        10,
        [VMEM] * 4,
        [VMEM],
        [jax.ShapeDtypeStruct((1, toks, D), F32)],
        name="project_back",
    )


def finish_kernel(above_count, row, tokens_ref, gain_ref, residual_ref, total_ref, activations_ref, *rest):
    activations_hbm, grad_hbm, grad_ref, semaphores = rest[-4:]
    toks = grad_ref.shape[0]
    copies = Copies(semaphores)
    copies.start("activations", activations_ref.at[0], activations_hbm.at[row])
    parts = 2
    for part in range(parts):
        span = pl.ds(part * (toks // parts), toks // parts)
        total = total_ref[0, span]
        for above_ref in rest[:above_count]:
            total = total + above_ref[0, span].astype(F32)
        normed, scale = normalize(tokens_ref[row, span].astype(F32))
        grad_ref[span] = residual_ref[0, span] + norm_back(total * gain_ref[...], normed, scale)
        copies.start(part, grad_ref.at[span], grad_hbm.at[row, span])
    for part in range(parts):
        copies.wait(part)
    copies.wait("activations")


def finish(after, tokens, gain, grad_residual, total, activations, above, row, earlier):
    toks = tokens.shape[1]
    return kernel_call(
        functools.partial(finish_kernel, len(above), row),
        after,
        (tokens, gain, grad_residual, total, activations, *above, *earlier),
        10,
        [VMEM] * (5 + len(above)) + [ANY] * len(earlier),
        [HBM] * 2,
        [jax.ShapeDtypeStruct(tokens.shape, BF16), jax.ShapeDtypeStruct(tokens.shape, F32)],
        scratch_shapes=[pltpu.VMEM((toks, D), F32), pltpu.SemaphoreType.DMA((3,))],
        input_output_aliases={5 + len(above) + at: at for at in range(len(earlier))},
        name="finish",
    )


def prefix_kernel(table_ref, lift_ref, lift_bias_ref, fan_ref, fan_bias_ref, lifted_ref, keyval_ref):
    lifted = jnp.tanh(dot(table_ref[...], lift_ref[...]) + lift_bias_ref[...])
    lifted_ref[...] = jnp.zeros_like(lifted_ref)
    lifted_ref[:PREFIX, :] = lifted
    keyval_ref[...] = jnp.zeros_like(keyval_ref)
    keyval = (dot(lifted.astype(BF16), fan_ref[...]) + fan_bias_ref[...]).astype(BF16)
    keyval_ref[0, :PREFIX, :] = keyval[:, :D]
    keyval_ref[1, :PREFIX, :] = keyval[:, D:]


def prefix_forward(after, table, lift, lift_bias, fan, fan_bias):
    return kernel_call(
        prefix_kernel,
        after,
        (table, lift, lift_bias, fan, fan_bias),
        8,
        [VMEM] * 5,
        [VMEM] * 2,
        [
            jax.ShapeDtypeStruct((PREFIX_PAD, lift.shape[1]), F32),
            jax.ShapeDtypeStruct((2, PREFIX_PAD, D), BF16),
        ],
        name="prefix_forward",
    )


def prefix_network_back_kernel(grad_ref, table_ref, lift_ref, fan_ref, lifted_ref, grad_table_ref, grad_lift_ref, grad_lift_bias_ref, grad_fan_ref, grad_fan_bias_ref):
    lifted = lifted_ref[...]
    lifted_t = jnp.concatenate([lifted.astype(BF16)] * 2, axis=0).T
    grad_lifted = None
    for half in range(2):
        cols = slice(half * D, (half + 1) * D)
        grad = unpack_prefix(grad_ref, half)
        grad_fan_bias_ref[:, cols] = jnp.sum(grad, axis=0, keepdims=True)
        both = jnp.concatenate(split(grad), axis=0)
        grad_fan_ref[:, cols] = dot(lifted_t, both)
        part = dot(both, fan_ref[:, cols], NT)
        grad_lifted = part if grad_lifted is None else grad_lifted + part
    grad_lifted = (grad_lifted[:PREFIX_PAD] + grad_lifted[PREFIX_PAD:]) * (1.0 - lifted * lifted)
    grad_lift_bias_ref[...] = jnp.sum(grad_lifted, axis=0, keepdims=True)
    both = jnp.concatenate(split(grad_lifted), axis=0)
    table = jnp.concatenate([table_ref[...].astype(F32), jnp.zeros((PREFIX_PAD - PREFIX, D), F32)], axis=0)
    table_t = jnp.concatenate([table.astype(BF16)] * 2, axis=0).T
    grad_lift_ref[...] = dot(table_t, both)
    grad_table = dot(both, lift_ref[...], NT)
    grad_table_ref[...] = (grad_table[:PREFIX_PAD] + grad_table[PREFIX_PAD:])[:PREFIX]


def prefix_network_back(after, grad, table, lift, fan, lifted):
    hidden = lift.shape[1]
    return kernel_call(
        prefix_network_back_kernel,
        after,
        (grad, table, lift, fan, lifted),
        20,
        [VMEM] * 5,
        [VMEM] * 5,
        [
            jax.ShapeDtypeStruct((PREFIX, D), F32),
            jax.ShapeDtypeStruct((D, hidden), F32),
            jax.ShapeDtypeStruct((1, hidden), F32),
            jax.ShapeDtypeStruct((hidden, 2 * D), F32),
            jax.ShapeDtypeStruct((1, 2 * D), F32),
        ],
        name="prefix_network_back",
    )


def add_kernel(*refs):
    total = refs[0][...]
    for ref in refs[1:-1]:
        total = total + ref[...]
    refs[-1][...] = total


def add(after, *values):
    return kernel_call(add_kernel, after, values, 2, [VMEM] * len(values), [VMEM], values[:1], name="add")


def mark_kernel(*refs):
    pass


def mark(after):
    return kernel_call(mark_kernel, after, (), 1, [], [], [], name="mark")


def hold(after, array):
    return kernel_call(mark_kernel, after, (array,), 1, [ANY], [ANY], [array], input_output_aliases={0: 0}, name="hold")


class Order:
    def __init__(self):
        self.before = ()

    def call(self, kernel, *operands):
        *outs, token = kernel(self.before, *operands)
        self.before = (token,)
        return outs[0] if len(outs) == 1 else outs


def sum_stages():
    stages = []
    for axis, most in (("seq", 1), ("dp", 2)):
        size = lax.axis_size(axis)
        if size & (size - 1):
            return None
        hop = 1
        while hop < size:
            bits = most if hop > 1 and hop * 2 < size else 1
            stages.append((axis, [[(at, at ^ (hop * step)) for at in range(size)] for step in range(1, 2**bits)]))
            hop *= 2**bits
    return stages


def per_device(tokens, cotangent, row_lengths, source_lengths, first_gain, first_shift, attend_weight, attend_bias, output_weight, output_bias, second_gain, second_shift, expand_weight, expand_bias, contract_weight, contract_bias, prefix_table, lift_weight, lift_bias, fan_weight, fan_bias):
    rows = tokens.shape[0]
    seq = lax.axis_size("seq")
    level_count = seq // 2
    levels = range(1, level_count)
    mates = [(at, at ^ 1) for at in range(seq)]
    place = lax.axis_index("seq").astype(jnp.int32).reshape(1)
    first_gain, first_shift, attend_bias, output_bias, second_gain, second_shift, expand_bias, contract_bias, lift_bias, fan_bias = [
        vector.reshape(1, -1)
        for vector in (first_gain, first_shift, attend_bias, output_bias, second_gain, second_shift, expand_bias, contract_bias, lift_bias, fan_bias)
    ]
    weights = (output_weight, output_bias, second_gain, second_shift, expand_weight, expand_bias, contract_weight, contract_bias)
    order = Order()
    hops = sum_stages()
    finished = ()
    prefix_grad = jnp.zeros(PACKED, F32)
    arriving = None

    def swap(array):
        return lax.ppermute(array, "seq", mates)

    def hop():
        nonlocal prefix_grad, arriving
        if arriving is not None:
            prefix_grad = order.call(add, prefix_grad, *arriving)
            arriving = None
        if hops:
            axis, partners = hops.pop(0)
            arriving = [lax.ppermute(prefix_grad, axis, pairs) for pairs in partners]

    def lower(row):
        blocks = []
        for level in levels:
            block = order.call(project_up, lower_tokens[row, level], first_gain, first_shift, attend_weight, attend_bias, (queries, cotangent) if row == 0 else ())
            blocks += [block, swap(block)]
        return blocks

    def keyvals_of(blocks):
        return [(keyval, None), (mate_keyval, None)] + [(block, 0) for block in blocks]

    row_tokens = [tokens[:1]]
    lower_tokens = {}

    def raise_tokens(row):
        for level in levels:
            pairs = [(at, at + 2 * level) for at in range(seq - 2 * level)]
            lower_tokens[row, level] = lax.ppermute(row_tokens[row], "seq", pairs)

    raise_tokens(0)
    queries, keyval, *later = order.call(project_own, tokens, first_gain, first_shift, attend_weight, attend_bias)
    row_tokens += later
    for row in range(1, rows):
        raise_tokens(row)
    mate_keyval = swap(keyval)
    lifted, prefix_keyval = order.call(prefix_forward, prefix_table, lift_weight, lift_bias, fan_weight, fan_bias)
    blocks = lower(0)
    order.call(mark)
    waiting = []
    finished_rows = 0
    for row in range(rows):
        last_row = row + 1 == rows
        row_activations, grad_residual, grad_query, *grads, prefix_grad = order.call(
            row_block, place, row_lengths, source_lengths, queries, tokens, cotangent, prefix_keyval,
            keyvals_of(blocks), weights, row, prefix_grad, (attend_weight,),
        )
        received = None if last_row else swap(grads[1])
        from_mates = [swap(grads[2 * level + 1]) for level in levels]
        if last_row:
            if hops is None:
                prefix_grad = lax.psum(prefix_grad, ("seq", "dp"))
            hop()
            for earlier in waiting:
                earlier()
                hop()
            received = swap(order.call(hold, grads[1]))
        else:
            blocks = lower(row + 1)
        above = []
        for level in levels:
            part = order.call(up_back, grads[2 * level], from_mates[level - 1], attend_weight)
            above.append(lax.ppermute(part, "seq", [(at + 2 * level, at) for at in range(seq - 2 * level)]))
        total = order.call(project_back, grad_query, grads[0], received, attend_weight)

        def end(row=row, grad_residual=grad_residual, total=total, row_activations=row_activations, above=above):
            nonlocal finished, finished_rows
            finished_rows += 1
            finished = order.call(finish, tokens, first_gain, grad_residual, total, row_activations, above, row, finished)

        waiting.append(end)
    while hops or arriving is not None:
        hop()
        if arriving is not None:
            if hops:
                order.call(mark)
            else:
                waiting[-1]()
    grad_table, grad_lift, grad_lift_bias, grad_fan, grad_fan_bias = order.call(
        prefix_network_back, prefix_grad, prefix_table, lift_weight, fan_weight, lifted
    )
    if finished_rows < rows:
        waiting[-1]()
    return (*finished, grad_table, grad_lift, grad_lift_bias.reshape(-1), grad_fan, grad_fan_bias.reshape(-1))


def solution(mesh):
    batch = P("dp", "seq", None)
    return jax.shard_map(
        per_device,
        mesh=mesh,
        in_specs=(batch, batch, P("dp"), P("dp")) + (P(),) * 17,
        out_specs=(batch, batch, P(), P(), P(), P(), P()),
        check_vma=False,
    )
```

```python
import functools

import jax
import jax.numpy as jnp
from jax import lax
from jax.experimental import pallas as pl
from jax.experimental.pallas import tpu as pltpu
from jax.sharding import PartitionSpec as P

D = 1024
HEADS = 16
HEAD_DIM = 64
PAIRS = HEADS // 2
PREFIX = 10
PREFIX_PAD = 16
LEAST_LENGTH = 512
NN = (((1,), (0,)), ((), ()))
NT = (((1,), (1,)), ((), ()))
MIB = 1 << 20
BF16 = jnp.bfloat16
F32 = jnp.float32


def dot(left, right, dims=NN):
    return lax.dot_general(left, right, dims, preferred_element_type=F32)


ANY = pl.BlockSpec(memory_space=pl.ANY)


VMEM = pl.BlockSpec(memory_space=pltpu.VMEM)
COVER = pl.CostEstimate(flops=10**10, bytes_accessed=10**9, transcendentals=0)
TOKEN = jax.ShapeDtypeStruct((8, 128), F32)


def kernel_call(kernel, after, operands, limit, in_specs, out_specs, out_shape, prefetched=0, scratch_shapes=(), warm=(), **rest):
    lead = prefetched + len(in_specs)

    def body(*refs):
        outs = lead + len(after) + len(warm)
        token_ref = refs[outs + len(out_shape)]
        token_ref[...] = jnp.zeros_like(token_ref)
        kernel(*refs[:lead], *refs[outs : outs + len(out_shape)], *refs[outs + len(out_shape) + 1 :])

    spec = pltpu.PrefetchScalarGridSpec(
        num_scalar_prefetch=prefetched,
        grid=(1,),
        in_specs=[*in_specs] + [ANY] * len(after) + [VMEM] * len(warm),
        out_specs=[*out_specs, VMEM],
        scratch_shapes=scratch_shapes,
    )
    return pl.pallas_call(
        body,
        grid_spec=spec,
        out_shape=[*(jax.ShapeDtypeStruct(out.shape, out.dtype) for out in out_shape), TOKEN],
        compiler_params=pltpu.CompilerParams(dimension_semantics=("arbitrary",), vmem_limit_bytes=limit * MIB),
        cost_estimate=COVER,
        **rest,
    )(*operands, *after, *warm)


def split(values):
    high = values.astype(BF16)
    return high, (values - high.astype(F32)).astype(BF16)


class Copies:
    def __init__(self, semaphores):
        self.semaphores = semaphores
        self.count = 0
        self.copies = {}

    def start(self, name, source, target):
        copy = pltpu.make_async_copy(source, target, self.semaphores.at[self.count])
        copy.start()
        self.count += 1
        self.copies[name] = copy

    def wait(self, name):
        self.copies[name].wait()


HBM = pl.BlockSpec(memory_space=pltpu.HBM)


def normalize(values):
    centred = values - jnp.mean(values, axis=-1, keepdims=True)
    scale = lax.rsqrt(jnp.mean(centred * centred, axis=-1, keepdims=True) + 1e-05)
    return centred * scale, scale


def norm_back(grad, normed, scale):
    return scale * (
        grad
        - jnp.mean(grad, axis=-1, keepdims=True)
        - normed * jnp.mean(grad * normed, axis=-1, keepdims=True)
    )


def first_row_kernel(tokens_ref, row_ref, semaphores):
    copies = Copies(semaphores)
    copies.start(0, tokens_ref.at[pl.ds(0, 1)], row_ref)
    copies.wait(0)


def first_row(after, tokens):
    _, toks, _ = tokens.shape
    return kernel_call(
        first_row_kernel,
        after,
        (tokens,),
        1,
        [ANY],
        [VMEM],
        [jax.ShapeDtypeStruct((1, toks, D), BF16)],
        scratch_shapes=[pltpu.SemaphoreType.DMA((1,))],
        name="first_row",
    )


def project_own_kernel(tokens_ref, gain_ref, shift_ref, bias_ref, weight_ref, query_ref, keyval_ref, *rest):
    later_refs, normed_ref = rest[:-1], rest[-1]
    rows, toks, _ = tokens_ref.shape
    for at, later_ref in enumerate(later_refs):
        later_ref[0] = tokens_ref[at + 1]
    normed, _ = normalize(tokens_ref[...].reshape(rows * toks, D).astype(F32))
    normed_ref[...] = (normed * gain_ref[...] + shift_ref[...]).astype(BF16)
    chunk = D // 2
    for at in range(6):
        span = slice(at * chunk, (at + 1) * chunk)
        result = (dot(normed_ref[...], weight_ref[:, span]) + bias_ref[:, span]).astype(BF16)
        cols = slice(at % 2 * chunk, (at % 2 + 1) * chunk)
        if at < 2:
            query_ref[:, :, cols] = (result * 0.125).reshape(rows, toks, chunk)
        else:
            keyval_ref[:, at // 2 - 1, :, cols] = result.reshape(rows, toks, chunk)


def project_own(after, tokens, gain, shift, weight, bias):
    rows, toks, _ = tokens.shape
    return kernel_call(
        project_own_kernel,
        after,
        (tokens, gain, shift, bias, weight),
        14,
        [VMEM] * 5,
        [VMEM] * (1 + rows),
        [jax.ShapeDtypeStruct((rows, toks, D), BF16), jax.ShapeDtypeStruct((rows, 2, toks, D), BF16)]
        + [jax.ShapeDtypeStruct((1, toks, D), BF16)] * (rows - 1),
        scratch_shapes=[pltpu.VMEM((rows * toks, D), BF16)],
        name="project_own",
    )


def project_up_kernel(tokens_ref, gain_ref, shift_ref, bias_ref, weight_ref, keyval_ref):
    toks = tokens_ref.shape[1]
    normed, _ = normalize(tokens_ref[0].astype(F32))
    normed = (normed * gain_ref[...] + shift_ref[...]).astype(BF16)
    for half in range(2):
        cols = slice((half + 1) * D, (half + 2) * D)
        keyval_ref[0, half] = (dot(normed, weight_ref[:, cols]) + bias_ref[:, cols]).astype(BF16)


def project_up(after, tokens, gain, shift, weight, bias, warm=()):
    toks = tokens.shape[1]
    return kernel_call(
        project_up_kernel,
        after,
        (tokens, gain, shift, bias, weight),
        10,
        [VMEM] * 5,
        [VMEM],
        [jax.ShapeDtypeStruct((1, 2, toks, D), BF16)],
        warm=warm,
        name="project_up",
    )


def head_lanes(values, head):
    lanes = lax.broadcasted_iota(jnp.int32, values.shape, 1)
    keep = lanes < HEAD_DIM if head == 0 else lanes >= HEAD_DIM
    return jnp.where(keep, values, jnp.zeros_like(values))


def prefix_mask(values, fill):
    places = lax.broadcasted_iota(jnp.int32, values.shape, 0)
    return jnp.where(places < PREFIX, values, fill)


class Places:
    def __init__(self, toks, level_count):
        self.toks = toks
        self.level_count = level_count

    def masked(self, block):
        if block < 2:
            return True
        level = block // 2
        return (self.level_count - level) * 2 * self.toks > LEAST_LENGTH

    def limits(self, place, length):
        base = place * self.toks
        queries = base + lax.broadcasted_iota(jnp.int32, (1, self.toks), 1)
        return jnp.minimum(queries, length - 1)

    def visible(self, block, place, limit):
        if block == 0:
            base = place * self.toks
        else:
            base = (lax.bitwise_xor(place, block % 2) - (block // 2) * 2) * self.toks
        keys = lax.broadcasted_iota(jnp.int32, (self.toks, self.toks), 0)
        return keys <= limit - base


def spread_prefix(prefix):
    tiled = jnp.concatenate([prefix] * HEADS, axis=0)
    rows = lax.broadcasted_iota(jnp.int32, tiled.shape, 0) // PREFIX_PAD
    cols = lax.broadcasted_iota(jnp.int32, tiled.shape, 1) // HEAD_DIM
    return jnp.where(rows == cols, tiled, jnp.zeros_like(tiled))


GELU_SCALE = 0.7978845608028654
GELU_CUBE = 0.044715
FAR = 1e30
ROW_LIMIT = 30


PACKED = (8, 2 * D + D // 2)


def pack_prefix(ref, halves):
    for half, values in enumerate(halves):
        ref[:, half * D : (half + 1) * D] = values[:8]
        for row in range(8, PREFIX):
            for part in range(2):
                at = (half * (PREFIX - 8) + row - 8) * 2 + part
                ref[at : at + 1, 2 * D :] = values[row : row + 1, part * (D // 2) : (part + 1) * (D // 2)]


def unpack_prefix(ref, half):
    rest = jnp.concatenate([ref[:, 2 * D :], jnp.zeros((8, D // 2), F32)], axis=0)
    rows = []
    for row in range(8, PREFIX):
        at = (half * (PREFIX - 8) + row - 8) * 2
        rows.append(jnp.concatenate([rest[at : at + 1], rest[at + 1 : at + 2]], axis=1))
    rows.append(jnp.zeros((PREFIX_PAD - PREFIX, D), F32))
    return jnp.concatenate([ref[:, half * D : (half + 1) * D]] + rows, axis=0)


class RowRefs:
    def __init__(self, names, refs):
        for name, ref in zip(names, refs):
            setattr(self, name, ref)


def column_group(group, width):
    return pl.ds(pl.multiple_of(group * width, width), width)


def attend_rows(places, refs, place, limit, pair_step):
    blocks = range(2 * places.level_count)
    masked_blocks = [block for block in blocks if places.masked(block)]
    level = place // 2
    width = 128 * pair_step
    refs.prefix_scores[...] = dot(refs.spread[0], refs.query[...], NT)
    for at, block in enumerate(masked_blocks):
        refs.hide[at] = jnp.where(places.visible(block, place, limit), 0.0, -jnp.inf)

    def beyond(block):
        return jnp.where(level >= block // 2, 0.0, FAR) if block > 1 else None

    def body(group, carry):
        span = column_group(group, width)
        group_queries = refs.query[:, span]
        group_keys = [refs.keyval(block, 0, span) for block in blocks]

        def scores_of(at):
            pair, head = at // 2, at % 2
            cols = slice(pair * 128, (pair + 1) * 128)
            queries = head_lanes(group_queries[:, cols], head)
            spot = pl.multiple_of((group * pair_step * 2 + at) * PREFIX_PAD, PREFIX_PAD)
            prefix_scores = prefix_mask(refs.prefix_scores[pl.ds(spot, PREFIX_PAD), :], -jnp.inf)
            highest = jnp.max(prefix_scores, axis=0, keepdims=True)
            scores = []
            for block in blocks:
                part = dot(group_keys[block][:, cols], queries, NT)
                if block in masked_blocks:
                    part = part + refs.hide[masked_blocks.index(block)]
                top = jnp.max(part, axis=0, keepdims=True)
                if block > 1:
                    top = top - beyond(block)
                highest = jnp.maximum(highest, top)
                scores.append(part)
            return prefix_scores, scores, highest

        ahead = scores_of(0)
        for at in range(2 * pair_step):
            pair, head = at // 2, at % 2
            cols = slice(pair * 128, (pair + 1) * 128)
            prefix_scores, scores, highest = ahead
            if at + 1 < 2 * pair_step:
                ahead = scores_of(at + 1)
            if head == 0:
                values_t = [refs.keyval(block, 1, span)[:, cols].T for block in blocks]
                prefix_values_t = refs.prefix[1, :, span][:, cols].T
                ones = jnp.ones((PREFIX_PAD, values_t[0].shape[1]), BF16)
                outs = []
            rows = slice(head * HEAD_DIM, (head + 1) * HEAD_DIM)
            prefix_weights = jnp.exp(prefix_scores - highest)
            total = jnp.sum(prefix_weights, axis=0, keepdims=True)
            mixed = dot(prefix_values_t[rows], prefix_weights.astype(BF16))
            for block in blocks:
                base = highest + beyond(block) if block > 1 else highest
                weights = jnp.exp(scores[block] - base)
                part = dot(jnp.concatenate([values_t[block][rows], ones], axis=0), weights.astype(BF16))
                total = total + part[HEAD_DIM : HEAD_DIM + 1]
                mixed = mixed + part[:HEAD_DIM]
            outs.append(mixed * (1.0 / total))
            refs.total[group, at : at + 1, :] = highest + jnp.log(total)
            if head == 1:
                refs.mixed[:, pl.ds(pl.multiple_of(group * width + pair * 128, 128), 128)] = jnp.concatenate(outs, axis=0).T.astype(BF16)
        return carry

    lax.fori_loop(0, PAIRS // pair_step, body, 0)


def feed_rows(refs, place, length, source, weight_copies, chunks, chunk, slots):
    toks = refs.tokens.shape[0]
    spots = place * toks + lax.broadcasted_iota(jnp.int32, (toks, D), 0)
    target = (spots >= source) & (spots < length)
    refs.grad_out[...] = jnp.where(target, refs.cotangent[...].astype(F32), 0.0).astype(BF16)
    residual = refs.tokens[...].astype(F32) + dot(refs.mixed[...], refs.output_weight[...]) + refs.output_bias[...]
    refs.residual[...] = residual
    normed, _ = normalize(residual)
    refs.normed[...] = (normed * refs.second_gain[...] + refs.second_shift[...]).astype(BF16)

    def first(at, slot):
        for copy in weight_copies(at):
            copy.wait()
        bias = refs.expand_bias[:, pl.ds(pl.multiple_of(at * chunk, chunk), chunk)]
        values = dot(refs.normed[...], refs.expand_weight[at % slots]) + bias
        grad_hidden = dot(refs.grad_out[...], refs.contract_weight[at % slots], NT)
        square = values * values
        bend = jnp.tanh(values * (GELU_SCALE + GELU_SCALE * GELU_CUBE * square))
        half = 0.5 + 0.5 * bend
        slope = half + (0.5 * values) * (1.0 - bend * bend) * (
            GELU_SCALE + 3.0 * GELU_SCALE * GELU_CUBE * square
        )
        refs.active[slot] = (values * half).astype(BF16)
        refs.grad_expand[slot] = (grad_hidden * slope).astype(BF16)

    def second(at, slot):
        refs.result[...] += dot(refs.active[slot], refs.contract_weight[at % slots])
        refs.grad_normed[...] += dot(refs.grad_expand[slot], refs.expand_weight[at % slots], NT)

    def refill(at):
        @pl.when(at + slots < chunks)
        def _():
            for copy in weight_copies(at + slots):
                copy.start()

    refs.result[...] = jnp.zeros_like(refs.result)
    refs.grad_normed[...] = jnp.zeros_like(refs.grad_normed)
    first(0, 0)

    def body(at, carry):
        first(2 * at + 1, 1)
        second(2 * at, 0)
        refill(2 * at)
        first(2 * at + 2, 0)
        second(2 * at + 1, 1)
        refill(2 * at + 1)
        return carry

    lax.fori_loop(0, chunks // 2 - 1, body, 0)
    first(chunks - 1, 1)
    second(chunks - 2, 0)
    second(chunks - 1, 1)

    residual = refs.residual[...]
    refs.activations[...] = (residual + refs.result[...] + refs.contract_bias[...]).astype(BF16)
    normed, scale = normalize(residual)
    grad = refs.grad_out[...].astype(F32) + norm_back(refs.grad_normed[...] * refs.second_gain[...], normed, scale)
    refs.grad_residual[0] = grad
    refs.grad_heads[...] = dot(grad.astype(BF16), refs.output_weight[...], NT).astype(BF16)


def prefix_back_rows(refs):
    toks = refs.query.shape[0]
    queries = refs.query[...]
    grads = refs.grad_heads[...]
    product = grads.astype(F32) * refs.mixed[...].astype(F32)
    head_of = lax.broadcasted_iota(jnp.int32, (HEADS, D), 1) // HEAD_DIM
    chosen = jnp.where(head_of == lax.broadcasted_iota(jnp.int32, (HEADS, D), 0), 1.0, 0.0).astype(BF16)
    high, low = split(product)
    inner = dot(chosen, high, NT) + dot(chosen, low, NT)
    refs.inner[...] = inner.reshape(refs.inner.shape)

    def per_head(values):
        return values.reshape(HEADS, PREFIX_PAD, toks)

    scores = per_head(refs.prefix_scores[...])
    grad_weights = per_head(dot(refs.spread[1], grads, NT))
    weights = jnp.exp(scores - refs.total[...].reshape(HEADS, 1, toks))
    valid = lax.broadcasted_iota(jnp.int32, weights.shape, 1) < PREFIX
    weights = jnp.where(valid, weights, 0.0)
    grad_scores = weights * (grad_weights - inner[:, None, :])
    weights = weights.reshape(HEADS * PREFIX_PAD, toks).astype(BF16)
    grad_scores = grad_scores.reshape(HEADS * PREFIX_PAD, toks).astype(BF16)
    refs.result[...] = dot(grad_scores.T, refs.spread[0])
    own = (
        lax.broadcasted_iota(jnp.int32, (HEADS * PREFIX_PAD, D), 0) // PREFIX_PAD
        == lax.broadcasted_iota(jnp.int32, (HEADS * PREFIX_PAD, D), 1) // HEAD_DIM
    )

    def gather(values):
        return jnp.sum(jnp.where(own, values, 0.0).reshape(HEADS, PREFIX_PAD, D), axis=0)

    sums = gather(dot(grad_scores, queries)), gather(dot(weights, grads))
    pack_prefix(refs.prefix_grad, sums)
    refs.prefix_grad[...] += refs.earlier_grad[...]


def attend_back_rows(places, refs, place, pair_step):
    blocks = range(2 * places.level_count)
    masked_blocks = [block for block in blocks if places.masked(block)]
    level = place // 2
    width = 128 * pair_step

    def body(group, carry):
        span = column_group(group, width)
        group_queries = refs.query[:, span]
        group_grads = refs.grad_heads[:, span]
        group_keys = [refs.keyval(block, 0, span) for block in blocks]
        group_values = [refs.keyval(block, 1, span) for block in blocks]

        sides = {}

        def side(at):
            if at not in sides:
                cols = slice(at // 2 * 128, (at // 2 + 1) * 128)
                sides[at] = head_lanes(group_queries[:, cols], at % 2), head_lanes(group_grads[:, cols], at % 2)
            return sides[at]

        def products_of(item):
            at, block = item
            cols = slice(at // 2 * 128, (at // 2 + 1) * 128)
            queries, grads = side(at)
            part = dot(group_keys[block][:, cols], queries, NT)
            if block in masked_blocks:
                part = part + refs.hide[masked_blocks.index(block)]
            return part, dot(group_values[block][:, cols], grads, NT)

        items = [(at, block) for at in range(2 * pair_step) for block in blocks]
        ahead = [products_of(item) for item in items[:2]]
        for spot, (at, block) in enumerate(items):
            pair, head = at // 2, at % 2
            cols = slice(pair * 128, (pair + 1) * 128)
            place_cols = pl.ds(pl.multiple_of(group * width + pair * 128, 128), 128)
            scores, grad_weights = ahead.pop(0)
            if spot + 2 < len(items):
                ahead.append(products_of(items[spot + 2]))
            queries, grads = side(at)
            if block == 0:
                if head == 0:
                    keys_t = [keys[:, cols].T for keys in group_keys]
                    grad_keys, grad_values, outs = [], [], []
                total = refs.total[group, at : at + 1, :]
                inner = refs.inner[group, at : at + 1, :]
                grad_query = None
            rows = slice(head * HEAD_DIM, (head + 1) * HEAD_DIM)
            base = total + jnp.where(level >= block // 2, 0.0, FAR) if block > 1 else total
            weights = jnp.exp(scores - base)
            grad_scores = (weights * (grad_weights - inner)).astype(BF16)
            part_values = dot(weights.astype(BF16), grads)
            part_keys = dot(grad_scores, queries)
            part_query = dot(keys_t[block][rows], grad_scores)
            if head == 0:
                grad_values.append(part_values)
                grad_keys.append(part_keys)
            else:
                refs.grad_keyval[block][0, 0, :, place_cols] = (grad_keys[block] + part_keys).astype(BF16)
                refs.grad_keyval[block][0, 1, :, place_cols] = (grad_values[block] + part_values).astype(BF16)
            grad_query = part_query if grad_query is None else grad_query + part_query
            if block == blocks[-1]:
                outs.append(grad_query)
                if head == 1:
                    grad_query = jnp.concatenate(outs, axis=0).T + refs.result[:, place_cols]
                    refs.grad_query[0, :, place_cols] = (grad_query * 0.125).astype(BF16)
        return carry

    lax.fori_loop(0, PAIRS // pair_step, body, 0)


ROW_NAMES = (
    "expand_weight", "contract_weight", "spread", "prefix_scores", "hide", "total",
    "mixed", "grad_out", "residual", "normed", "active", "grad_expand", "result", "grad_normed",
    "grad_heads", "inner",
)


def row_kernel(places, keyval_rows, pair_step, chunk, row_ref, place_ref, length_ref, source_ref, *rest):
    block_count = 2 * places.level_count
    row = row_ref[0]
    query_ref, tokens_ref, cotangent_ref, prefix_ref = rest[:4]
    keyval_refs = rest[4 : 4 + block_count]
    rest = rest[4 + block_count :]
    output_weight_ref, expand_weight_hbm, contract_weight_hbm = rest[:3]
    vectors = rest[3:8]
    earlier_grad_ref = rest[8]
    rest = rest[9:]
    activations_ref, grad_residual_ref, grad_query_ref = rest[:3]
    grad_keyval_refs = rest[3 : 3 + block_count]
    prefix_grad_ref = rest[3 + block_count]
    rest = rest[4 + block_count :]
    refs = RowRefs(ROW_NAMES, rest)
    refs.output_bias, refs.second_gain, refs.second_shift, refs.expand_bias, refs.contract_bias = vectors
    refs.prefix_grad, refs.earlier_grad = prefix_grad_ref, earlier_grad_ref
    refs.activations = activations_ref.at[0]
    refs.query, refs.prefix = query_ref.at[row], prefix_ref
    refs.keyval = lambda block, half, span: keyval_refs[block][row if keyval_rows[block] is None else keyval_rows[block], half, :, span]
    refs.grad_residual, refs.grad_query, refs.grad_keyval = grad_residual_ref, grad_query_ref, grad_keyval_refs
    (weight_semaphores,) = rest[len(ROW_NAMES) :]
    slots = refs.expand_weight.shape[0]
    chunks = expand_weight_hbm.shape[1] // chunk

    refs.output_weight, refs.tokens, refs.cotangent = output_weight_ref, tokens_ref.at[row], cotangent_ref.at[row]

    def weight_copies(at):
        span = pl.ds(pl.multiple_of(at * chunk, chunk), chunk)
        return (
            pltpu.make_async_copy(expand_weight_hbm.at[:, span], refs.expand_weight.at[at % slots], weight_semaphores.at[at]),
            pltpu.make_async_copy(contract_weight_hbm.at[span, :], refs.contract_weight.at[at % slots], weight_semaphores.at[chunks + at]),
        )

    def start_weights(at, carry):
        for copy in weight_copies(at):
            copy.start()
        return carry

    lax.fori_loop(0, slots, start_weights, 0)
    place = place_ref[0]
    length = length_ref[row]
    limit = places.limits(place, length)
    for half in range(2):
        refs.spread[half] = spread_prefix(refs.prefix[half])
    attend_rows(places, refs, place, limit, pair_step)
    feed_rows(refs, place, length, source_ref[row], weight_copies, chunks, chunk, slots)
    prefix_back_rows(refs)
    attend_back_rows(places, refs, place, pair_step)


def row_block(after, place, lengths, sources, queries, tokens, cotangent, prefix_keyval, keyvals, weights, row, earlier_grad, warm=(), pair_step=4, chunk=512, slots=3):
    toks = queries.shape[1]
    block_count = len(keyvals)
    places = Places(toks, block_count // 2)
    output_weight, output_bias, gain, shift, expand_weight, expand_bias, contract_weight, contract_bias = weights
    hidden = expand_weight.shape[1]
    chunks = hidden // chunk
    masked = sum(places.masked(block) for block in range(block_count))
    per_group = 2 * pair_step
    scratch = dict(
        expand_weight=((slots, D, chunk), BF16), contract_weight=((slots, chunk, D), BF16),
        spread=((2, HEADS * PREFIX_PAD, D), BF16), prefix_scores=((HEADS * PREFIX_PAD, toks), F32),
        hide=((masked, toks, toks), F32), total=((HEADS // per_group, per_group, toks), F32), mixed=((toks, D), BF16),
        grad_out=((toks, D), BF16), residual=((toks, D), F32), normed=((toks, D), BF16),
        active=((2, toks, chunk), BF16), grad_expand=((2, toks, chunk), BF16), result=((toks, D), F32),
        grad_normed=((toks, D), F32),
        grad_heads=((toks, D), BF16), inner=((HEADS // per_group, per_group, toks), F32),
    )
    return kernel_call(
        functools.partial(row_kernel, places, [at for _, at in keyvals], pair_step, chunk),
        after,
        (
            jnp.full((1,), row, jnp.int32), place, lengths, sources, queries, tokens, cotangent, prefix_keyval, *[array for array, _ in keyvals],
            output_weight, expand_weight, contract_weight, output_bias, gain, shift, expand_bias, contract_bias, earlier_grad,
        ),
        ROW_LIMIT,
        [VMEM] * (4 + block_count) + [VMEM, HBM, HBM] + [VMEM] * 6,
        [VMEM] * (4 + block_count),
        [
            jax.ShapeDtypeStruct((1, toks, D), BF16),
            jax.ShapeDtypeStruct((1, toks, D), F32),
            jax.ShapeDtypeStruct((1, toks, D), BF16),
        ]
        + [jax.ShapeDtypeStruct((1, 2, toks, D), BF16)] * block_count
        + [jax.ShapeDtypeStruct(PACKED, F32)],
        prefetched=4,
        scratch_shapes=[pltpu.VMEM(*scratch[name]) for name in ROW_NAMES]
        + [pltpu.SemaphoreType.DMA((2 * chunks,))],
        warm=warm,
        name="row_block",
    )


def up_back_kernel(own_ref, received_ref, weight_ref, grad_ref):
    total = None
    for half in range(2):
        values = (own_ref[0, half].astype(F32) + received_ref[0, half].astype(F32)).astype(BF16)
        part = dot(values, weight_ref[:, (half + 1) * D : (half + 2) * D], NT)
        total = part if total is None else total + part
    grad_ref[0] = total.astype(BF16)


def up_back(after, own, received, weight):
    toks = own.shape[2]
    return kernel_call(
        up_back_kernel,
        after,
        (own, received, weight),
        10,
        [VMEM] * 3,
        [VMEM],
        [jax.ShapeDtypeStruct((1, toks, D), BF16)],
        name="up_back",
    )


def project_back_kernel(query_ref, own_ref, received_ref, weight_ref, total_ref):
    total = dot(query_ref[0], weight_ref[:, :D], NT)
    for half in range(2):
        values = (own_ref[0, half].astype(F32) + received_ref[0, half].astype(F32)).astype(BF16)
        total = total + dot(values, weight_ref[:, (half + 1) * D : (half + 2) * D], NT)
    total_ref[0] = total


def project_back(after, grad_query, own, received, weight):
    toks = grad_query.shape[1]
    return kernel_call(
        project_back_kernel,
        after,
        (grad_query, own, received, weight),
        10,
        [VMEM] * 4,
        [VMEM],
        [jax.ShapeDtypeStruct((1, toks, D), F32)],
        name="project_back",
    )


def finish_kernel(above_count, row, tokens_ref, gain_ref, residual_ref, total_ref, activations_ref, *rest):
    activations_hbm, grad_hbm, grad_ref, semaphores = rest[-4:]
    toks = grad_ref.shape[0]
    copies = Copies(semaphores)
    copies.start("activations", activations_ref.at[0], activations_hbm.at[row])
    parts = 2
    for part in range(parts):
        span = pl.ds(part * (toks // parts), toks // parts)
        total = total_ref[0, span]
        for above_ref in rest[:above_count]:
            total = total + above_ref[0, span].astype(F32)
        normed, scale = normalize(tokens_ref[row, span].astype(F32))
        grad_ref[span] = residual_ref[0, span] + norm_back(total * gain_ref[...], normed, scale)
        copies.start(part, grad_ref.at[span], grad_hbm.at[row, span])
    for part in range(parts):
        copies.wait(part)
    copies.wait("activations")


def finish(after, tokens, gain, grad_residual, total, activations, above, row, earlier):
    toks = tokens.shape[1]
    return kernel_call(
        functools.partial(finish_kernel, len(above), row),
        after,
        (tokens, gain, grad_residual, total, activations, *above, *earlier),
        10,
        [VMEM] * (5 + len(above)) + [ANY] * len(earlier),
        [HBM] * 2,
        [jax.ShapeDtypeStruct(tokens.shape, BF16), jax.ShapeDtypeStruct(tokens.shape, F32)],
        scratch_shapes=[pltpu.VMEM((toks, D), F32), pltpu.SemaphoreType.DMA((3,))],
        input_output_aliases={5 + len(above) + at: at for at in range(len(earlier))},
        name="finish",
    )


def prefix_kernel(table_ref, lift_ref, lift_bias_ref, fan_ref, fan_bias_ref, lifted_ref, keyval_ref):
    lifted = jnp.tanh(dot(table_ref[...], lift_ref[...]) + lift_bias_ref[...])
    lifted_ref[...] = jnp.zeros_like(lifted_ref)
    lifted_ref[:PREFIX, :] = lifted
    keyval_ref[...] = jnp.zeros_like(keyval_ref)
    keyval = (dot(lifted.astype(BF16), fan_ref[...]) + fan_bias_ref[...]).astype(BF16)
    keyval_ref[0, :PREFIX, :] = keyval[:, :D]
    keyval_ref[1, :PREFIX, :] = keyval[:, D:]


def prefix_forward(after, table, lift, lift_bias, fan, fan_bias):
    return kernel_call(
        prefix_kernel,
        after,
        (table, lift, lift_bias, fan, fan_bias),
        8,
        [VMEM] * 5,
        [VMEM] * 2,
        [
            jax.ShapeDtypeStruct((PREFIX_PAD, lift.shape[1]), F32),
            jax.ShapeDtypeStruct((2, PREFIX_PAD, D), BF16),
        ],
        name="prefix_forward",
    )


def prefix_network_back_kernel(grad_ref, table_ref, lift_ref, fan_ref, lifted_ref, grad_table_ref, grad_lift_ref, grad_lift_bias_ref, grad_fan_ref, grad_fan_bias_ref):
    lifted = lifted_ref[...]
    lifted_t = jnp.concatenate([lifted.astype(BF16)] * 2, axis=0).T
    grad_lifted = None
    for half in range(2):
        cols = slice(half * D, (half + 1) * D)
        grad = unpack_prefix(grad_ref, half)
        grad_fan_bias_ref[:, cols] = jnp.sum(grad, axis=0, keepdims=True)
        both = jnp.concatenate(split(grad), axis=0)
        grad_fan_ref[:, cols] = dot(lifted_t, both)
        part = dot(both, fan_ref[:, cols], NT)
        grad_lifted = part if grad_lifted is None else grad_lifted + part
    grad_lifted = (grad_lifted[:PREFIX_PAD] + grad_lifted[PREFIX_PAD:]) * (1.0 - lifted * lifted)
    grad_lift_bias_ref[...] = jnp.sum(grad_lifted, axis=0, keepdims=True)
    both = jnp.concatenate(split(grad_lifted), axis=0)
    table = jnp.concatenate([table_ref[...].astype(F32), jnp.zeros((PREFIX_PAD - PREFIX, D), F32)], axis=0)
    table_t = jnp.concatenate([table.astype(BF16)] * 2, axis=0).T
    grad_lift_ref[...] = dot(table_t, both)
    grad_table = dot(both, lift_ref[...], NT)
    grad_table_ref[...] = (grad_table[:PREFIX_PAD] + grad_table[PREFIX_PAD:])[:PREFIX]


def prefix_network_back(after, grad, table, lift, fan, lifted):
    hidden = lift.shape[1]
    return kernel_call(
        prefix_network_back_kernel,
        after,
        (grad, table, lift, fan, lifted),
        20,
        [VMEM] * 5,
        [VMEM] * 5,
        [
            jax.ShapeDtypeStruct((PREFIX, D), F32),
            jax.ShapeDtypeStruct((D, hidden), F32),
            jax.ShapeDtypeStruct((1, hidden), F32),
            jax.ShapeDtypeStruct((hidden, 2 * D), F32),
            jax.ShapeDtypeStruct((1, 2 * D), F32),
        ],
        name="prefix_network_back",
    )


def add_kernel(*refs):
    total = refs[0][...]
    for ref in refs[1:-1]:
        total = total + ref[...]
    refs[-1][...] = total


def add(after, *values):
    return kernel_call(add_kernel, after, values, 2, [VMEM] * len(values), [VMEM], values[:1], name="add")


def mark_kernel(*refs):
    pass


def mark(after, warm=()):
    return kernel_call(mark_kernel, after, (), 8, [], [], [], warm=warm, name="mark")


def hold(after, array):
    return kernel_call(mark_kernel, after, (array,), 1, [ANY], [ANY], [array], input_output_aliases={0: 0}, name="hold")


class Order:
    def __init__(self):
        self.before = ()

    def call(self, kernel, *operands):
        *outs, token = kernel(self.before, *operands)
        self.before = (token,)
        return outs[0] if len(outs) == 1 else outs


def sum_stages():
    stages = []
    for axis, most in (("seq", 1), ("dp", 2)):
        size = lax.axis_size(axis)
        if size & (size - 1):
            return None
        hop = 1
        while hop < size:
            bits = most if hop > 1 and hop * 2 < size else 1
            stages.append((axis, [[(at, at ^ (hop * step)) for at in range(size)] for step in range(1, 2**bits)]))
            hop *= 2**bits
    return stages


def per_device(tokens, cotangent, row_lengths, source_lengths, first_gain, first_shift, attend_weight, attend_bias, output_weight, output_bias, second_gain, second_shift, expand_weight, expand_bias, contract_weight, contract_bias, prefix_table, lift_weight, lift_bias, fan_weight, fan_bias):
    rows = tokens.shape[0]
    seq = lax.axis_size("seq")
    level_count = seq // 2
    levels = range(1, level_count)
    mates = [(at, at ^ 1) for at in range(seq)]
    place = lax.axis_index("seq").astype(jnp.int32).reshape(1)
    first_gain, first_shift, attend_bias, output_bias, second_gain, second_shift, expand_bias, contract_bias, lift_bias, fan_bias = [
        vector.reshape(1, -1)
        for vector in (first_gain, first_shift, attend_bias, output_bias, second_gain, second_shift, expand_bias, contract_bias, lift_bias, fan_bias)
    ]
    weights = (output_weight, output_bias, second_gain, second_shift, expand_weight, expand_bias, contract_weight, contract_bias)
    order = Order()
    hops = sum_stages()
    finished = ()
    prefix_grad = jnp.zeros(PACKED, F32)
    arriving = None

    def swap(array):
        return lax.ppermute(array, "seq", mates)

    def hop():
        nonlocal prefix_grad, arriving
        if arriving is not None:
            prefix_grad = order.call(add, prefix_grad, *arriving)
            arriving = None
        if hops:
            axis, partners = hops.pop(0)
            arriving = [lax.ppermute(prefix_grad, axis, pairs) for pairs in partners]

    def lower(row):
        blocks = []
        for level in levels:
            block = order.call(project_up, lower_tokens[row, level], first_gain, first_shift, attend_weight, attend_bias, (queries, cotangent) if row == 0 else ())
            blocks += [block, swap(block)]
        return blocks

    def keyvals_of(blocks):
        return [(keyval, None), (mate_keyval, None)] + [(block, 0) for block in blocks]

    row_tokens = [order.call(first_row, tokens)]
    lower_tokens = {}

    def raise_tokens(row):
        for level in levels:
            pairs = [(at, at + 2 * level) for at in range(seq - 2 * level)]
            lower_tokens[row, level] = lax.ppermute(row_tokens[row], "seq", pairs)

    raise_tokens(0)
    queries, keyval, *later = order.call(project_own, tokens, first_gain, first_shift, attend_weight, attend_bias)
    row_tokens += later
    for row in range(1, rows):
        raise_tokens(row)
    mate_keyval = swap(keyval)
    lifted, prefix_keyval = order.call(prefix_forward, prefix_table, lift_weight, lift_bias, fan_weight, fan_bias)
    blocks = lower(0)
    order.call(mark)
    waiting = []
    finished_rows = 0
    for row in range(rows):
        last_row = row + 1 == rows
        row_activations, grad_residual, grad_query, *grads, prefix_grad = order.call(
            row_block, place, row_lengths, source_lengths, queries, tokens, cotangent, prefix_keyval,
            keyvals_of(blocks), weights, row, prefix_grad, (attend_weight,),
        )
        received = None if last_row else swap(grads[1])
        from_mates = [swap(grads[2 * level + 1]) for level in levels]
        if last_row:
            if hops is None:
                prefix_grad = lax.psum(prefix_grad, ("seq", "dp"))
            hop()
            for earlier in waiting:
                earlier()
                hop()
            received = swap(order.call(hold, grads[1]))
        else:
            blocks = lower(row + 1)
        above = []
        for level in levels:
            part = order.call(up_back, grads[2 * level], from_mates[level - 1], attend_weight)
            above.append(lax.ppermute(part, "seq", [(at + 2 * level, at) for at in range(seq - 2 * level)]))
        total = order.call(project_back, grad_query, grads[0], received, attend_weight)

        def end(row=row, grad_residual=grad_residual, total=total, row_activations=row_activations, above=above):
            nonlocal finished, finished_rows
            finished_rows += 1
            finished = order.call(finish, tokens, first_gain, grad_residual, total, row_activations, above, row, finished)

        waiting.append(end)
    while hops or arriving is not None:
        hop()
        if arriving is not None:
            if hops:
                order.call(mark, (lift_weight, fan_weight))
            else:
                waiting[-1]()
    grad_table, grad_lift, grad_lift_bias, grad_fan, grad_fan_bias = order.call(
        prefix_network_back, prefix_grad, prefix_table, lift_weight, fan_weight, lifted
    )
    if finished_rows < rows:
        waiting[-1]()
    return (*finished, grad_table, grad_lift, grad_lift_bias.reshape(-1), grad_fan, grad_fan_bias.reshape(-1))


def solution(mesh):
    batch = P("dp", "seq", None)
    return jax.shard_map(
        per_device,
        mesh=mesh,
        in_specs=(batch, batch, P("dp"), P("dp")) + (P(),) * 17,
        out_specs=(batch, batch, P(), P(), P(), P(), P()),
        check_vma=False,
    )
```

```python
import functools

import jax
import jax.numpy as jnp
from jax import lax
from jax.experimental import pallas as pl
from jax.experimental.pallas import tpu as pltpu
from jax.sharding import PartitionSpec as P

D = 1024
HEADS = 16
HEAD_DIM = 64
PAIRS = HEADS // 2
PREFIX = 10
PREFIX_PAD = 16
LEAST_LENGTH = 512
NN = (((1,), (0,)), ((), ()))
NT = (((1,), (1,)), ((), ()))
MIB = 1 << 20
BF16 = jnp.bfloat16
F32 = jnp.float32


def dot(left, right, dims=NN):
    return lax.dot_general(left, right, dims, preferred_element_type=F32)


ANY = pl.BlockSpec(memory_space=pl.ANY)


VMEM = pl.BlockSpec(memory_space=pltpu.VMEM)
COVER = pl.CostEstimate(flops=10**10, bytes_accessed=10**9, transcendentals=0)
LONG_COVER = pl.CostEstimate(flops=5 * 10**10, bytes_accessed=10**9, transcendentals=0)
TOKEN = jax.ShapeDtypeStruct((8, 128), F32)


def kernel_call(kernel, after, operands, limit, in_specs, out_specs, out_shape, prefetched=0, scratch_shapes=(), warm=(), cover=COVER, **rest):
    lead = prefetched + len(in_specs)

    def body(*refs):
        outs = lead + len(after) + len(warm)
        token_ref = refs[outs + len(out_shape)]
        token_ref[...] = jnp.zeros_like(token_ref)
        kernel(*refs[:lead], *refs[outs : outs + len(out_shape)], *refs[outs + len(out_shape) + 1 :])

    spec = pltpu.PrefetchScalarGridSpec(
        num_scalar_prefetch=prefetched,
        grid=(1,),
        in_specs=[*in_specs] + [ANY] * len(after) + [VMEM] * len(warm),
        out_specs=[*out_specs, VMEM],
        scratch_shapes=scratch_shapes,
    )
    return pl.pallas_call(
        body,
        grid_spec=spec,
        out_shape=[*(jax.ShapeDtypeStruct(out.shape, out.dtype) for out in out_shape), TOKEN],
        compiler_params=pltpu.CompilerParams(dimension_semantics=("arbitrary",), vmem_limit_bytes=limit * MIB),
        cost_estimate=cover,
        **rest,
    )(*operands, *after, *warm)


def split(values):
    high = values.astype(BF16)
    return high, (values - high.astype(F32)).astype(BF16)


class Copies:
    def __init__(self, semaphores):
        self.semaphores = semaphores
        self.count = 0
        self.copies = {}

    def start(self, name, source, target):
        copy = pltpu.make_async_copy(source, target, self.semaphores.at[self.count])
        copy.start()
        self.count += 1
        self.copies[name] = copy

    def wait(self, name):
        self.copies[name].wait()


HBM = pl.BlockSpec(memory_space=pltpu.HBM)


def normalize(values):
    centred = values - jnp.mean(values, axis=-1, keepdims=True)
    scale = lax.rsqrt(jnp.mean(centred * centred, axis=-1, keepdims=True) + 1e-05)
    return centred * scale, scale


def norm_back(grad, normed, scale):
    return scale * (
        grad
        - jnp.mean(grad, axis=-1, keepdims=True)
        - normed * jnp.mean(grad * normed, axis=-1, keepdims=True)
    )


def first_row_kernel(tokens_ref, row_ref, semaphores):
    copies = Copies(semaphores)
    copies.start(0, tokens_ref.at[pl.ds(0, 1)], row_ref)
    copies.wait(0)


def first_row(after, tokens):
    _, toks, _ = tokens.shape
    return kernel_call(
        first_row_kernel,
        after,
        (tokens,),
        1,
        [ANY],
        [VMEM],
        [jax.ShapeDtypeStruct((1, toks, D), BF16)],
        scratch_shapes=[pltpu.SemaphoreType.DMA((1,))],
        name="first_row",
    )


def project_own_kernel(tokens_ref, gain_ref, shift_ref, bias_ref, weight_ref, query_ref, keyval_ref, *rest):
    later_refs, normed_ref = rest[:-1], rest[-1]
    rows, toks, _ = tokens_ref.shape
    for at, later_ref in enumerate(later_refs):
        later_ref[0] = tokens_ref[at + 1]
    normed, _ = normalize(tokens_ref[...].reshape(rows * toks, D).astype(F32))
    normed_ref[...] = (normed * gain_ref[...] + shift_ref[...]).astype(BF16)
    chunk = D // 2
    for at in range(6):
        span = slice(at * chunk, (at + 1) * chunk)
        result = (dot(normed_ref[...], weight_ref[:, span]) + bias_ref[:, span]).astype(BF16)
        cols = slice(at % 2 * chunk, (at % 2 + 1) * chunk)
        if at < 2:
            query_ref[:, :, cols] = (result * 0.125).reshape(rows, toks, chunk)
        else:
            keyval_ref[:, at // 2 - 1, :, cols] = result.reshape(rows, toks, chunk)


def project_own(after, tokens, gain, shift, weight, bias):
    rows, toks, _ = tokens.shape
    return kernel_call(
        project_own_kernel,
        after,
        (tokens, gain, shift, bias, weight),
        14,
        [VMEM] * 5,
        [VMEM] * (1 + rows),
        [jax.ShapeDtypeStruct((rows, toks, D), BF16), jax.ShapeDtypeStruct((rows, 2, toks, D), BF16)]
        + [jax.ShapeDtypeStruct((1, toks, D), BF16)] * (rows - 1),
        scratch_shapes=[pltpu.VMEM((rows * toks, D), BF16)],
        name="project_own",
    )


def project_up_kernel(tokens_ref, gain_ref, shift_ref, bias_ref, weight_ref, keyval_ref):
    toks = tokens_ref.shape[1]
    normed, _ = normalize(tokens_ref[0].astype(F32))
    normed = (normed * gain_ref[...] + shift_ref[...]).astype(BF16)
    for half in range(2):
        cols = slice((half + 1) * D, (half + 2) * D)
        keyval_ref[0, half] = (dot(normed, weight_ref[:, cols]) + bias_ref[:, cols]).astype(BF16)


def project_up(after, tokens, gain, shift, weight, bias, warm=()):
    toks = tokens.shape[1]
    return kernel_call(
        project_up_kernel,
        after,
        (tokens, gain, shift, bias, weight),
        10,
        [VMEM] * 5,
        [VMEM],
        [jax.ShapeDtypeStruct((1, 2, toks, D), BF16)],
        warm=warm,
        name="project_up",
    )


def head_lanes(values, head):
    lanes = lax.broadcasted_iota(jnp.int32, values.shape, 1)
    keep = lanes < HEAD_DIM if head == 0 else lanes >= HEAD_DIM
    return jnp.where(keep, values, jnp.zeros_like(values))


def prefix_mask(values, fill):
    places = lax.broadcasted_iota(jnp.int32, values.shape, 0)
    return jnp.where(places < PREFIX, values, fill)


class Places:
    def __init__(self, toks, level_count):
        self.toks = toks
        self.level_count = level_count

    def masked(self, block):
        if block < 2:
            return True
        level = block // 2
        return (self.level_count - level) * 2 * self.toks > LEAST_LENGTH

    def limits(self, place, length):
        base = place * self.toks
        queries = base + lax.broadcasted_iota(jnp.int32, (1, self.toks), 1)
        return jnp.minimum(queries, length - 1)

    def visible(self, block, place, limit):
        if block == 0:
            base = place * self.toks
        else:
            base = (lax.bitwise_xor(place, block % 2) - (block // 2) * 2) * self.toks
        keys = lax.broadcasted_iota(jnp.int32, (self.toks, self.toks), 0)
        return keys <= limit - base


def spread_prefix(prefix):
    tiled = jnp.concatenate([prefix] * HEADS, axis=0)
    rows = lax.broadcasted_iota(jnp.int32, tiled.shape, 0) // PREFIX_PAD
    cols = lax.broadcasted_iota(jnp.int32, tiled.shape, 1) // HEAD_DIM
    return jnp.where(rows == cols, tiled, jnp.zeros_like(tiled))


GELU_SCALE = 0.7978845608028654
GELU_CUBE = 0.044715
FAR = 1e30
ROW_LIMIT = 30


PACKED = (8, 2 * D + D // 2)


def pack_prefix(ref, halves):
    for half, values in enumerate(halves):
        ref[:, half * D : (half + 1) * D] = values[:8]
        for row in range(8, PREFIX):
            for part in range(2):
                at = (half * (PREFIX - 8) + row - 8) * 2 + part
                ref[at : at + 1, 2 * D :] = values[row : row + 1, part * (D // 2) : (part + 1) * (D // 2)]


def unpack_prefix(ref, half):
    rest = jnp.concatenate([ref[:, 2 * D :], jnp.zeros((8, D // 2), F32)], axis=0)
    rows = []
    for row in range(8, PREFIX):
        at = (half * (PREFIX - 8) + row - 8) * 2
        rows.append(jnp.concatenate([rest[at : at + 1], rest[at + 1 : at + 2]], axis=1))
    rows.append(jnp.zeros((PREFIX_PAD - PREFIX, D), F32))
    return jnp.concatenate([ref[:, half * D : (half + 1) * D]] + rows, axis=0)


class RowRefs:
    def __init__(self, names, refs):
        for name, ref in zip(names, refs):
            setattr(self, name, ref)


def column_group(group, width):
    return pl.ds(pl.multiple_of(group * width, width), width)


def attend_rows(places, refs, place, limit, pair_step):
    blocks = range(2 * places.level_count)
    masked_blocks = [block for block in blocks if places.masked(block)]
    level = place // 2
    width = 128 * pair_step
    refs.prefix_scores[...] = dot(refs.spread[0], refs.query[...], NT)
    for at, block in enumerate(masked_blocks):
        refs.hide[at] = jnp.where(places.visible(block, place, limit), 0.0, -jnp.inf)

    def beyond(block):
        return jnp.where(level >= block // 2, 0.0, FAR) if block > 1 else None

    def body(group, carry):
        span = column_group(group, width)
        group_queries = refs.query[:, span]
        group_keys = [refs.keyval(block, 0, span) for block in blocks]

        def scores_of(at):
            pair, head = at // 2, at % 2
            cols = slice(pair * 128, (pair + 1) * 128)
            queries = head_lanes(group_queries[:, cols], head)
            spot = pl.multiple_of((group * pair_step * 2 + at) * PREFIX_PAD, PREFIX_PAD)
            prefix_scores = prefix_mask(refs.prefix_scores[pl.ds(spot, PREFIX_PAD), :], -jnp.inf)
            highest = jnp.max(prefix_scores, axis=0, keepdims=True)
            scores = []
            for block in blocks:
                part = dot(group_keys[block][:, cols], queries, NT)
                if block in masked_blocks:
                    part = part + refs.hide[masked_blocks.index(block)]
                top = jnp.max(part, axis=0, keepdims=True)
                if block > 1:
                    top = top - beyond(block)
                highest = jnp.maximum(highest, top)
                scores.append(part)
            return prefix_scores, scores, highest

        ahead = scores_of(0)
        for at in range(2 * pair_step):
            pair, head = at // 2, at % 2
            cols = slice(pair * 128, (pair + 1) * 128)
            prefix_scores, scores, highest = ahead
            if at + 1 < 2 * pair_step:
                ahead = scores_of(at + 1)
            if head == 0:
                values_t = [refs.keyval(block, 1, span)[:, cols].T for block in blocks]
                prefix_values_t = refs.prefix[1, :, span][:, cols].T
                ones = jnp.ones((PREFIX_PAD, values_t[0].shape[1]), BF16)
                outs = []
            rows = slice(head * HEAD_DIM, (head + 1) * HEAD_DIM)
            prefix_weights = jnp.exp(prefix_scores - highest)
            total = jnp.sum(prefix_weights, axis=0, keepdims=True)
            mixed = dot(prefix_values_t[rows], prefix_weights.astype(BF16))
            for block in blocks:
                base = highest + beyond(block) if block > 1 else highest
                weights = jnp.exp(scores[block] - base)
                part = dot(jnp.concatenate([values_t[block][rows], ones], axis=0), weights.astype(BF16))
                total = total + part[HEAD_DIM : HEAD_DIM + 1]
                mixed = mixed + part[:HEAD_DIM]
            outs.append(mixed * (1.0 / total))
            refs.total[group, at : at + 1, :] = highest + jnp.log(total)
            if head == 1:
                refs.mixed[:, pl.ds(pl.multiple_of(group * width + pair * 128, 128), 128)] = jnp.concatenate(outs, axis=0).T.astype(BF16)
        return carry

    lax.fori_loop(0, PAIRS // pair_step, body, 0)


def feed_rows(refs, place, length, source, weight_copies, chunks, chunk, slots):
    toks = refs.tokens.shape[0]
    spots = place * toks + lax.broadcasted_iota(jnp.int32, (toks, D), 0)
    target = (spots >= source) & (spots < length)
    refs.grad_out[...] = jnp.where(target, refs.cotangent[...].astype(F32), 0.0).astype(BF16)
    residual = refs.tokens[...].astype(F32) + dot(refs.mixed[...], refs.output_weight[...]) + refs.output_bias[...]
    refs.residual[...] = residual
    normed, _ = normalize(residual)
    refs.normed[...] = (normed * refs.second_gain[...] + refs.second_shift[...]).astype(BF16)

    def first(at, slot):
        for copy in weight_copies(at):
            copy.wait()
        bias = refs.expand_bias[:, pl.ds(pl.multiple_of(at * chunk, chunk), chunk)]
        values = dot(refs.normed[...], refs.expand_weight[at % slots]) + bias
        grad_hidden = dot(refs.grad_out[...], refs.contract_weight[at % slots], NT)
        square = values * values
        bend = jnp.tanh(values * (GELU_SCALE + GELU_SCALE * GELU_CUBE * square))
        half = 0.5 + 0.5 * bend
        slope = half + (0.5 * values) * (1.0 - bend * bend) * (
            GELU_SCALE + 3.0 * GELU_SCALE * GELU_CUBE * square
        )
        refs.active[slot] = (values * half).astype(BF16)
        refs.grad_expand[slot] = (grad_hidden * slope).astype(BF16)

    def second(at, slot):
        refs.result[...] += dot(refs.active[slot], refs.contract_weight[at % slots])
        refs.grad_normed[...] += dot(refs.grad_expand[slot], refs.expand_weight[at % slots], NT)

    def refill(at):
        @pl.when(at + slots < chunks)
        def _():
            for copy in weight_copies(at + slots):
                copy.start()

    refs.result[...] = jnp.zeros_like(refs.result)
    refs.grad_normed[...] = jnp.zeros_like(refs.grad_normed)
    first(0, 0)

    def body(at, carry):
        first(2 * at + 1, 1)
        second(2 * at, 0)
        refill(2 * at)
        first(2 * at + 2, 0)
        second(2 * at + 1, 1)
        refill(2 * at + 1)
        return carry

    lax.fori_loop(0, chunks // 2 - 1, body, 0)
    first(chunks - 1, 1)
    second(chunks - 2, 0)
    second(chunks - 1, 1)

    residual = refs.residual[...]
    refs.activations[...] = (residual + refs.result[...] + refs.contract_bias[...]).astype(BF16)
    normed, scale = normalize(residual)
    grad = refs.grad_out[...].astype(F32) + norm_back(refs.grad_normed[...] * refs.second_gain[...], normed, scale)
    refs.grad_residual[0] = grad
    refs.grad_heads[...] = dot(grad.astype(BF16), refs.output_weight[...], NT).astype(BF16)


def prefix_back_rows(refs):
    toks = refs.query.shape[0]
    queries = refs.query[...]
    grads = refs.grad_heads[...]
    product = grads.astype(F32) * refs.mixed[...].astype(F32)
    head_of = lax.broadcasted_iota(jnp.int32, (HEADS, D), 1) // HEAD_DIM
    chosen = jnp.where(head_of == lax.broadcasted_iota(jnp.int32, (HEADS, D), 0), 1.0, 0.0).astype(BF16)
    high, low = split(product)
    inner = dot(chosen, high, NT) + dot(chosen, low, NT)
    refs.inner[...] = inner.reshape(refs.inner.shape)

    def per_head(values):
        return values.reshape(HEADS, PREFIX_PAD, toks)

    scores = per_head(refs.prefix_scores[...])
    grad_weights = per_head(dot(refs.spread[1], grads, NT))
    weights = jnp.exp(scores - refs.total[...].reshape(HEADS, 1, toks))
    valid = lax.broadcasted_iota(jnp.int32, weights.shape, 1) < PREFIX
    weights = jnp.where(valid, weights, 0.0)
    grad_scores = weights * (grad_weights - inner[:, None, :])
    weights = weights.reshape(HEADS * PREFIX_PAD, toks).astype(BF16)
    grad_scores = grad_scores.reshape(HEADS * PREFIX_PAD, toks).astype(BF16)
    refs.result[...] = dot(grad_scores.T, refs.spread[0])
    own = (
        lax.broadcasted_iota(jnp.int32, (HEADS * PREFIX_PAD, D), 0) // PREFIX_PAD
        == lax.broadcasted_iota(jnp.int32, (HEADS * PREFIX_PAD, D), 1) // HEAD_DIM
    )

    def gather(values):
        return jnp.sum(jnp.where(own, values, 0.0).reshape(HEADS, PREFIX_PAD, D), axis=0)

    sums = gather(dot(grad_scores, queries)), gather(dot(weights, grads))
    pack_prefix(refs.prefix_grad, sums)
    refs.prefix_grad[...] += refs.earlier_grad[...]


def attend_back_rows(places, refs, place, pair_step):
    blocks = range(2 * places.level_count)
    masked_blocks = [block for block in blocks if places.masked(block)]
    level = place // 2
    width = 128 * pair_step

    def body(group, carry):
        span = column_group(group, width)
        group_queries = refs.query[:, span]
        group_grads = refs.grad_heads[:, span]
        group_keys = [refs.keyval(block, 0, span) for block in blocks]
        group_values = [refs.keyval(block, 1, span) for block in blocks]

        sides = {}

        def side(at):
            if at not in sides:
                cols = slice(at // 2 * 128, (at // 2 + 1) * 128)
                sides[at] = head_lanes(group_queries[:, cols], at % 2), head_lanes(group_grads[:, cols], at % 2)
            return sides[at]

        def products_of(item):
            at, block = item
            cols = slice(at // 2 * 128, (at // 2 + 1) * 128)
            queries, grads = side(at)
            part = dot(group_keys[block][:, cols], queries, NT)
            if block in masked_blocks:
                part = part + refs.hide[masked_blocks.index(block)]
            return part, dot(group_values[block][:, cols], grads, NT)

        items = [(at, block) for at in range(2 * pair_step) for block in blocks]
        ahead = [products_of(item) for item in items[:2]]
        for spot, (at, block) in enumerate(items):
            pair, head = at // 2, at % 2
            cols = slice(pair * 128, (pair + 1) * 128)
            place_cols = pl.ds(pl.multiple_of(group * width + pair * 128, 128), 128)
            scores, grad_weights = ahead.pop(0)
            if spot + 2 < len(items):
                ahead.append(products_of(items[spot + 2]))
            queries, grads = side(at)
            if block == 0:
                if head == 0:
                    keys_t = [keys[:, cols].T for keys in group_keys]
                    grad_keys, grad_values, outs = [], [], []
                total = refs.total[group, at : at + 1, :]
                inner = refs.inner[group, at : at + 1, :]
                grad_query = None
            rows = slice(head * HEAD_DIM, (head + 1) * HEAD_DIM)
            base = total + jnp.where(level >= block // 2, 0.0, FAR) if block > 1 else total
            weights = jnp.exp(scores - base)
            grad_scores = (weights * (grad_weights - inner)).astype(BF16)
            part_values = dot(weights.astype(BF16), grads)
            part_keys = dot(grad_scores, queries)
            part_query = dot(keys_t[block][rows], grad_scores)
            if head == 0:
                grad_values.append(part_values)
                grad_keys.append(part_keys)
            else:
                refs.grad_keyval[block][0, 0, :, place_cols] = (grad_keys[block] + part_keys).astype(BF16)
                refs.grad_keyval[block][0, 1, :, place_cols] = (grad_values[block] + part_values).astype(BF16)
            grad_query = part_query if grad_query is None else grad_query + part_query
            if block == blocks[-1]:
                outs.append(grad_query)
                if head == 1:
                    grad_query = jnp.concatenate(outs, axis=0).T + refs.result[:, place_cols]
                    refs.grad_query[0, :, place_cols] = (grad_query * 0.125).astype(BF16)
        return carry

    lax.fori_loop(0, PAIRS // pair_step, body, 0)


ROW_NAMES = (
    "expand_weight", "contract_weight", "spread", "prefix_scores", "hide", "total",
    "mixed", "grad_out", "residual", "normed", "active", "grad_expand", "result", "grad_normed",
    "grad_heads", "inner",
)


def row_kernel(places, keyval_rows, pair_step, chunk, row_ref, place_ref, length_ref, source_ref, *rest):
    block_count = 2 * places.level_count
    row = row_ref[0]
    query_ref, tokens_ref, cotangent_ref, prefix_ref = rest[:4]
    keyval_refs = rest[4 : 4 + block_count]
    rest = rest[4 + block_count :]
    output_weight_ref, expand_weight_hbm, contract_weight_hbm = rest[:3]
    vectors = rest[3:8]
    earlier_grad_ref = rest[8]
    rest = rest[9:]
    activations_ref, grad_residual_ref, grad_query_ref = rest[:3]
    grad_keyval_refs = rest[3 : 3 + block_count]
    prefix_grad_ref = rest[3 + block_count]
    rest = rest[4 + block_count :]
    refs = RowRefs(ROW_NAMES, rest)
    refs.output_bias, refs.second_gain, refs.second_shift, refs.expand_bias, refs.contract_bias = vectors
    refs.prefix_grad, refs.earlier_grad = prefix_grad_ref, earlier_grad_ref
    refs.activations = activations_ref.at[0]
    refs.query, refs.prefix = query_ref.at[row], prefix_ref
    refs.keyval = lambda block, half, span: keyval_refs[block][row if keyval_rows[block] is None else keyval_rows[block], half, :, span]
    refs.grad_residual, refs.grad_query, refs.grad_keyval = grad_residual_ref, grad_query_ref, grad_keyval_refs
    (weight_semaphores,) = rest[len(ROW_NAMES) :]
    slots = refs.expand_weight.shape[0]
    chunks = expand_weight_hbm.shape[1] // chunk

    refs.output_weight, refs.tokens, refs.cotangent = output_weight_ref, tokens_ref.at[row], cotangent_ref.at[row]

    def weight_copies(at):
        span = pl.ds(pl.multiple_of(at * chunk, chunk), chunk)
        return (
            pltpu.make_async_copy(expand_weight_hbm.at[:, span], refs.expand_weight.at[at % slots], weight_semaphores.at[at]),
            pltpu.make_async_copy(contract_weight_hbm.at[span, :], refs.contract_weight.at[at % slots], weight_semaphores.at[chunks + at]),
        )

    def start_weights(at, carry):
        for copy in weight_copies(at):
            copy.start()
        return carry

    lax.fori_loop(0, slots, start_weights, 0)
    place = place_ref[0]
    length = length_ref[row]
    limit = places.limits(place, length)
    for half in range(2):
        refs.spread[half] = spread_prefix(refs.prefix[half])
    attend_rows(places, refs, place, limit, pair_step)
    feed_rows(refs, place, length, source_ref[row], weight_copies, chunks, chunk, slots)
    prefix_back_rows(refs)
    attend_back_rows(places, refs, place, pair_step)


def row_block(after, place, lengths, sources, queries, tokens, cotangent, prefix_keyval, keyvals, weights, row, earlier_grad, warm=(), pair_step=4, chunk=512, slots=3):
    toks = queries.shape[1]
    block_count = len(keyvals)
    places = Places(toks, block_count // 2)
    output_weight, output_bias, gain, shift, expand_weight, expand_bias, contract_weight, contract_bias = weights
    hidden = expand_weight.shape[1]
    chunks = hidden // chunk
    masked = sum(places.masked(block) for block in range(block_count))
    per_group = 2 * pair_step
    scratch = dict(
        expand_weight=((slots, D, chunk), BF16), contract_weight=((slots, chunk, D), BF16),
        spread=((2, HEADS * PREFIX_PAD, D), BF16), prefix_scores=((HEADS * PREFIX_PAD, toks), F32),
        hide=((masked, toks, toks), F32), total=((HEADS // per_group, per_group, toks), F32), mixed=((toks, D), BF16),
        grad_out=((toks, D), BF16), residual=((toks, D), F32), normed=((toks, D), BF16),
        active=((2, toks, chunk), BF16), grad_expand=((2, toks, chunk), BF16), result=((toks, D), F32),
        grad_normed=((toks, D), F32),
        grad_heads=((toks, D), BF16), inner=((HEADS // per_group, per_group, toks), F32),
    )
    return kernel_call(
        functools.partial(row_kernel, places, [at for _, at in keyvals], pair_step, chunk),
        after,
        (
            jnp.full((1,), row, jnp.int32), place, lengths, sources, queries, tokens, cotangent, prefix_keyval, *[array for array, _ in keyvals],
            output_weight, expand_weight, contract_weight, output_bias, gain, shift, expand_bias, contract_bias, earlier_grad,
        ),
        ROW_LIMIT,
        [VMEM] * (4 + block_count) + [VMEM, HBM, HBM] + [VMEM] * 6,
        [VMEM] * (4 + block_count),
        [
            jax.ShapeDtypeStruct((1, toks, D), BF16),
            jax.ShapeDtypeStruct((1, toks, D), F32),
            jax.ShapeDtypeStruct((1, toks, D), BF16),
        ]
        + [jax.ShapeDtypeStruct((1, 2, toks, D), BF16)] * block_count
        + [jax.ShapeDtypeStruct(PACKED, F32)],
        prefetched=4,
        scratch_shapes=[pltpu.VMEM(*scratch[name]) for name in ROW_NAMES]
        + [pltpu.SemaphoreType.DMA((2 * chunks,))],
        warm=warm,
        name="row_block",
    )


def up_back_kernel(own_ref, received_ref, weight_ref, grad_ref):
    total = None
    for half in range(2):
        values = (own_ref[0, half].astype(F32) + received_ref[0, half].astype(F32)).astype(BF16)
        part = dot(values, weight_ref[:, (half + 1) * D : (half + 2) * D], NT)
        total = part if total is None else total + part
    grad_ref[0] = total.astype(BF16)


def up_back(after, own, received, weight):
    toks = own.shape[2]
    return kernel_call(
        up_back_kernel,
        after,
        (own, received, weight),
        10,
        [VMEM] * 3,
        [VMEM],
        [jax.ShapeDtypeStruct((1, toks, D), BF16)],
        name="up_back",
    )


def project_back_kernel(query_ref, own_ref, received_ref, weight_ref, total_ref):
    total = dot(query_ref[0], weight_ref[:, :D], NT)
    for half in range(2):
        values = (own_ref[0, half].astype(F32) + received_ref[0, half].astype(F32)).astype(BF16)
        total = total + dot(values, weight_ref[:, (half + 1) * D : (half + 2) * D], NT)
    total_ref[0] = total


def project_back(after, grad_query, own, received, weight):
    toks = grad_query.shape[1]
    return kernel_call(
        project_back_kernel,
        after,
        (grad_query, own, received, weight),
        10,
        [VMEM] * 4,
        [VMEM],
        [jax.ShapeDtypeStruct((1, toks, D), F32)],
        name="project_back",
    )


def finish_kernel(above_count, row, tokens_ref, gain_ref, residual_ref, total_ref, activations_ref, *rest):
    activations_hbm, grad_hbm, grad_ref, semaphores = rest[-4:]
    toks = grad_ref.shape[0]
    copies = Copies(semaphores)
    copies.start("activations", activations_ref.at[0], activations_hbm.at[row])
    parts = 2
    for part in range(parts):
        span = pl.ds(part * (toks // parts), toks // parts)
        total = total_ref[0, span]
        for above_ref in rest[:above_count]:
            total = total + above_ref[0, span].astype(F32)
        normed, scale = normalize(tokens_ref[row, span].astype(F32))
        grad_ref[span] = residual_ref[0, span] + norm_back(total * gain_ref[...], normed, scale)
        copies.start(part, grad_ref.at[span], grad_hbm.at[row, span])
    for part in range(parts):
        copies.wait(part)
    copies.wait("activations")


def finish(after, tokens, gain, grad_residual, total, activations, above, row, earlier):
    toks = tokens.shape[1]
    return kernel_call(
        functools.partial(finish_kernel, len(above), row),
        after,
        (tokens, gain, grad_residual, total, activations, *above, *earlier),
        10,
        [VMEM] * (5 + len(above)) + [ANY] * len(earlier),
        [HBM] * 2,
        [jax.ShapeDtypeStruct(tokens.shape, BF16), jax.ShapeDtypeStruct(tokens.shape, F32)],
        scratch_shapes=[pltpu.VMEM((toks, D), F32), pltpu.SemaphoreType.DMA((3,))],
        input_output_aliases={5 + len(above) + at: at for at in range(len(earlier))},
        name="finish",
    )


def prefix_kernel(table_ref, lift_ref, lift_bias_ref, fan_ref, fan_bias_ref, lifted_ref, keyval_ref):
    lifted = jnp.tanh(dot(table_ref[...], lift_ref[...]) + lift_bias_ref[...])
    lifted_ref[...] = jnp.zeros_like(lifted_ref)
    lifted_ref[:PREFIX, :] = lifted
    keyval_ref[...] = jnp.zeros_like(keyval_ref)
    keyval = (dot(lifted.astype(BF16), fan_ref[...]) + fan_bias_ref[...]).astype(BF16)
    keyval_ref[0, :PREFIX, :] = keyval[:, :D]
    keyval_ref[1, :PREFIX, :] = keyval[:, D:]


def prefix_forward(after, table, lift, lift_bias, fan, fan_bias):
    return kernel_call(
        prefix_kernel,
        after,
        (table, lift, lift_bias, fan, fan_bias),
        8,
        [VMEM] * 5,
        [VMEM] * 2,
        [
            jax.ShapeDtypeStruct((PREFIX_PAD, lift.shape[1]), F32),
            jax.ShapeDtypeStruct((2, PREFIX_PAD, D), BF16),
        ],
        name="prefix_forward",
    )


def prefix_network_back_kernel(grad_ref, table_ref, lift_ref, fan_ref, lifted_ref, grad_table_ref, grad_lift_ref, grad_lift_bias_ref, grad_fan_ref, grad_fan_bias_ref):
    lifted = lifted_ref[...]
    lifted_t = jnp.concatenate([lifted.astype(BF16)] * 2, axis=0).T
    grad_lifted = None
    for half in range(2):
        cols = slice(half * D, (half + 1) * D)
        grad = unpack_prefix(grad_ref, half)
        grad_fan_bias_ref[:, cols] = jnp.sum(grad, axis=0, keepdims=True)
        both = jnp.concatenate(split(grad), axis=0)
        grad_fan_ref[:, cols] = dot(lifted_t, both)
        part = dot(both, fan_ref[:, cols], NT)
        grad_lifted = part if grad_lifted is None else grad_lifted + part
    grad_lifted = (grad_lifted[:PREFIX_PAD] + grad_lifted[PREFIX_PAD:]) * (1.0 - lifted * lifted)
    grad_lift_bias_ref[...] = jnp.sum(grad_lifted, axis=0, keepdims=True)
    both = jnp.concatenate(split(grad_lifted), axis=0)
    table = jnp.concatenate([table_ref[...].astype(F32), jnp.zeros((PREFIX_PAD - PREFIX, D), F32)], axis=0)
    table_t = jnp.concatenate([table.astype(BF16)] * 2, axis=0).T
    grad_lift_ref[...] = dot(table_t, both)
    grad_table = dot(both, lift_ref[...], NT)
    grad_table_ref[...] = (grad_table[:PREFIX_PAD] + grad_table[PREFIX_PAD:])[:PREFIX]


def prefix_network_back(after, grad, table, lift, fan, lifted):
    hidden = lift.shape[1]
    return kernel_call(
        prefix_network_back_kernel,
        after,
        (grad, table, lift, fan, lifted),
        20,
        [VMEM] * 5,
        [VMEM] * 5,
        [
            jax.ShapeDtypeStruct((PREFIX, D), F32),
            jax.ShapeDtypeStruct((D, hidden), F32),
            jax.ShapeDtypeStruct((1, hidden), F32),
            jax.ShapeDtypeStruct((hidden, 2 * D), F32),
            jax.ShapeDtypeStruct((1, 2 * D), F32),
        ],
        name="prefix_network_back",
    )


def add_kernel(*refs):
    total = refs[0][...]
    for ref in refs[1:-1]:
        total = total + ref[...]
    refs[-1][...] = total


def add(after, *values):
    return kernel_call(add_kernel, after, values, 2, [VMEM] * len(values), [VMEM], values[:1], name="add")


def mark_kernel(*refs):
    pass


def mark(after, warm=()):
    return kernel_call(mark_kernel, after, (), 8, [], [], [], warm=warm, cover=LONG_COVER, name="mark")


def hold(after, array):
    return kernel_call(mark_kernel, after, (array,), 1, [ANY], [ANY], [array], input_output_aliases={0: 0}, name="hold")


class Order:
    def __init__(self):
        self.before = ()

    def call(self, kernel, *operands):
        *outs, token = kernel(self.before, *operands)
        self.before = (token,)
        return outs[0] if len(outs) == 1 else outs


def sum_stages():
    stages = []
    for axis, most in (("seq", 1), ("dp", 2)):
        size = lax.axis_size(axis)
        if size & (size - 1):
            return None
        hop = 1
        while hop < size:
            bits = most if hop > 1 and hop * 2 < size else 1
            stages.append((axis, [[(at, at ^ (hop * step)) for at in range(size)] for step in range(1, 2**bits)]))
            hop *= 2**bits
    return stages


def per_device(tokens, cotangent, row_lengths, source_lengths, first_gain, first_shift, attend_weight, attend_bias, output_weight, output_bias, second_gain, second_shift, expand_weight, expand_bias, contract_weight, contract_bias, prefix_table, lift_weight, lift_bias, fan_weight, fan_bias):
    rows = tokens.shape[0]
    seq = lax.axis_size("seq")
    level_count = seq // 2
    levels = range(1, level_count)
    mates = [(at, at ^ 1) for at in range(seq)]
    place = lax.axis_index("seq").astype(jnp.int32).reshape(1)
    first_gain, first_shift, attend_bias, output_bias, second_gain, second_shift, expand_bias, contract_bias, lift_bias, fan_bias = [
        vector.reshape(1, -1)
        for vector in (first_gain, first_shift, attend_bias, output_bias, second_gain, second_shift, expand_bias, contract_bias, lift_bias, fan_bias)
    ]
    weights = (output_weight, output_bias, second_gain, second_shift, expand_weight, expand_bias, contract_weight, contract_bias)
    order = Order()
    hops = sum_stages()
    finished = ()
    prefix_grad = jnp.zeros(PACKED, F32)
    arriving = None

    def swap(array):
        return lax.ppermute(array, "seq", mates)

    def hop():
        nonlocal prefix_grad, arriving
        if arriving is not None:
            prefix_grad = order.call(add, prefix_grad, *arriving)
            arriving = None
        if hops:
            axis, partners = hops.pop(0)
            arriving = [lax.ppermute(prefix_grad, axis, pairs) for pairs in partners]

    def lower(row):
        blocks = []
        for level in levels:
            block = order.call(project_up, lower_tokens[row, level], first_gain, first_shift, attend_weight, attend_bias, (queries, cotangent) if row == 0 else ())
            blocks += [block, swap(block)]
        return blocks

    def keyvals_of(blocks):
        return [(keyval, None), (mate_keyval, None)] + [(block, 0) for block in blocks]

    row_tokens = [order.call(first_row, tokens)]
    lower_tokens = {}

    def raise_tokens(row):
        for level in levels:
            pairs = [(at, at + 2 * level) for at in range(seq - 2 * level)]
            lower_tokens[row, level] = lax.ppermute(row_tokens[row], "seq", pairs)

    raise_tokens(0)
    queries, keyval, *later = order.call(project_own, tokens, first_gain, first_shift, attend_weight, attend_bias)
    row_tokens += later
    for row in range(1, rows):
        raise_tokens(row)
    mate_keyval = swap(keyval)
    lifted, prefix_keyval = order.call(prefix_forward, prefix_table, lift_weight, lift_bias, fan_weight, fan_bias)
    blocks = lower(0)
    order.call(mark)
    waiting = []
    finished_rows = 0
    for row in range(rows):
        last_row = row + 1 == rows
        row_activations, grad_residual, grad_query, *grads, prefix_grad = order.call(
            row_block, place, row_lengths, source_lengths, queries, tokens, cotangent, prefix_keyval,
            keyvals_of(blocks), weights, row, prefix_grad, (attend_weight,),
        )
        received = None if last_row else swap(grads[1])
        from_mates = [swap(grads[2 * level + 1]) for level in levels]
        if last_row:
            if hops is None:
                prefix_grad = lax.psum(prefix_grad, ("seq", "dp"))
            hop()
            for earlier in waiting:
                earlier()
                hop()
            received = swap(order.call(hold, grads[1]))
        else:
            blocks = lower(row + 1)
        above = []
        for level in levels:
            part = order.call(up_back, grads[2 * level], from_mates[level - 1], attend_weight)
            above.append(lax.ppermute(part, "seq", [(at + 2 * level, at) for at in range(seq - 2 * level)]))
        total = order.call(project_back, grad_query, grads[0], received, attend_weight)

        def end(row=row, grad_residual=grad_residual, total=total, row_activations=row_activations, above=above):
            nonlocal finished, finished_rows
            finished_rows += 1
            finished = order.call(finish, tokens, first_gain, grad_residual, total, row_activations, above, row, finished)

        waiting.append(end)
    while hops or arriving is not None:
        hop()
        if arriving is not None:
            if hops:
                order.call(mark, (lift_weight, fan_weight))
            else:
                waiting[-1]()
    grad_table, grad_lift, grad_lift_bias, grad_fan, grad_fan_bias = order.call(
        prefix_network_back, prefix_grad, prefix_table, lift_weight, fan_weight, lifted
    )
    if finished_rows < rows:
        waiting[-1]()
    return (*finished, grad_table, grad_lift, grad_lift_bias.reshape(-1), grad_fan, grad_fan_bias.reshape(-1))


def solution(mesh):
    batch = P("dp", "seq", None)
    return jax.shard_map(
        per_device,
        mesh=mesh,
        in_specs=(batch, batch, P("dp"), P("dp")) + (P(),) * 17,
        out_specs=(batch, batch, P(), P(), P(), P(), P()),
        check_vma=False,
    )
```

```python
import functools

import jax
import jax.numpy as jnp
from jax import lax
from jax.experimental import pallas as pl
from jax.experimental.pallas import tpu as pltpu
from jax.sharding import PartitionSpec as P

D = 1024
HEADS = 16
HEAD_DIM = 64
PAIRS = HEADS // 2
PREFIX = 10
PREFIX_PAD = 16
LEAST_LENGTH = 512
NN = (((1,), (0,)), ((), ()))
NT = (((1,), (1,)), ((), ()))
MIB = 1 << 20
BF16 = jnp.bfloat16
F32 = jnp.float32


def dot(left, right, dims=NN):
    return lax.dot_general(left, right, dims, preferred_element_type=F32)


ANY = pl.BlockSpec(memory_space=pl.ANY)


VMEM = pl.BlockSpec(memory_space=pltpu.VMEM)
COVER = pl.CostEstimate(flops=10**10, bytes_accessed=10**9, transcendentals=0)
LONG_COVER = pl.CostEstimate(flops=5 * 10**10, bytes_accessed=10**9, transcendentals=0)
TOKEN = jax.ShapeDtypeStruct((8, 128), F32)


def kernel_call(kernel, after, operands, limit, in_specs, out_specs, out_shape, prefetched=0, scratch_shapes=(), warm=(), cover=COVER, **rest):
    lead = prefetched + len(in_specs)

    def body(*refs):
        outs = lead + len(after) + len(warm)
        token_ref = refs[outs + len(out_shape)]
        token_ref[...] = jnp.zeros_like(token_ref)
        kernel(*refs[:lead], *refs[outs : outs + len(out_shape)], *refs[outs + len(out_shape) + 1 :])

    spec = pltpu.PrefetchScalarGridSpec(
        num_scalar_prefetch=prefetched,
        grid=(1,),
        in_specs=[*in_specs] + [ANY] * len(after) + [VMEM] * len(warm),
        out_specs=[*out_specs, VMEM],
        scratch_shapes=scratch_shapes,
    )
    return pl.pallas_call(
        body,
        grid_spec=spec,
        out_shape=[*(jax.ShapeDtypeStruct(out.shape, out.dtype) for out in out_shape), TOKEN],
        compiler_params=pltpu.CompilerParams(dimension_semantics=("arbitrary",), vmem_limit_bytes=limit * MIB),
        cost_estimate=cover,
        **rest,
    )(*operands, *after, *warm)


def split(values):
    high = values.astype(BF16)
    return high, (values - high.astype(F32)).astype(BF16)


class Copies:
    def __init__(self, semaphores):
        self.semaphores = semaphores
        self.count = 0
        self.copies = {}

    def start(self, name, source, target):
        copy = pltpu.make_async_copy(source, target, self.semaphores.at[self.count])
        copy.start()
        self.count += 1
        self.copies[name] = copy

    def wait(self, name):
        self.copies[name].wait()


HBM = pl.BlockSpec(memory_space=pltpu.HBM)


def normalize(values):
    centred = values - jnp.mean(values, axis=-1, keepdims=True)
    scale = lax.rsqrt(jnp.mean(centred * centred, axis=-1, keepdims=True) + 1e-05)
    return centred * scale, scale


def norm_back(grad, normed, scale):
    return scale * (
        grad
        - jnp.mean(grad, axis=-1, keepdims=True)
        - normed * jnp.mean(grad * normed, axis=-1, keepdims=True)
    )


def first_row_kernel(tokens_ref, row_ref, semaphores):
    copies = Copies(semaphores)
    copies.start(0, tokens_ref.at[pl.ds(0, 1)], row_ref)
    copies.wait(0)


def first_row(after, tokens):
    _, toks, _ = tokens.shape
    return kernel_call(
        first_row_kernel,
        after,
        (tokens,),
        1,
        [ANY],
        [VMEM],
        [jax.ShapeDtypeStruct((1, toks, D), BF16)],
        scratch_shapes=[pltpu.SemaphoreType.DMA((1,))],
        name="first_row",
    )


def project_own_kernel(tokens_ref, gain_ref, shift_ref, bias_ref, weight_ref, query_ref, keyval_ref, *rest):
    later_refs, normed_ref = rest[:-1], rest[-1]
    rows, toks, _ = tokens_ref.shape
    for at, later_ref in enumerate(later_refs):
        later_ref[0] = tokens_ref[at + 1]
    normed, _ = normalize(tokens_ref[...].reshape(rows * toks, D).astype(F32))
    normed_ref[...] = (normed * gain_ref[...] + shift_ref[...]).astype(BF16)
    chunk = D // 2
    for at in range(6):
        span = slice(at * chunk, (at + 1) * chunk)
        result = (dot(normed_ref[...], weight_ref[:, span]) + bias_ref[:, span]).astype(BF16)
        cols = slice(at % 2 * chunk, (at % 2 + 1) * chunk)
        if at < 2:
            query_ref[:, :, cols] = (result * 0.125).reshape(rows, toks, chunk)
        else:
            keyval_ref[:, at // 2 - 1, :, cols] = result.reshape(rows, toks, chunk)


def project_own(after, tokens, gain, shift, weight, bias):
    rows, toks, _ = tokens.shape
    return kernel_call(
        project_own_kernel,
        after,
        (tokens, gain, shift, bias, weight),
        14,
        [VMEM] * 5,
        [VMEM] * (1 + rows),
        [jax.ShapeDtypeStruct((rows, toks, D), BF16), jax.ShapeDtypeStruct((rows, 2, toks, D), BF16)]
        + [jax.ShapeDtypeStruct((1, toks, D), BF16)] * (rows - 1),
        scratch_shapes=[pltpu.VMEM((rows * toks, D), BF16)],
        name="project_own",
    )


def project_up_kernel(tokens_ref, gain_ref, shift_ref, bias_ref, weight_ref, keyval_ref):
    toks = tokens_ref.shape[1]
    normed, _ = normalize(tokens_ref[0].astype(F32))
    normed = (normed * gain_ref[...] + shift_ref[...]).astype(BF16)
    for half in range(2):
        cols = slice((half + 1) * D, (half + 2) * D)
        keyval_ref[0, half] = (dot(normed, weight_ref[:, cols]) + bias_ref[:, cols]).astype(BF16)


def project_up(after, tokens, gain, shift, weight, bias, warm=()):
    toks = tokens.shape[1]
    return kernel_call(
        project_up_kernel,
        after,
        (tokens, gain, shift, bias, weight),
        10,
        [VMEM] * 5,
        [VMEM],
        [jax.ShapeDtypeStruct((1, 2, toks, D), BF16)],
        warm=warm,
        name="project_up",
    )


def head_lanes(values, head):
    lanes = lax.broadcasted_iota(jnp.int32, values.shape, 1)
    keep = lanes < HEAD_DIM if head == 0 else lanes >= HEAD_DIM
    return jnp.where(keep, values, jnp.zeros_like(values))


def prefix_mask(values, fill):
    places = lax.broadcasted_iota(jnp.int32, values.shape, 0)
    return jnp.where(places < PREFIX, values, fill)


class Places:
    def __init__(self, toks, level_count):
        self.toks = toks
        self.level_count = level_count

    def masked(self, block):
        if block < 2:
            return True
        level = block // 2
        return (self.level_count - level) * 2 * self.toks > LEAST_LENGTH

    def limits(self, place, length):
        base = place * self.toks
        queries = base + lax.broadcasted_iota(jnp.int32, (1, self.toks), 1)
        return jnp.minimum(queries, length - 1)

    def visible(self, block, place, limit):
        if block == 0:
            base = place * self.toks
        else:
            base = (lax.bitwise_xor(place, block % 2) - (block // 2) * 2) * self.toks
        keys = lax.broadcasted_iota(jnp.int32, (self.toks, self.toks), 0)
        return keys <= limit - base


def spread_prefix(prefix):
    tiled = jnp.concatenate([prefix] * HEADS, axis=0)
    rows = lax.broadcasted_iota(jnp.int32, tiled.shape, 0) // PREFIX_PAD
    cols = lax.broadcasted_iota(jnp.int32, tiled.shape, 1) // HEAD_DIM
    return jnp.where(rows == cols, tiled, jnp.zeros_like(tiled))


GELU_SCALE = 0.7978845608028654
GELU_CUBE = 0.044715
FAR = 1e30
ROW_LIMIT = 30


PACKED = (8, 2 * D + D // 2)


def pack_prefix(ref, halves):
    for half, values in enumerate(halves):
        ref[:, half * D : (half + 1) * D] = values[:8]
        for row in range(8, PREFIX):
            for part in range(2):
                at = (half * (PREFIX - 8) + row - 8) * 2 + part
                ref[at : at + 1, 2 * D :] = values[row : row + 1, part * (D // 2) : (part + 1) * (D // 2)]


def unpack_prefix(ref, half):
    rest = jnp.concatenate([ref[:, 2 * D :], jnp.zeros((8, D // 2), F32)], axis=0)
    rows = []
    for row in range(8, PREFIX):
        at = (half * (PREFIX - 8) + row - 8) * 2
        rows.append(jnp.concatenate([rest[at : at + 1], rest[at + 1 : at + 2]], axis=1))
    rows.append(jnp.zeros((PREFIX_PAD - PREFIX, D), F32))
    return jnp.concatenate([ref[:, half * D : (half + 1) * D]] + rows, axis=0)


class RowRefs:
    def __init__(self, names, refs):
        for name, ref in zip(names, refs):
            setattr(self, name, ref)


def column_group(group, width):
    return pl.ds(pl.multiple_of(group * width, width), width)


def attend_rows(places, refs, place, limit, pair_step):
    blocks = range(2 * places.level_count)
    masked_blocks = [block for block in blocks if places.masked(block)]
    level = place // 2
    width = 128 * pair_step
    refs.prefix_scores[...] = dot(refs.spread[0], refs.query[...], NT)
    for at, block in enumerate(masked_blocks):
        refs.hide[at] = jnp.where(places.visible(block, place, limit), 0.0, -jnp.inf)

    def beyond(block):
        return jnp.where(level >= block // 2, 0.0, FAR) if block > 1 else None

    def body(group, carry):
        span = column_group(group, width)
        group_queries = refs.query[:, span]
        group_keys = [refs.keyval(block, 0, span) for block in blocks]

        def scores_of(at):
            pair, head = at // 2, at % 2
            cols = slice(pair * 128, (pair + 1) * 128)
            queries = head_lanes(group_queries[:, cols], head)
            spot = pl.multiple_of((group * pair_step * 2 + at) * PREFIX_PAD, PREFIX_PAD)
            prefix_scores = prefix_mask(refs.prefix_scores[pl.ds(spot, PREFIX_PAD), :], -jnp.inf)
            highest = jnp.max(prefix_scores, axis=0, keepdims=True)
            scores = []
            for block in blocks:
                part = dot(group_keys[block][:, cols], queries, NT)
                if block in masked_blocks:
                    part = part + refs.hide[masked_blocks.index(block)]
                top = jnp.max(part, axis=0, keepdims=True)
                if block > 1:
                    top = top - beyond(block)
                highest = jnp.maximum(highest, top)
                scores.append(part)
            return prefix_scores, scores, highest

        ahead = scores_of(0)
        for at in range(2 * pair_step):
            pair, head = at // 2, at % 2
            cols = slice(pair * 128, (pair + 1) * 128)
            prefix_scores, scores, highest = ahead
            if at + 1 < 2 * pair_step:
                ahead = scores_of(at + 1)
            if head == 0:
                values_t = [refs.keyval(block, 1, span)[:, cols].T for block in blocks]
                prefix_values_t = refs.prefix[1, :, span][:, cols].T
                ones = jnp.ones((PREFIX_PAD, values_t[0].shape[1]), BF16)
                outs = []
            rows = slice(head * HEAD_DIM, (head + 1) * HEAD_DIM)
            prefix_weights = jnp.exp(prefix_scores - highest)
            total = jnp.sum(prefix_weights, axis=0, keepdims=True)
            mixed = dot(prefix_values_t[rows], prefix_weights.astype(BF16))
            for block in blocks:
                base = highest + beyond(block) if block > 1 else highest
                weights = jnp.exp(scores[block] - base)
                part = dot(jnp.concatenate([values_t[block][rows], ones], axis=0), weights.astype(BF16))
                total = total + part[HEAD_DIM : HEAD_DIM + 1]
                mixed = mixed + part[:HEAD_DIM]
            outs.append(mixed * (1.0 / total))
            refs.total[group, at : at + 1, :] = highest + jnp.log(total)
            if head == 1:
                refs.mixed[:, pl.ds(pl.multiple_of(group * width + pair * 128, 128), 128)] = jnp.concatenate(outs, axis=0).T.astype(BF16)
        return carry

    lax.fori_loop(0, PAIRS // pair_step, body, 0)


def feed_rows(refs, place, length, source, weight_copies, chunks, chunk, slots):
    toks = refs.tokens.shape[0]
    spots = place * toks + lax.broadcasted_iota(jnp.int32, (toks, D), 0)
    target = (spots >= source) & (spots < length)
    refs.grad_out[...] = jnp.where(target, refs.cotangent[...].astype(F32), 0.0).astype(BF16)
    residual = refs.tokens[...].astype(F32) + dot(refs.mixed[...], refs.output_weight[...]) + refs.output_bias[...]
    refs.residual[...] = residual
    normed, _ = normalize(residual)
    refs.normed[...] = (normed * refs.second_gain[...] + refs.second_shift[...]).astype(BF16)

    def first(at, slot):
        for copy in weight_copies(at):
            copy.wait()
        bias = refs.expand_bias[:, pl.ds(pl.multiple_of(at * chunk, chunk), chunk)]
        values = dot(refs.normed[...], refs.expand_weight[at % slots]) + bias
        grad_hidden = dot(refs.grad_out[...], refs.contract_weight[at % slots], NT)
        square = values * values
        bend = jnp.tanh(values * (GELU_SCALE + GELU_SCALE * GELU_CUBE * square))
        half = 0.5 + 0.5 * bend
        slope = half + (0.5 * values) * (1.0 - bend * bend) * (
            GELU_SCALE + 3.0 * GELU_SCALE * GELU_CUBE * square
        )
        refs.active[slot] = (values * half).astype(BF16)
        refs.grad_expand[slot] = (grad_hidden * slope).astype(BF16)

    def second(at, slot):
        refs.result[...] += dot(refs.active[slot], refs.contract_weight[at % slots])
        refs.grad_normed[...] += dot(refs.grad_expand[slot], refs.expand_weight[at % slots], NT)

    def refill(at):
        @pl.when(at + slots < chunks)
        def _():
            for copy in weight_copies(at + slots):
                copy.start()

    refs.result[...] = jnp.zeros_like(refs.result)
    refs.grad_normed[...] = jnp.zeros_like(refs.grad_normed)
    first(0, 0)

    def body(at, carry):
        first(2 * at + 1, 1)
        second(2 * at, 0)
        refill(2 * at)
        first(2 * at + 2, 0)
        second(2 * at + 1, 1)
        refill(2 * at + 1)
        return carry

    lax.fori_loop(0, chunks // 2 - 1, body, 0)
    first(chunks - 1, 1)
    second(chunks - 2, 0)
    second(chunks - 1, 1)

    residual = refs.residual[...]
    refs.activations[...] = (residual + refs.result[...] + refs.contract_bias[...]).astype(BF16)
    normed, scale = normalize(residual)
    grad = refs.grad_out[...].astype(F32) + norm_back(refs.grad_normed[...] * refs.second_gain[...], normed, scale)
    refs.grad_residual[0] = grad
    refs.grad_heads[...] = dot(grad.astype(BF16), refs.output_weight[...], NT).astype(BF16)


def prefix_back_rows(refs):
    toks = refs.query.shape[0]
    queries = refs.query[...]
    grads = refs.grad_heads[...]
    product = grads.astype(F32) * refs.mixed[...].astype(F32)
    head_of = lax.broadcasted_iota(jnp.int32, (HEADS, D), 1) // HEAD_DIM
    chosen = jnp.where(head_of == lax.broadcasted_iota(jnp.int32, (HEADS, D), 0), 1.0, 0.0).astype(BF16)
    high, low = split(product)
    inner = dot(chosen, high, NT) + dot(chosen, low, NT)
    refs.inner[...] = inner.reshape(refs.inner.shape)

    def per_head(values):
        return values.reshape(HEADS, PREFIX_PAD, toks)

    scores = per_head(refs.prefix_scores[...])
    grad_weights = per_head(dot(refs.spread[1], grads, NT))
    weights = jnp.exp(scores - refs.total[...].reshape(HEADS, 1, toks))
    valid = lax.broadcasted_iota(jnp.int32, weights.shape, 1) < PREFIX
    weights = jnp.where(valid, weights, 0.0)
    grad_scores = weights * (grad_weights - inner[:, None, :])
    weights = weights.reshape(HEADS * PREFIX_PAD, toks).astype(BF16)
    grad_scores = grad_scores.reshape(HEADS * PREFIX_PAD, toks).astype(BF16)
    refs.result[...] = dot(grad_scores.T, refs.spread[0])
    own = (
        lax.broadcasted_iota(jnp.int32, (HEADS * PREFIX_PAD, D), 0) // PREFIX_PAD
        == lax.broadcasted_iota(jnp.int32, (HEADS * PREFIX_PAD, D), 1) // HEAD_DIM
    )

    def gather(values):
        return jnp.sum(jnp.where(own, values, 0.0).reshape(HEADS, PREFIX_PAD, D), axis=0)

    sums = gather(dot(grad_scores, queries)), gather(dot(weights, grads))
    pack_prefix(refs.prefix_grad, sums)
    refs.prefix_grad[...] += refs.earlier_grad[...]


def attend_back_rows(places, refs, place, pair_step):
    blocks = range(2 * places.level_count)
    masked_blocks = [block for block in blocks if places.masked(block)]
    level = place // 2
    width = 128 * pair_step

    def body(group, carry):
        span = column_group(group, width)
        group_queries = refs.query[:, span]
        group_grads = refs.grad_heads[:, span]
        group_keys = [refs.keyval(block, 0, span) for block in blocks]
        group_values = [refs.keyval(block, 1, span) for block in blocks]

        sides = {}

        def side(at):
            if at not in sides:
                cols = slice(at // 2 * 128, (at // 2 + 1) * 128)
                sides[at] = head_lanes(group_queries[:, cols], at % 2), head_lanes(group_grads[:, cols], at % 2)
            return sides[at]

        def products_of(item):
            at, block = item
            cols = slice(at // 2 * 128, (at // 2 + 1) * 128)
            queries, grads = side(at)
            part = dot(group_keys[block][:, cols], queries, NT)
            if block in masked_blocks:
                part = part + refs.hide[masked_blocks.index(block)]
            return part, dot(group_values[block][:, cols], grads, NT)

        items = [(at, block) for at in range(2 * pair_step) for block in blocks]
        ahead = [products_of(item) for item in items[:2]]
        for spot, (at, block) in enumerate(items):
            pair, head = at // 2, at % 2
            cols = slice(pair * 128, (pair + 1) * 128)
            place_cols = pl.ds(pl.multiple_of(group * width + pair * 128, 128), 128)
            scores, grad_weights = ahead.pop(0)
            if spot + 2 < len(items):
                ahead.append(products_of(items[spot + 2]))
            queries, grads = side(at)
            if block == 0:
                if head == 0:
                    keys_t = [keys[:, cols].T for keys in group_keys]
                    grad_keys, grad_values, outs = [], [], []
                total = refs.total[group, at : at + 1, :]
                inner = refs.inner[group, at : at + 1, :]
                grad_query = None
            rows = slice(head * HEAD_DIM, (head + 1) * HEAD_DIM)
            base = total + jnp.where(level >= block // 2, 0.0, FAR) if block > 1 else total
            weights = jnp.exp(scores - base)
            grad_scores = (weights * (grad_weights - inner)).astype(BF16)
            part_values = dot(weights.astype(BF16), grads)
            part_keys = dot(grad_scores, queries)
            part_query = dot(keys_t[block][rows], grad_scores)
            if head == 0:
                grad_values.append(part_values)
                grad_keys.append(part_keys)
            else:
                refs.grad_keyval[block][0, 0, :, place_cols] = (grad_keys[block] + part_keys).astype(BF16)
                refs.grad_keyval[block][0, 1, :, place_cols] = (grad_values[block] + part_values).astype(BF16)
            grad_query = part_query if grad_query is None else grad_query + part_query
            if block == blocks[-1]:
                outs.append(grad_query)
                if head == 1:
                    grad_query = jnp.concatenate(outs, axis=0).T + refs.result[:, place_cols]
                    refs.grad_query[0, :, place_cols] = (grad_query * 0.125).astype(BF16)
        return carry

    lax.fori_loop(0, PAIRS // pair_step, body, 0)


ROW_NAMES = (
    "expand_weight", "contract_weight", "spread", "prefix_scores", "hide", "total",
    "mixed", "grad_out", "residual", "normed", "active", "grad_expand", "result", "grad_normed",
    "grad_heads", "inner",
)


def row_kernel(places, keyval_rows, pair_step, chunk, row_ref, place_ref, length_ref, source_ref, *rest):
    block_count = 2 * places.level_count
    row = row_ref[0]
    query_ref, tokens_ref, cotangent_ref, prefix_ref = rest[:4]
    keyval_refs = rest[4 : 4 + block_count]
    rest = rest[4 + block_count :]
    output_weight_ref, expand_weight_hbm, contract_weight_hbm = rest[:3]
    vectors = rest[3:8]
    earlier_grad_ref = rest[8]
    rest = rest[9:]
    activations_ref, grad_residual_ref, grad_query_ref = rest[:3]
    grad_keyval_refs = rest[3 : 3 + block_count]
    prefix_grad_ref = rest[3 + block_count]
    rest = rest[4 + block_count :]
    refs = RowRefs(ROW_NAMES, rest)
    refs.output_bias, refs.second_gain, refs.second_shift, refs.expand_bias, refs.contract_bias = vectors
    refs.prefix_grad, refs.earlier_grad = prefix_grad_ref, earlier_grad_ref
    refs.activations = activations_ref.at[0]
    refs.query, refs.prefix = query_ref.at[row], prefix_ref
    refs.keyval = lambda block, half, span: keyval_refs[block][row if keyval_rows[block] is None else keyval_rows[block], half, :, span]
    refs.grad_residual, refs.grad_query, refs.grad_keyval = grad_residual_ref, grad_query_ref, grad_keyval_refs
    (weight_semaphores,) = rest[len(ROW_NAMES) :]
    slots = refs.expand_weight.shape[0]
    chunks = expand_weight_hbm.shape[1] // chunk

    refs.output_weight, refs.tokens, refs.cotangent = output_weight_ref, tokens_ref.at[row], cotangent_ref.at[row]

    def weight_copies(at):
        span = pl.ds(pl.multiple_of(at * chunk, chunk), chunk)
        return (
            pltpu.make_async_copy(expand_weight_hbm.at[:, span], refs.expand_weight.at[at % slots], weight_semaphores.at[at]),
            pltpu.make_async_copy(contract_weight_hbm.at[span, :], refs.contract_weight.at[at % slots], weight_semaphores.at[chunks + at]),
        )

    def start_weights(at, carry):
        for copy in weight_copies(at):
            copy.start()
        return carry

    lax.fori_loop(0, slots, start_weights, 0)
    place = place_ref[0]
    length = length_ref[row]
    limit = places.limits(place, length)
    for half in range(2):
        refs.spread[half] = spread_prefix(refs.prefix[half])
    attend_rows(places, refs, place, limit, pair_step)
    feed_rows(refs, place, length, source_ref[row], weight_copies, chunks, chunk, slots)
    prefix_back_rows(refs)
    attend_back_rows(places, refs, place, pair_step)


def row_block(after, place, lengths, sources, queries, tokens, cotangent, prefix_keyval, keyvals, weights, row, earlier_grad, warm=(), pair_step=4, chunk=512, slots=3):
    toks = queries.shape[1]
    block_count = len(keyvals)
    places = Places(toks, block_count // 2)
    output_weight, output_bias, gain, shift, expand_weight, expand_bias, contract_weight, contract_bias = weights
    hidden = expand_weight.shape[1]
    chunks = hidden // chunk
    masked = sum(places.masked(block) for block in range(block_count))
    per_group = 2 * pair_step
    scratch = dict(
        expand_weight=((slots, D, chunk), BF16), contract_weight=((slots, chunk, D), BF16),
        spread=((2, HEADS * PREFIX_PAD, D), BF16), prefix_scores=((HEADS * PREFIX_PAD, toks), F32),
        hide=((masked, toks, toks), F32), total=((HEADS // per_group, per_group, toks), F32), mixed=((toks, D), BF16),
        grad_out=((toks, D), BF16), residual=((toks, D), F32), normed=((toks, D), BF16),
        active=((2, toks, chunk), BF16), grad_expand=((2, toks, chunk), BF16), result=((toks, D), F32),
        grad_normed=((toks, D), F32),
        grad_heads=((toks, D), BF16), inner=((HEADS // per_group, per_group, toks), F32),
    )
    return kernel_call(
        functools.partial(row_kernel, places, [at for _, at in keyvals], pair_step, chunk),
        after,
        (
            jnp.full((1,), row, jnp.int32), place, lengths, sources, queries, tokens, cotangent, prefix_keyval, *[array for array, _ in keyvals],
            output_weight, expand_weight, contract_weight, output_bias, gain, shift, expand_bias, contract_bias, earlier_grad,
        ),
        ROW_LIMIT,
        [VMEM] * (4 + block_count) + [VMEM, HBM, HBM] + [VMEM] * 6,
        [VMEM] * (4 + block_count),
        [
            jax.ShapeDtypeStruct((1, toks, D), BF16),
            jax.ShapeDtypeStruct((1, toks, D), F32),
            jax.ShapeDtypeStruct((1, toks, D), BF16),
        ]
        + [jax.ShapeDtypeStruct((1, 2, toks, D), BF16)] * block_count
        + [jax.ShapeDtypeStruct(PACKED, F32)],
        prefetched=4,
        scratch_shapes=[pltpu.VMEM(*scratch[name]) for name in ROW_NAMES]
        + [pltpu.SemaphoreType.DMA((2 * chunks,))],
        warm=warm,
        name="row_block",
    )


def up_back_kernel(own_ref, received_ref, weight_ref, grad_ref):
    total = None
    for half in range(2):
        values = (own_ref[0, half].astype(F32) + received_ref[0, half].astype(F32)).astype(BF16)
        part = dot(values, weight_ref[:, (half + 1) * D : (half + 2) * D], NT)
        total = part if total is None else total + part
    grad_ref[0] = total.astype(BF16)


def up_back(after, own, received, weight):
    toks = own.shape[2]
    return kernel_call(
        up_back_kernel,
        after,
        (own, received, weight),
        10,
        [VMEM] * 3,
        [VMEM],
        [jax.ShapeDtypeStruct((1, toks, D), BF16)],
        name="up_back",
    )


def project_back_kernel(query_ref, own_ref, received_ref, weight_ref, total_ref):
    total = dot(query_ref[0], weight_ref[:, :D], NT)
    for half in range(2):
        values = (own_ref[0, half].astype(F32) + received_ref[0, half].astype(F32)).astype(BF16)
        total = total + dot(values, weight_ref[:, (half + 1) * D : (half + 2) * D], NT)
    total_ref[0] = total


def project_back(after, grad_query, own, received, weight):
    toks = grad_query.shape[1]
    return kernel_call(
        project_back_kernel,
        after,
        (grad_query, own, received, weight),
        10,
        [VMEM] * 4,
        [VMEM],
        [jax.ShapeDtypeStruct((1, toks, D), F32)],
        name="project_back",
    )


def finish_kernel(above_count, row, tokens_ref, gain_ref, residual_ref, total_ref, activations_ref, *rest):
    activations_hbm, grad_hbm, grad_ref, semaphores = rest[-4:]
    toks = grad_ref.shape[0]
    copies = Copies(semaphores)
    copies.start("activations", activations_ref.at[0], activations_hbm.at[row])
    parts = 2
    for part in range(parts):
        span = pl.ds(part * (toks // parts), toks // parts)
        total = total_ref[0, span]
        for above_ref in rest[:above_count]:
            total = total + above_ref[0, span].astype(F32)
        normed, scale = normalize(tokens_ref[row, span].astype(F32))
        grad_ref[span] = residual_ref[0, span] + norm_back(total * gain_ref[...], normed, scale)
        copies.start(part, grad_ref.at[span], grad_hbm.at[row, span])
    for part in range(parts):
        copies.wait(part)
    copies.wait("activations")


def finish(after, tokens, gain, grad_residual, total, activations, above, row, earlier):
    toks = tokens.shape[1]
    return kernel_call(
        functools.partial(finish_kernel, len(above), row),
        after,
        (tokens, gain, grad_residual, total, activations, *above, *earlier),
        10,
        [VMEM] * (5 + len(above)) + [ANY] * len(earlier),
        [HBM] * 2,
        [jax.ShapeDtypeStruct(tokens.shape, BF16), jax.ShapeDtypeStruct(tokens.shape, F32)],
        scratch_shapes=[pltpu.VMEM((toks, D), F32), pltpu.SemaphoreType.DMA((3,))],
        input_output_aliases={5 + len(above) + at: at for at in range(len(earlier))},
        name="finish",
    )


def prefix_kernel(table_ref, lift_ref, lift_bias_ref, fan_ref, fan_bias_ref, lifted_ref, keyval_ref):
    lifted = jnp.tanh(dot(table_ref[...], lift_ref[...]) + lift_bias_ref[...])
    lifted_ref[...] = jnp.zeros_like(lifted_ref)
    lifted_ref[:PREFIX, :] = lifted
    keyval_ref[...] = jnp.zeros_like(keyval_ref)
    keyval = (dot(lifted.astype(BF16), fan_ref[...]) + fan_bias_ref[...]).astype(BF16)
    keyval_ref[0, :PREFIX, :] = keyval[:, :D]
    keyval_ref[1, :PREFIX, :] = keyval[:, D:]


def prefix_forward(after, table, lift, lift_bias, fan, fan_bias):
    return kernel_call(
        prefix_kernel,
        after,
        (table, lift, lift_bias, fan, fan_bias),
        8,
        [VMEM] * 5,
        [VMEM] * 2,
        [
            jax.ShapeDtypeStruct((PREFIX_PAD, lift.shape[1]), F32),
            jax.ShapeDtypeStruct((2, PREFIX_PAD, D), BF16),
        ],
        name="prefix_forward",
    )


def prefix_network_back_kernel(grad_ref, table_ref, lift_ref, fan_ref, lifted_ref, grad_table_ref, grad_lift_hbm, grad_lift_bias_ref, grad_fan_hbm, grad_fan_bias_ref, grad_lift_ref, grad_fan_ref, semaphores):
    copies = Copies(semaphores)
    lifted = lifted_ref[...]
    lifted_t = jnp.concatenate([lifted.astype(BF16)] * 2, axis=0).T
    grad_lifted = None
    for half in range(2):
        cols = slice(half * D, (half + 1) * D)
        grad = unpack_prefix(grad_ref, half)
        grad_fan_bias_ref[:, cols] = jnp.sum(grad, axis=0, keepdims=True)
        both = jnp.concatenate(split(grad), axis=0)
        grad_fan_ref[half] = dot(lifted_t, both)
        copies.start(half, grad_fan_ref.at[half], grad_fan_hbm.at[:, cols])
        part = dot(both, fan_ref[:, cols], NT)
        grad_lifted = part if grad_lifted is None else grad_lifted + part
    grad_lifted = (grad_lifted[:PREFIX_PAD] + grad_lifted[PREFIX_PAD:]) * (1.0 - lifted * lifted)
    grad_lift_bias_ref[...] = jnp.sum(grad_lifted, axis=0, keepdims=True)
    both = jnp.concatenate(split(grad_lifted), axis=0)
    table = jnp.concatenate([table_ref[...].astype(F32), jnp.zeros((PREFIX_PAD - PREFIX, D), F32)], axis=0)
    table_t = jnp.concatenate([table.astype(BF16)] * 2, axis=0).T
    grad_lift_ref[...] = dot(table_t, both)
    copies.start("lift", grad_lift_ref, grad_lift_hbm)
    grad_table = dot(both, lift_ref[...], NT)
    grad_table_ref[...] = (grad_table[:PREFIX_PAD] + grad_table[PREFIX_PAD:])[:PREFIX]
    for name in (0, 1, "lift"):
        copies.wait(name)


def prefix_network_back(after, grad, table, lift, fan, lifted):
    hidden = lift.shape[1]
    return kernel_call(
        prefix_network_back_kernel,
        after,
        (grad, table, lift, fan, lifted),
        20,
        [VMEM] * 5,
        [VMEM, HBM, VMEM, HBM, VMEM],
        [
            jax.ShapeDtypeStruct((PREFIX, D), F32),
            jax.ShapeDtypeStruct((D, hidden), F32),
            jax.ShapeDtypeStruct((1, hidden), F32),
            jax.ShapeDtypeStruct((hidden, 2 * D), F32),
            jax.ShapeDtypeStruct((1, 2 * D), F32),
        ],
        scratch_shapes=[
            pltpu.VMEM((D, hidden), F32),
            pltpu.VMEM((2, hidden, D), F32),
            pltpu.SemaphoreType.DMA((3,)),
        ],
        name="prefix_network_back",
    )


def add_kernel(*refs):
    total = refs[0][...]
    for ref in refs[1:-1]:
        total = total + ref[...]
    refs[-1][...] = total


def add(after, *values):
    return kernel_call(add_kernel, after, values, 2, [VMEM] * len(values), [VMEM], values[:1], name="add")


def mark_kernel(*refs):
    pass


def mark(after, warm=()):
    return kernel_call(mark_kernel, after, (), 8, [], [], [], warm=warm, cover=LONG_COVER, name="mark")


def hold(after, array):
    return kernel_call(mark_kernel, after, (array,), 1, [ANY], [ANY], [array], input_output_aliases={0: 0}, name="hold")


class Order:
    def __init__(self):
        self.before = ()

    def call(self, kernel, *operands):
        *outs, token = kernel(self.before, *operands)
        self.before = (token,)
        return outs[0] if len(outs) == 1 else outs


def sum_stages():
    stages = []
    for axis, most in (("seq", 1), ("dp", 2)):
        size = lax.axis_size(axis)
        if size & (size - 1):
            return None
        hop = 1
        while hop < size:
            bits = most if hop > 1 and hop * 2 < size else 1
            stages.append((axis, [[(at, at ^ (hop * step)) for at in range(size)] for step in range(1, 2**bits)]))
            hop *= 2**bits
    return stages


def per_device(tokens, cotangent, row_lengths, source_lengths, first_gain, first_shift, attend_weight, attend_bias, output_weight, output_bias, second_gain, second_shift, expand_weight, expand_bias, contract_weight, contract_bias, prefix_table, lift_weight, lift_bias, fan_weight, fan_bias):
    rows = tokens.shape[0]
    seq = lax.axis_size("seq")
    level_count = seq // 2
    levels = range(1, level_count)
    mates = [(at, at ^ 1) for at in range(seq)]
    place = lax.axis_index("seq").astype(jnp.int32).reshape(1)
    first_gain, first_shift, attend_bias, output_bias, second_gain, second_shift, expand_bias, contract_bias, lift_bias, fan_bias = [
        vector.reshape(1, -1)
        for vector in (first_gain, first_shift, attend_bias, output_bias, second_gain, second_shift, expand_bias, contract_bias, lift_bias, fan_bias)
    ]
    weights = (output_weight, output_bias, second_gain, second_shift, expand_weight, expand_bias, contract_weight, contract_bias)
    order = Order()
    hops = sum_stages()
    finished = ()
    prefix_grad = jnp.zeros(PACKED, F32)
    arriving = None

    def swap(array):
        return lax.ppermute(array, "seq", mates)

    def hop():
        nonlocal prefix_grad, arriving
        if arriving is not None:
            prefix_grad = order.call(add, prefix_grad, *arriving)
            arriving = None
        if hops:
            axis, partners = hops.pop(0)
            arriving = [lax.ppermute(prefix_grad, axis, pairs) for pairs in partners]

    def lower(row):
        blocks = []
        for level in levels:
            block = order.call(project_up, lower_tokens[row, level], first_gain, first_shift, attend_weight, attend_bias, (queries, cotangent) if row == 0 else ())
            blocks += [block, swap(block)]
        return blocks

    def keyvals_of(blocks):
        return [(keyval, None), (mate_keyval, None)] + [(block, 0) for block in blocks]

    row_tokens = [order.call(first_row, tokens)]
    lower_tokens = {}

    def raise_tokens(row):
        for level in levels:
            pairs = [(at, at + 2 * level) for at in range(seq - 2 * level)]
            lower_tokens[row, level] = lax.ppermute(row_tokens[row], "seq", pairs)

    raise_tokens(0)
    queries, keyval, *later = order.call(project_own, tokens, first_gain, first_shift, attend_weight, attend_bias)
    row_tokens += later
    for row in range(1, rows):
        raise_tokens(row)
    mate_keyval = swap(keyval)
    lifted, prefix_keyval = order.call(prefix_forward, prefix_table, lift_weight, lift_bias, fan_weight, fan_bias)
    blocks = lower(0)
    order.call(mark)
    waiting = []
    finished_rows = 0
    for row in range(rows):
        last_row = row + 1 == rows
        row_activations, grad_residual, grad_query, *grads, prefix_grad = order.call(
            row_block, place, row_lengths, source_lengths, queries, tokens, cotangent, prefix_keyval,
            keyvals_of(blocks), weights, row, prefix_grad, (attend_weight,),
        )
        received = None if last_row else swap(grads[1])
        from_mates = [swap(grads[2 * level + 1]) for level in levels]
        if last_row:
            if hops is None:
                prefix_grad = lax.psum(prefix_grad, ("seq", "dp"))
            hop()
            for earlier in waiting:
                earlier()
                hop()
            received = swap(order.call(hold, grads[1]))
        else:
            blocks = lower(row + 1)
        above = []
        for level in levels:
            part = order.call(up_back, grads[2 * level], from_mates[level - 1], attend_weight)
            above.append(lax.ppermute(part, "seq", [(at + 2 * level, at) for at in range(seq - 2 * level)]))
        total = order.call(project_back, grad_query, grads[0], received, attend_weight)

        def end(row=row, grad_residual=grad_residual, total=total, row_activations=row_activations, above=above):
            nonlocal finished, finished_rows
            finished_rows += 1
            finished = order.call(finish, tokens, first_gain, grad_residual, total, row_activations, above, row, finished)

        waiting.append(end)
    while hops or arriving is not None:
        hop()
        if arriving is not None:
            if hops:
                order.call(mark, (lift_weight, fan_weight))
            else:
                waiting[-1]()
    grad_table, grad_lift, grad_lift_bias, grad_fan, grad_fan_bias = order.call(
        prefix_network_back, prefix_grad, prefix_table, lift_weight, fan_weight, lifted
    )
    if finished_rows < rows:
        waiting[-1]()
    return (*finished, grad_table, grad_lift, grad_lift_bias.reshape(-1), grad_fan, grad_fan_bias.reshape(-1))


def solution(mesh):
    batch = P("dp", "seq", None)
    return jax.shard_map(
        per_device,
        mesh=mesh,
        in_specs=(batch, batch, P("dp"), P("dp")) + (P(),) * 17,
        out_specs=(batch, batch, P(), P(), P(), P(), P()),
        check_vma=False,
    )
```
